128 devices in a mesh: req: 16 (over y, x), exp: 8 (over z, core).
Axes of the slice: x: 4, y: 4, z: 4, core: 2. Of those that a mesh axis runs over, the one named last changes fastest.
Arguments:
- attention_out: bfloat16 [2048, 4096], P('req'), may hold values from -6 to 6
- residual: bfloat16 [2048, 4096], P('req', 'exp'), may hold values from -6 to 6
- w_out: bfloat16 [4096, 4096], P('req', 'exp'), may hold values from -0.09375 to 0.09375
- router_w: float32 [4096, 8], P('exp'), may hold values from -0.09375 to 0.09375
- norm_gain: float32 [4096], P('exp'), may hold values from 0.5 to 1.5
- page_pool: bfloat16 [4096, 8, 2048], P('req', None, 'exp'), may hold values from -6 to 6
- page_table: int32 [2048, 2], P('req'), may hold values from 0 to 255, as said below
- cache_len: int32 [2048], P('req'), may hold values from 1 to 16
- came_from: int32 [2048], replicated, may hold values from 0 to 2047, as said below
- routes: int32 [2048, 2], P('req'), may hold values from 0 to 7, all different within a row; in each aligned block of 128 rows (0 to 127, 128 to 255, ...) at most 64 rows name the same one
- w_gate: bfloat16 [16, 4096, 7168], P('req', None, 'exp'), as said below
- w_up: bfloat16 [16, 4096, 7168], P('req', None, 'exp'), as said below
- w_down: bfloat16 [16, 7168, 4096], P('req', 'exp'), as said below
Outputs:
- mixed: float32 [2048, 4096], P('req', 'exp')
- new_pages: bfloat16 [2048, 2, 8, 2048], P('req', None, None, 'exp')
The draws below stay inside these ranges and needn't reach their ends.
Inputs may be any that keep to these rules, and one draw needn't show every extreme that they name: page_table's entries for the requests of one req group are distinct. came_from is a permutation; from each req group 4 rows go to each of the other 15 groups, each group receives 4 rows from each of them, and all other rows keep their place. `routes`: within the rows of one req group every expert is named by at most 64 rows, and some expert by exactly 64 rows in some group. `w_gate`: slices e and e + 8 along the first dimension are equal. `w_up`: slices e and e + 8 along the first dimension are equal. `w_down`: slices e and e + 8 along the first dimension are equal.
All inputs are finite; a program needn't handle non-finite values.
Results may differ from the reference program's by a relative error of at most 0.0055.
Values may be sent and summed in bfloat16 or wider, within the bound.
A program may use at most 128 MiB of HBM per device.

```python
import math
import jax
import jax.numpy as jnp
import numpy as np
from jax import lax

D = 4096
KVS = 2048
FF = 7168
SLICE = 896
EXPERTS = 8
TOP = 2
ROW_REQ = 128
ROWS = 2048
CAP = 32
MIG_PAIR = 4
PAGE = 8
PPR = 2
POOL = 256
N_REQ = 16
N_EXP = 8


def stacked_weight(key, shape, fan):
    base_weight = jax.random.normal(key, shape, jnp.float32) * fan ** (-0.5)
    return jnp.concatenate([base_weight, base_weight], axis=0).astype(jnp.bfloat16)


def draw_w_gate(key, part):
    return stacked_weight(jax.random.fold_in(key, 11), (EXPERTS, D, FF), D)


def draw_w_up(key, part):
    return stacked_weight(jax.random.fold_in(key, 12), (EXPERTS, D, FF), D)


def draw_w_down(key, part):
    return stacked_weight(jax.random.fold_in(key, 13), (EXPERTS, FF, D), FF)


def draw_page_table(key, part):
    groups = ROWS // ROW_REQ
    group_keys = jax.random.split(jax.random.fold_in(key, 21), groups)
    orders = jax.vmap(lambda one_key: jax.random.permutation(one_key, POOL))(group_keys)
    return orders.reshape(ROWS, PPR).astype(jnp.int32)


def draw_came_from(key, part):
    groups = ROWS // ROW_REQ
    senders = groups - 1
    moving = senders * MIG_PAIR
    order_key = jax.random.fold_in(key, 32)
    shifts = jnp.arange(1, groups, dtype=jnp.int32)
    orders = jax.vmap(lambda one_key: jax.random.permutation(one_key, ROW_REQ))(jax.random.split(order_key, groups)).astype(jnp.int32)
    slot_ids = jnp.arange(moving, dtype=jnp.int32)
    block_index = slot_ids // MIG_PAIR
    group_ids = jnp.arange(groups, dtype=jnp.int32)
    source = (group_ids[:, None] - shifts[block_index][None, :]) % groups
    src_rows = source * ROW_REQ + orders[source, slot_ids[None, :]]
    dest_rows = group_ids[:, None] * ROW_REQ + orders[:, :moving]
    identity_rows = jnp.arange(ROWS, dtype=jnp.int32)
    return identity_rows.at[dest_rows.reshape(-1)].set(src_rows.reshape(-1)).astype(jnp.int32)


def place_ends(entries, key, least, top_value):
    spot = [jax.random.randint(jax.random.fold_in(key, axis), (), 0, length) for axis, length in enumerate(entries.shape)]
    main_axis = entries.shape.index(max(entries.shape))
    beside = spot[:main_axis] + [(spot[main_axis] + 1) % entries.shape[main_axis]] + spot[main_axis + 1:]
    return entries.at[tuple(spot)].set(least).at[tuple(beside)].set(top_value)


def steps_of(key, shape, shards, smallest, largest):
    factor_of = 1.0
    for axis_at, parts in shards:
        steps = jax.random.uniform(jax.random.fold_in(jax.random.fold_in(key, 6), axis_at), (parts,), jnp.float32, smallest / len(shards), largest / len(shards))
        factor_of = factor_of * jnp.repeat(jnp.exp(steps), shape[axis_at] // parts).reshape((-1,) + (1,) * (len(shape) - 1 - axis_at))
    return factor_of


def shared_out(own_key, own, number, rows, number_of, top, reach, lean):
    ranking = jax.random.permutation(own_key, number_of)
    crowded, ordinary = load_shares(number_of, rows * top, reach, lean, True), load_shares(number_of, rows * top, reach, lean, False)
    places = jnp.arange(number_of)

    def named(tallies, turn):
        used = int((tallies > 0).sum())
        fixed = max(1, used // 4)
        passed = fixed + (places - fixed + turn * (used - fixed)) % max(1, number_of - fixed)
        return jnp.zeros((number_of,), jnp.int32).at[ranking[jnp.where(places < fixed, places, passed)]].set(jnp.asarray(tallies, jnp.int32))

    tallies = jnp.where(number % 4 == 0, named(crowded, number // 4), named(ordinary, number - number // 4 - 1))
    mixed = jax.random.permutation(jax.random.fold_in(own, 3), number_of)
    giver, receiver = mixed[0:number_of // 2 * 2:2], mixed[1:number_of // 2 * 2:2]
    slack = jnp.minimum(tallies[giver] - 1, reach - tallies[receiver]) // 2
    slack = jnp.where((giver == ranking[0]) | (receiver == ranking[0]) | (tallies[receiver] == 0), 0, jnp.maximum(slack, 0))
    passed = jax.random.randint(jax.random.fold_in(own, 4), (number_of // 2,), 0, 1 << 20) % (slack + 1)
    tallies = tallies.at[giver].add(-passed).at[receiver].add(passed)
    items = jnp.searchsorted(jnp.cumsum(tallies), jnp.arange(rows * top), side="right").astype(jnp.int32)
    listing = items.reshape(top, rows).T
    listing = listing[jax.random.permutation(jax.random.fold_in(own, 1), rows)]
    turn = jax.random.randint(jax.random.fold_in(own, 2), (rows, 1), 0, top)
    return jnp.take_along_axis(listing, (jnp.arange(top)[None, :] + turn) % top, axis=1)


def load_shares(count, total, most, slope, full):
    loads = [(1 << 20) // math.isqrt(standing ** slope) + 1 for standing in range(1, count + 1)]
    largest = most if full else min(most, max(-(-total // count), total * loads[0] // sum(loads)))
    least = 1 if total - largest >= count - 1 else 0
    given, spare = [largest] + [least] * (count - 1), total - largest - least * (count - 1)
    while spare > 0:
        candidates = [i for i in range(1, count) if given[i] < largest] or [i for i in range(1, count) if given[i] < most]
        pool, remaining = sum([loads[i] for i in candidates]), spare
        for i in candidates:
            addition = min(most - given[i], max(1, remaining * loads[i] // pool), spare)
            given[i] = given[i] + addition
            spare = spare - addition
    return np.array(given)


def gaussian(key, shape, width, most, cuts=(), held_as=jnp.bfloat16):
    array = width * jax.random.normal(key, shape, jnp.float32)
    if cuts:
        array = array * steps_of(key, shape, cuts, -0.22, 0.18)
    return jnp.clip(array, -most, most).astype(held_as)


def setup_inputs(seed: int = 0) -> dict:
    key_of = jax.random.split(jax.random.key(seed), 14)
    attention_out = gaussian(key_of[0], (ROWS, D), 1.0, 6.0, ((0, 16),))
    residual = gaussian(key_of[1], (ROWS, D), 1.0, 6.0, ((0, 16), (1, 8)))
    w_out = gaussian(key_of[2], (D, D), D ** -0.5, 0.09375, ((0, 16), (1, 8)))
    router_w = gaussian(key_of[3], (D, EXPERTS), D ** -0.5, 0.09375, ((0, 8),), jnp.float32)
    norm_gain = jnp.clip(1.0 + 0.1 * jax.random.normal(key_of[4], (D,), jnp.float32), 0.5, 1.5)
    page_pool = gaussian(key_of[5], (POOL * N_REQ, PAGE, KVS), 1.0, 6.0, ((0, 16), (2, 8)))
    page_table = draw_page_table(jax.random.fold_in(key_of[13], 71), 0)
    cache_len = place_ends(jax.random.randint(key_of[7], (ROWS,), 1, PPR * PAGE + 1), jax.random.fold_in(key_of[7], 1), 1, PPR * PAGE).astype(jnp.int32)
    came_from = draw_came_from(jax.random.fold_in(key_of[13], 71), 0)
    routes_keys = jax.random.split(jax.random.fold_in(key_of[9], 1), ROWS // ROW_REQ)
    routes_turns = jax.random.permutation(jax.random.fold_in(key_of[9], 3), ROWS // ROW_REQ)
    routes = jax.vmap(lambda own, number: shared_out(jax.random.fold_in(key_of[9], 2), own, number, ROW_REQ, EXPERTS, 2, 2 * CAP, 2))(routes_keys, routes_turns).reshape((ROWS, TOP))
    w_gate = draw_w_gate(jax.random.fold_in(key_of[13], 71), 0)
    w_up = draw_w_up(jax.random.fold_in(key_of[13], 71), 0)
    w_down = draw_w_down(jax.random.fold_in(key_of[13], 71), 0)
    return dict(attention_out=attention_out, residual=residual, w_out=w_out, router_w=router_w, norm_gain=norm_gain, page_pool=page_pool, page_table=page_table, cache_len=cache_len, came_from=came_from, routes=routes, w_gate=w_gate, w_up=w_up, w_down=w_down)


EPSILON = 1e-05

def reference(attention_out, residual, w_out, router_w, norm_gain, page_pool, page_table, cache_len, came_from, routes, w_gate, w_up, w_down):
    experts = N_REQ // 2
    attn_new = jnp.take(attention_out, came_from, axis=0)
    resid_new = jnp.take(residual, came_from, axis=0)
    source_group = came_from // ROW_REQ
    pool_slots = source_group[:, None] * POOL + jnp.take(page_table, came_from, axis=0)
    gathered = jnp.take(page_pool, pool_slots.reshape(-1), axis=0).reshape(ROWS, PPR, PAGE, KVS)
    position = jnp.arange(PPR, dtype=jnp.int32)[:, None] * PAGE + jnp.arange(PAGE, dtype=jnp.int32)[None, :]
    kept_mask = position[None, :, :] < jnp.take(cache_len, came_from)[:, None, None]
    new_pages = jnp.where(kept_mask[..., None], gathered, jnp.zeros((), gathered.dtype))
    projected = jnp.dot(attn_new, w_out, preferred_element_type=jnp.float32)
    hidden = resid_new.astype(jnp.float32) + projected
    mean_sq = lax.optimization_barrier(jnp.sum(hidden * hidden, axis=1)) / D
    normed = hidden * norm_gain[None, :] * lax.rsqrt(mean_sq + EPSILON)[:, None]
    logits = jnp.dot(normed, router_w, precision=lax.Precision.HIGHEST)
    chosen = jnp.take_along_axis(logits, routes, axis=1)
    gate_pair = jax.nn.sigmoid(chosen - chosen[:, ::-1])
    normed_rows = normed.astype(jnp.bfloat16)
    grouped = routes.reshape(N_REQ, ROW_REQ * TOP)
    expert_hot = (grouped[:, :, None] == jnp.arange(experts, dtype=jnp.int32)[None, None, :]).astype(jnp.int32)
    expert_rank = lax.optimization_barrier(jnp.sum((jnp.cumsum(expert_hot, axis=1) - expert_hot) * expert_hot, axis=2)).reshape(-1)
    target_dev = routes.reshape(-1) + experts * (expert_rank % 2)
    count_all = ROWS * TOP
    capacity_all = N_REQ * CAP
    assign_ids = jnp.arange(count_all, dtype=jnp.int32)

    def one_target(device):
        ordered = jnp.sort(jnp.where(target_dev == device, assign_ids, count_all))[:capacity_all]
        rows_in = jnp.take(normed_rows, jnp.minimum(ordered, count_all - 1) // TOP, axis=0)
        gate_h = jnp.dot(rows_in, w_gate[device], preferred_element_type=jnp.float32)
        up_h = jnp.dot(rows_in, w_up[device], preferred_element_type=jnp.float32)
        active = (jax.nn.silu(gate_h) * up_h).astype(jnp.bfloat16)
        down_all = w_down[device]
        summed = jnp.zeros((capacity_all, D), jnp.float32)
        for block_index in range(N_EXP):
            block_out = jnp.dot(active[:, block_index * SLICE:(block_index + 1) * SLICE], down_all[block_index * SLICE:(block_index + 1) * SLICE], preferred_element_type=jnp.float32)
            summed = summed + lax.optimization_barrier(block_out.astype(jnp.bfloat16)).astype(jnp.float32)
        return (ordered, summed)
    ordered_all, outputs = lax.map(one_target, jnp.arange(2 * experts, dtype=jnp.int32))
    expert_out = jnp.zeros((count_all, D), jnp.float32).at[ordered_all.reshape(-1)].set(outputs.reshape(-1, D), mode='drop')
    expert_out = expert_out.reshape(ROWS, TOP, D)
    mixed = hidden + gate_pair[:, 0:1] * expert_out[:, 0] + gate_pair[:, 1:2] * expert_out[:, 1]
    return (mixed, new_pages)
```

```python
import jax
import jax.numpy as jnp
from jax import lax
from jax.sharding import PartitionSpec as P

D = 4096
CAP = 32
MIG_PAIR = 4


EPSILON = 1e-05


def pick_rows(source, row_index, live_slot):
    taken_rows = jnp.take(source, row_index, axis=0)
    return jnp.where(live_slot[:, None], taken_rows, jnp.zeros((), source.dtype))


def body(
    attention_out,
    residual,
    w_out,
    router_w,
    norm_gain,
    page_pool,
    page_table,
    cache_len,
    came_from,
    routes,
    w_gate,
    w_up,
    w_down,
):
    groups = lax.axis_size("req")
    own_group = lax.axis_index("req")
    row_req = attention_out.shape[0]
    rows_all = came_from.shape[0]
    pages_req = page_table.shape[1]
    page_len = page_pool.shape[1]
    kv_slice = page_pool.shape[2]
    experts = groups // 2
    targets = jnp.arange(groups, dtype=jnp.int32)
    local_ids = jnp.arange(row_req, dtype=jnp.int32)
    dest_of = (
        jnp.zeros((rows_all,), jnp.int32).at[came_from].set(jnp.arange(rows_all, dtype=jnp.int32))
    )
    dest_group = dest_of // row_req
    dest_hot = (
        (dest_group[:, None] == targets[None, :]).astype(jnp.int32).reshape(groups, row_req, groups)
    )
    pair_rank = jnp.sum((jnp.cumsum(dest_hot, axis=1) - dest_hot) * dest_hot, axis=2).reshape(
        rows_all
    )
    own_dest = lax.dynamic_slice_in_dim(dest_group, own_group * row_req, row_req)
    own_rank = lax.dynamic_slice_in_dim(pair_rank, own_group * row_req, row_req)
    chosen_send = (
        (own_dest[None, None, :] == targets[:, None, None])
        & (own_rank[None, None, :] == jnp.arange(MIG_PAIR, dtype=jnp.int32)[None, :, None])
        & (targets[:, None, None] != own_group)
    )
    send_index = jnp.sum(jnp.where(chosen_send, local_ids[None, None, :], 0), axis=2).reshape(-1)
    send_live = jnp.any(chosen_send, axis=2).reshape(-1)
    page_rows = jnp.take(page_pool, page_table.reshape(-1), axis=0).reshape(
        row_req, pages_req, page_len, kv_slice
    )
    position = (
        jnp.arange(pages_req, dtype=jnp.int32)[:, None] * page_len
        + jnp.arange(page_len, dtype=jnp.int32)[None, :]
    )
    kept_mask = position[None, :, :] < cache_len[:, None, None]
    page_rows = jnp.where(kept_mask[..., None], page_rows, jnp.zeros((), page_rows.dtype)).reshape(
        row_req, -1
    )
    moved_attn, moved_resid, moved_pages = (
        lax.all_to_all(
            pick_rows(attention_out, send_index, send_live),
            "req",
            split_axis=0,
            concat_axis=0,
            tiled=True,
        ),
        lax.all_to_all(
            pick_rows(residual, send_index, send_live),
            "req",
            split_axis=0,
            concat_axis=0,
            tiled=True,
        ),
        lax.all_to_all(
            pick_rows(page_rows, send_index, send_live),
            "req",
            split_axis=0,
            concat_axis=0,
            tiled=True,
        ),
    )
    new_source = lax.dynamic_slice_in_dim(came_from, own_group * row_req, row_req)
    source_group = new_source // row_req
    stays_home = source_group == own_group
    arrival = jnp.where(
        stays_home,
        new_source - own_group * row_req,
        row_req + source_group * MIG_PAIR + jnp.take(pair_rank, new_source),
    )
    attn_new = jnp.take(jnp.concatenate([attention_out, moved_attn], axis=0), arrival, axis=0)
    resid_new = jnp.take(jnp.concatenate([residual, moved_resid], axis=0), arrival, axis=0)
    new_pages = jnp.take(
        jnp.concatenate([page_rows, moved_pages], axis=0), arrival, axis=0
    ).reshape(row_req, pages_req, page_len, kv_slice)
    new_pages, attn_new = lax.optimization_barrier((new_pages, attn_new))
    projected = jnp.dot(
        attn_new,
        lax.all_gather(w_out, "req", axis=0, tiled=True),
        preferred_element_type=jnp.float32,
    )
    hidden = resid_new.astype(jnp.float32) + projected
    squares = jnp.sum(hidden * hidden, axis=1)
    scaled = hidden * norm_gain[None, :]
    raw_logits = jnp.dot(scaled, router_w, precision=lax.Precision.HIGHEST)
    row_stats = lax.psum(jnp.concatenate([squares[:, None], raw_logits], axis=1), "exp")
    total_sq = row_stats[:, 0]
    inverse = lax.rsqrt(total_sq / D + EPSILON)
    normed = scaled * inverse[:, None]
    logits = row_stats[:, 1:] * inverse[:, None]
    normed_rows = normed.astype(jnp.bfloat16)
    expert_ids = jnp.arange(experts, dtype=jnp.int32)
    chosen = jnp.sum(
        jnp.where(routes[:, :, None] == expert_ids[None, None, :], logits[:, None, :], 0.0), axis=2
    )
    gate_first = jax.nn.sigmoid(chosen[:, 0] - chosen[:, 1])
    gate_second = jax.nn.sigmoid(chosen[:, 1] - chosen[:, 0])
    flat_routes = routes.reshape(-1)
    expert_hot = (flat_routes[:, None] == expert_ids[None, :]).astype(jnp.int32)
    expert_rank = jnp.sum((jnp.cumsum(expert_hot, axis=0) - expert_hot) * expert_hot, axis=1)
    target_dev = flat_routes + experts * (expert_rank % 2)
    slot_index = expert_rank // 2
    assign_ids = jnp.arange(flat_routes.shape[0], dtype=jnp.int32)
    chosen_slot = (target_dev[None, None, :] == targets[:, None, None]) & (
        slot_index[None, None, :] == jnp.arange(CAP, dtype=jnp.int32)[None, :, None]
    )
    slot_source = jnp.sum(
        jnp.where(chosen_slot, assign_ids[None, None, :] // 2, 0), axis=2
    ).reshape(-1)
    slot_live = jnp.any(chosen_slot, axis=2).reshape(-1)
    outgoing = pick_rows(normed_rows, slot_source, slot_live)
    arrived = lax.all_to_all(outgoing, "req", split_axis=0, concat_axis=0, tiled=True)
    rows_full = lax.all_gather(arrived, "exp", axis=1, tiled=True)
    gate_h = jnp.dot(rows_full, w_gate[0], preferred_element_type=jnp.float32)
    up_h = jnp.dot(rows_full, w_up[0], preferred_element_type=jnp.float32)
    active = (jax.nn.silu(gate_h) * up_h).astype(jnp.bfloat16)
    partial_value = lax.optimization_barrier(
        jnp.dot(active, w_down[0], preferred_element_type=jnp.float32).astype(jnp.bfloat16)
    )
    summed_value = lax.psum_scatter(partial_value, "exp", scatter_dimension=1, tiled=True)
    lookup = target_dev * CAP + slot_index
    returned = lax.all_to_all(summed_value, "req", split_axis=0, concat_axis=0, tiled=True)
    taken_rows = jnp.take(returned, lookup, axis=0).reshape(row_req, 2, -1).astype(jnp.float32)
    expert_part = gate_first[:, None] * taken_rows[:, 0] + gate_second[:, None] * taken_rows[:, 1]
    mixed = hidden + expert_part
    return (mixed, new_pages)


def solution(mesh):
    in_specs = (
        P("req", None),
        P("req", "exp"),
        P("req", "exp"),
        P("exp", None),
        P("exp"),
        P("req", None, "exp"),
        P("req", None),
        P("req"),
        P(),
        P("req", None),
        P("req", None, "exp"),
        P("req", None, "exp"),
        P("req", "exp", None),
    )
    out_specs = (P("req", "exp"), P("req", None, None, "exp"))
    return jax.shard_map(body, mesh=mesh, in_specs=in_specs, out_specs=out_specs, check_vma=False)
```

```python
import jax
import jax.numpy as jnp
from jax import lax
from jax.sharding import PartitionSpec as P

D = 4096
CAP = 32
MIG_PAIR = 4


EPSILON = 1e-05


def pick_rows(source, row_index, live_slot):
    taken_rows = jnp.take(source, row_index, axis=0)
    return jnp.where(live_slot[:, None], taken_rows, jnp.zeros((), source.dtype))


def body(
    attention_out,
    residual,
    w_out,
    router_w,
    norm_gain,
    page_pool,
    page_table,
    cache_len,
    came_from,
    routes,
    w_gate,
    w_up,
    w_down,
):
    groups = lax.axis_size("req")
    own_group = lax.axis_index("req")
    row_req = attention_out.shape[0]
    rows_all = came_from.shape[0]
    pages_req = page_table.shape[1]
    page_len = page_pool.shape[1]
    kv_slice = page_pool.shape[2]
    experts = groups // 2
    targets = jnp.arange(groups, dtype=jnp.int32)
    local_ids = jnp.arange(row_req, dtype=jnp.int32)
    dest_of = (
        jnp.zeros((rows_all,), jnp.int32).at[came_from].set(jnp.arange(rows_all, dtype=jnp.int32))
    )
    dest_group = dest_of // row_req
    dest_hot = (
        (dest_group[:, None] == targets[None, :]).astype(jnp.int32).reshape(groups, row_req, groups)
    )
    pair_rank = jnp.sum((jnp.cumsum(dest_hot, axis=1) - dest_hot) * dest_hot, axis=2).reshape(
        rows_all
    )
    own_dest = lax.dynamic_slice_in_dim(dest_group, own_group * row_req, row_req)
    own_rank = lax.dynamic_slice_in_dim(pair_rank, own_group * row_req, row_req)
    chosen_send = (
        (own_dest[None, None, :] == targets[:, None, None])
        & (own_rank[None, None, :] == jnp.arange(MIG_PAIR, dtype=jnp.int32)[None, :, None])
        & (targets[:, None, None] != own_group)
    )
    send_index = jnp.sum(jnp.where(chosen_send, local_ids[None, None, :], 0), axis=2).reshape(-1)
    send_live = jnp.any(chosen_send, axis=2).reshape(-1)
    moved_attn, moved_resid = (
        lax.all_to_all(
            pick_rows(attention_out, send_index, send_live),
            "req",
            split_axis=0,
            concat_axis=0,
            tiled=True,
        ),
        lax.all_to_all(
            pick_rows(residual, send_index, send_live),
            "req",
            split_axis=0,
            concat_axis=0,
            tiled=True,
        ),
    )
    new_source = lax.dynamic_slice_in_dim(came_from, own_group * row_req, row_req)
    source_group = new_source // row_req
    stays_home = source_group == own_group
    arrival = jnp.where(
        stays_home,
        new_source - own_group * row_req,
        row_req + source_group * MIG_PAIR + jnp.take(pair_rank, new_source),
    )
    attn_new = jnp.take(jnp.concatenate([attention_out, moved_attn], axis=0), arrival, axis=0)
    resid_new = jnp.take(jnp.concatenate([residual, moved_resid], axis=0), arrival, axis=0)
    projected = jnp.dot(
        attn_new,
        lax.all_gather(w_out, "req", axis=0, tiled=True),
        preferred_element_type=jnp.float32,
    )
    hidden = resid_new.astype(jnp.float32) + projected
    squares = jnp.sum(hidden * hidden, axis=1)
    scaled = hidden * norm_gain[None, :]
    raw_logits = jnp.dot(scaled, router_w, precision=lax.Precision.HIGHEST)
    row_stats = lax.psum(jnp.concatenate([squares[:, None], raw_logits], axis=1), "exp")
    total_sq = row_stats[:, 0]
    inverse = lax.rsqrt(total_sq / D + EPSILON)
    normed = scaled * inverse[:, None]
    logits = row_stats[:, 1:] * inverse[:, None]
    normed_rows = normed.astype(jnp.bfloat16)
    expert_ids = jnp.arange(experts, dtype=jnp.int32)
    chosen = jnp.sum(
        jnp.where(routes[:, :, None] == expert_ids[None, None, :], logits[:, None, :], 0.0), axis=2
    )
    gate_first = jax.nn.sigmoid(chosen[:, 0] - chosen[:, 1])
    gate_second = jax.nn.sigmoid(chosen[:, 1] - chosen[:, 0])
    flat_routes = routes.reshape(-1)
    expert_hot = (flat_routes[:, None] == expert_ids[None, :]).astype(jnp.int32)
    expert_rank = jnp.sum((jnp.cumsum(expert_hot, axis=0) - expert_hot) * expert_hot, axis=1)
    target_dev = flat_routes + experts * (expert_rank % 2)
    slot_index = expert_rank // 2
    assign_ids = jnp.arange(flat_routes.shape[0], dtype=jnp.int32)
    chosen_slot = (target_dev[None, None, :] == targets[:, None, None]) & (
        slot_index[None, None, :] == jnp.arange(CAP, dtype=jnp.int32)[None, :, None]
    )
    slot_source = jnp.sum(
        jnp.where(chosen_slot, assign_ids[None, None, :] // 2, 0), axis=2
    ).reshape(-1)
    slot_live = jnp.any(chosen_slot, axis=2).reshape(-1)
    outgoing = pick_rows(normed_rows, slot_source, slot_live)
    arrived = lax.all_to_all(outgoing, "req", split_axis=0, concat_axis=0, tiled=True)
    half = arrived.shape[0] // 2
    summed_parts = []
    for part in range(2):
        rows_full = lax.all_gather(
            arrived[part * half:(part + 1) * half], "exp", axis=1, tiled=True
        )
        gate_h = jnp.dot(rows_full, w_gate[0], preferred_element_type=jnp.float32)
        up_h = jnp.dot(rows_full, w_up[0], preferred_element_type=jnp.float32)
        active = (jax.nn.silu(gate_h) * up_h).astype(jnp.bfloat16)
        partial_value = lax.optimization_barrier(
            jnp.dot(active, w_down[0], preferred_element_type=jnp.float32).astype(jnp.bfloat16)
        )
        if part == 1:
            partial_value, page_pool = lax.optimization_barrier((partial_value, page_pool))
        summed_parts.append(
            lax.psum_scatter(partial_value, "exp", scatter_dimension=1, tiled=True)
        )
    summed_value = jnp.concatenate(summed_parts, axis=0)
    page_rows = jnp.take(page_pool, page_table.reshape(-1), axis=0).reshape(
        row_req, pages_req, page_len, kv_slice
    )
    position = (
        jnp.arange(pages_req, dtype=jnp.int32)[:, None] * page_len
        + jnp.arange(page_len, dtype=jnp.int32)[None, :]
    )
    kept_mask = position[None, :, :] < cache_len[:, None, None]
    page_rows = jnp.where(kept_mask[..., None], page_rows, jnp.zeros((), page_rows.dtype)).reshape(
        row_req, -1
    )
    moved_pages = lax.all_to_all(
        pick_rows(page_rows, send_index, send_live), "req", split_axis=0, concat_axis=0, tiled=True
    )
    new_pages = jnp.take(
        jnp.concatenate([page_rows, moved_pages], axis=0), arrival, axis=0
    ).reshape(row_req, pages_req, page_len, kv_slice)
    lookup = target_dev * CAP + slot_index
    returned = lax.all_to_all(summed_value, "req", split_axis=0, concat_axis=0, tiled=True)
    taken_rows = jnp.take(returned, lookup, axis=0).reshape(row_req, 2, -1).astype(jnp.float32)
    expert_part = gate_first[:, None] * taken_rows[:, 0] + gate_second[:, None] * taken_rows[:, 1]
    mixed = hidden + expert_part
    return (mixed, new_pages)


def solution(mesh):
    in_specs = (
        P("req", None),
        P("req", "exp"),
        P("req", "exp"),
        P("exp", None),
        P("exp"),
        P("req", None, "exp"),
        P("req", None),
        P("req"),
        P(),
        P("req", None),
        P("req", None, "exp"),
        P("req", None, "exp"),
        P("req", "exp", None),
    )
    out_specs = (P("req", "exp"), P("req", None, None, "exp"))
    return jax.shard_map(body, mesh=mesh, in_specs=in_specs, out_specs=out_specs, check_vma=False)
```

```python
import jax
import jax.numpy as jnp
from jax import lax
from jax.sharding import PartitionSpec as P

D = 4096
CAP = 32
MIG_PAIR = 4


EPSILON = 1e-05


def pick_rows(source, row_index, live_slot):
    taken_rows = jnp.take(source, row_index, axis=0)
    return jnp.where(live_slot[:, None], taken_rows, jnp.zeros((), source.dtype))


def body(
    attention_out,
    residual,
    w_out,
    router_w,
    norm_gain,
    page_pool,
    page_table,
    cache_len,
    came_from,
    routes,
    w_gate,
    w_up,
    w_down,
):
    groups = lax.axis_size("req")
    own_group = lax.axis_index("req")
    row_req = attention_out.shape[0]
    rows_all = came_from.shape[0]
    pages_req = page_table.shape[1]
    page_len = page_pool.shape[1]
    kv_slice = page_pool.shape[2]
    experts = groups // 2
    targets = jnp.arange(groups, dtype=jnp.int32)
    local_ids = jnp.arange(row_req, dtype=jnp.int32)
    dest_of = (
        jnp.zeros((rows_all,), jnp.int32).at[came_from].set(jnp.arange(rows_all, dtype=jnp.int32))
    )
    dest_group = dest_of // row_req
    dest_hot = (
        (dest_group[:, None] == targets[None, :]).astype(jnp.int32).reshape(groups, row_req, groups)
    )
    pair_rank = jnp.sum((jnp.cumsum(dest_hot, axis=1) - dest_hot) * dest_hot, axis=2).reshape(
        rows_all
    )
    own_dest = lax.dynamic_slice_in_dim(dest_group, own_group * row_req, row_req)
    own_rank = lax.dynamic_slice_in_dim(pair_rank, own_group * row_req, row_req)
    chosen_send = (
        (own_dest[None, None, :] == targets[:, None, None])
        & (own_rank[None, None, :] == jnp.arange(MIG_PAIR, dtype=jnp.int32)[None, :, None])
        & (targets[:, None, None] != own_group)
    )
    send_index = jnp.sum(jnp.where(chosen_send, local_ids[None, None, :], 0), axis=2).reshape(-1)
    send_live = jnp.any(chosen_send, axis=2).reshape(-1)
    moved_attn, moved_resid = (
        lax.all_to_all(
            pick_rows(attention_out, send_index, send_live),
            "req",
            split_axis=0,
            concat_axis=0,
            tiled=True,
        ),
        lax.all_to_all(
            pick_rows(residual, send_index, send_live),
            "req",
            split_axis=0,
            concat_axis=0,
            tiled=True,
        ),
    )
    new_source = lax.dynamic_slice_in_dim(came_from, own_group * row_req, row_req)
    source_group = new_source // row_req
    stays_home = source_group == own_group
    arrival = jnp.where(
        stays_home,
        new_source - own_group * row_req,
        row_req + source_group * MIG_PAIR + jnp.take(pair_rank, new_source),
    )
    attn_new = jnp.take(jnp.concatenate([attention_out, moved_attn], axis=0), arrival, axis=0)
    resid_new = jnp.take(jnp.concatenate([residual, moved_resid], axis=0), arrival, axis=0)
    projected = jnp.dot(
        attn_new,
        lax.all_gather(w_out, "req", axis=0, tiled=True),
        preferred_element_type=jnp.float32,
    )
    hidden = resid_new.astype(jnp.float32) + projected
    squares = jnp.sum(hidden * hidden, axis=1)
    scaled = hidden * norm_gain[None, :]
    raw_logits = jnp.dot(scaled, router_w, precision=lax.Precision.HIGHEST)
    row_stats = lax.psum(jnp.concatenate([squares[:, None], raw_logits], axis=1), "exp")
    total_sq = row_stats[:, 0]
    inverse = lax.rsqrt(total_sq / D + EPSILON)
    normed = scaled * inverse[:, None]
    logits = row_stats[:, 1:] * inverse[:, None]
    normed_rows = normed.astype(jnp.bfloat16)
    expert_ids = jnp.arange(experts, dtype=jnp.int32)
    chosen = jnp.sum(
        jnp.where(routes[:, :, None] == expert_ids[None, None, :], logits[:, None, :], 0.0), axis=2
    )
    gate_first = jax.nn.sigmoid(chosen[:, 0] - chosen[:, 1])
    gate_second = jax.nn.sigmoid(chosen[:, 1] - chosen[:, 0])
    flat_routes = routes.reshape(-1)
    expert_hot = (flat_routes[:, None] == expert_ids[None, :]).astype(jnp.int32)
    expert_rank = jnp.sum((jnp.cumsum(expert_hot, axis=0) - expert_hot) * expert_hot, axis=1)
    target_dev = flat_routes + experts * (expert_rank % 2)
    slot_index = expert_rank // 2
    assign_ids = jnp.arange(flat_routes.shape[0], dtype=jnp.int32)
    chosen_slot = (target_dev[None, None, :] == targets[:, None, None]) & (
        slot_index[None, None, :] == jnp.arange(CAP, dtype=jnp.int32)[None, :, None]
    )
    slot_source = jnp.sum(
        jnp.where(chosen_slot, assign_ids[None, None, :] // 2, 0), axis=2
    ).reshape(-1)
    slot_live = jnp.any(chosen_slot, axis=2).reshape(-1)
    outgoing = pick_rows(normed_rows, slot_source, slot_live)
    arrived = lax.all_to_all(outgoing, "req", split_axis=0, concat_axis=0, tiled=True)
    rows_full = lax.all_gather(arrived, "exp", axis=1, tiled=True)
    gate_h = jnp.dot(rows_full, w_gate[0], preferred_element_type=jnp.float32)
    up_h = jnp.dot(rows_full, w_up[0], preferred_element_type=jnp.float32)
    active = (jax.nn.silu(gate_h) * up_h).astype(jnp.bfloat16)
    partial_value = lax.optimization_barrier(
        jnp.dot(active, w_down[0], preferred_element_type=jnp.float32).astype(jnp.bfloat16)
    )
    partial_value, page_pool = lax.optimization_barrier((partial_value, page_pool))
    summed_value = lax.psum_scatter(partial_value, "exp", scatter_dimension=1, tiled=True)
    page_rows = jnp.take(page_pool, page_table.reshape(-1), axis=0).reshape(
        row_req, pages_req, page_len, kv_slice
    )
    position = (
        jnp.arange(pages_req, dtype=jnp.int32)[:, None] * page_len
        + jnp.arange(page_len, dtype=jnp.int32)[None, :]
    )
    kept_mask = position[None, :, :] < cache_len[:, None, None]
    page_rows = jnp.where(kept_mask[..., None], page_rows, jnp.zeros((), page_rows.dtype)).reshape(
        row_req, -1
    )
    moved_pages = lax.all_to_all(
        pick_rows(page_rows, send_index, send_live), "req", split_axis=0, concat_axis=0, tiled=True
    )
    new_pages = jnp.take(
        jnp.concatenate([page_rows, moved_pages], axis=0), arrival, axis=0
    ).reshape(row_req, pages_req, page_len, kv_slice)
    lookup = target_dev * CAP + slot_index
    returned = lax.all_to_all(summed_value, "req", split_axis=0, concat_axis=0, tiled=True)
    taken_rows = jnp.take(returned, lookup, axis=0).reshape(row_req, 2, -1).astype(jnp.float32)
    expert_part = gate_first[:, None] * taken_rows[:, 0] + gate_second[:, None] * taken_rows[:, 1]
    mixed = hidden + expert_part
    return (mixed, new_pages)


def solution(mesh):
    in_specs = (
        P("req", None),
        P("req", "exp"),
        P("req", "exp"),
        P("exp", None),
        P("exp"),
        P("req", None, "exp"),
        P("req", None),
        P("req"),
        P(),
        P("req", None),
        P("req", None, "exp"),
        P("req", None, "exp"),
        P("req", "exp", None),
    )
    out_specs = (P("req", "exp"), P("req", None, None, "exp"))
    return jax.shard_map(body, mesh=mesh, in_specs=in_specs, out_specs=out_specs, check_vma=False)
```

```python
import jax
import jax.numpy as jnp
from jax import lax
from jax.experimental import pallas as pl
from jax.experimental.pallas import tpu as pltpu
from jax.sharding import PartitionSpec as P
import functools

D = 4096
CAP = 32
MIG_PAIR = 4


EPSILON = 1e-05

MESH = pl.DeviceIdType.MESH


def exchange_kernel(axis, n, gather, x_ref, y_ref, send_sems, recv_sems):
    me = lax.axis_index(axis)
    barrier = pltpu.get_barrier_semaphore()
    for k in range(1, n):
        pl.semaphore_signal(
            barrier, inc=1, device_id={axis: lax.rem(me + k, n)}, device_id_type=MESH
        )
    pl.semaphore_wait(barrier, n - 1)
    copies = []
    for k in range(1, n):
        peer = lax.rem(me + k, n)
        copy = pltpu.make_async_remote_copy(
            src_ref=x_ref if gather else x_ref.at[peer],
            dst_ref=y_ref.at[me],
            send_sem=send_sems.at[k],
            recv_sem=recv_sems.at[k],
            device_id={axis: peer},
            device_id_type=MESH,
        )
        copy.start()
        copies.append(copy)
    if gather:
        y_ref[me] = x_ref[...]
    else:
        y_ref[me] = x_ref[me]
    for k in range(1, n):
        copies[k - 1].wait_send()
        source = lax.rem(me + n - k, n)
        pltpu.make_async_remote_copy(
            src_ref=x_ref if gather else x_ref.at[source],
            dst_ref=y_ref.at[source],
            send_sem=send_sems.at[k],
            recv_sem=recv_sems.at[k],
            device_id={axis: source},
            device_id_type=MESH,
        ).wait_recv()


def exchange(x, axis, n, gather, collective_id):
    out_shape = (n,) + x.shape if gather else x.shape
    return pl.pallas_call(
        functools.partial(exchange_kernel, axis, n, gather),
        out_shape=jax.ShapeDtypeStruct(out_shape, x.dtype),
        in_specs=[pl.BlockSpec(memory_space=pltpu.VMEM)],
        out_specs=pl.BlockSpec(memory_space=pltpu.VMEM),
        scratch_shapes=[pltpu.SemaphoreType.DMA((n,)), pltpu.SemaphoreType.DMA((n,))],
        compiler_params=pltpu.CompilerParams(collective_id=collective_id, has_side_effects=True),
    )(x)


def pick_rows(source, row_index, live_slot):
    taken_rows = jnp.take(source, row_index, axis=0)
    return jnp.where(live_slot[:, None], taken_rows, jnp.zeros((), source.dtype))


def body(
    attention_out,
    residual,
    w_out,
    router_w,
    norm_gain,
    page_pool,
    page_table,
    cache_len,
    came_from,
    routes,
    w_gate,
    w_up,
    w_down,
):
    groups = lax.axis_size("req")
    own_group = lax.axis_index("req")
    row_req = attention_out.shape[0]
    rows_all = came_from.shape[0]
    pages_req = page_table.shape[1]
    page_len = page_pool.shape[1]
    kv_slice = page_pool.shape[2]
    experts = groups // 2
    targets = jnp.arange(groups, dtype=jnp.int32)
    local_ids = jnp.arange(row_req, dtype=jnp.int32)
    dest_of = (
        jnp.zeros((rows_all,), jnp.int32).at[came_from].set(jnp.arange(rows_all, dtype=jnp.int32))
    )
    dest_group = dest_of // row_req
    dest_hot = (
        (dest_group[:, None] == targets[None, :]).astype(jnp.int32).reshape(groups, row_req, groups)
    )
    pair_rank = jnp.sum((jnp.cumsum(dest_hot, axis=1) - dest_hot) * dest_hot, axis=2).reshape(
        rows_all
    )
    own_dest = lax.dynamic_slice_in_dim(dest_group, own_group * row_req, row_req)
    own_rank = lax.dynamic_slice_in_dim(pair_rank, own_group * row_req, row_req)
    chosen_send = (
        (own_dest[None, None, :] == targets[:, None, None])
        & (own_rank[None, None, :] == jnp.arange(MIG_PAIR, dtype=jnp.int32)[None, :, None])
        & (targets[:, None, None] != own_group)
    )
    send_index = jnp.sum(jnp.where(chosen_send, local_ids[None, None, :], 0), axis=2).reshape(-1)
    send_live = jnp.any(chosen_send, axis=2).reshape(-1)
    moved_attn, moved_resid = (
        lax.all_to_all(
            pick_rows(attention_out, send_index, send_live),
            "req",
            split_axis=0,
            concat_axis=0,
            tiled=True,
        ),
        lax.all_to_all(
            pick_rows(residual, send_index, send_live),
            "req",
            split_axis=0,
            concat_axis=0,
            tiled=True,
        ),
    )
    new_source = lax.dynamic_slice_in_dim(came_from, own_group * row_req, row_req)
    source_group = new_source // row_req
    stays_home = source_group == own_group
    arrival = jnp.where(
        stays_home,
        new_source - own_group * row_req,
        row_req + source_group * MIG_PAIR + jnp.take(pair_rank, new_source),
    )
    attn_new = jnp.take(jnp.concatenate([attention_out, moved_attn], axis=0), arrival, axis=0)
    resid_new = jnp.take(jnp.concatenate([residual, moved_resid], axis=0), arrival, axis=0)
    projected = jnp.dot(
        attn_new,
        lax.all_gather(w_out, "req", axis=0, tiled=True),
        preferred_element_type=jnp.float32,
    )
    hidden = resid_new.astype(jnp.float32) + projected
    squares = jnp.sum(hidden * hidden, axis=1)
    scaled = hidden * norm_gain[None, :]
    raw_logits = jnp.dot(scaled, router_w, precision=lax.Precision.HIGHEST)
    stats_t = jnp.concatenate([squares[None, :], raw_logits.T], axis=0)
    stats_t = jnp.pad(stats_t, ((0, 16 - stats_t.shape[0]), (0, 0)))
    n_exp = lax.axis_size("exp")
    row_stats = jnp.sum(exchange(stats_t, "exp", n_exp, True, 0), axis=0)[:9].T
    total_sq = row_stats[:, 0]
    inverse = lax.rsqrt(total_sq / D + EPSILON)
    normed = scaled * inverse[:, None]
    logits = row_stats[:, 1:] * inverse[:, None]
    normed_rows = normed.astype(jnp.bfloat16)
    expert_ids = jnp.arange(experts, dtype=jnp.int32)
    chosen = jnp.sum(
        jnp.where(routes[:, :, None] == expert_ids[None, None, :], logits[:, None, :], 0.0), axis=2
    )
    gate_first = jax.nn.sigmoid(chosen[:, 0] - chosen[:, 1])
    gate_second = jax.nn.sigmoid(chosen[:, 1] - chosen[:, 0])
    flat_routes = routes.reshape(-1)
    expert_hot = (flat_routes[:, None] == expert_ids[None, :]).astype(jnp.int32)
    expert_rank = jnp.sum((jnp.cumsum(expert_hot, axis=0) - expert_hot) * expert_hot, axis=1)
    target_dev = flat_routes + experts * (expert_rank % 2)
    slot_index = expert_rank // 2
    assign_ids = jnp.arange(flat_routes.shape[0], dtype=jnp.int32)
    chosen_slot = (target_dev[None, None, :] == targets[:, None, None]) & (
        slot_index[None, None, :] == jnp.arange(CAP, dtype=jnp.int32)[None, :, None]
    )
    slot_source = jnp.sum(
        jnp.where(chosen_slot, assign_ids[None, None, :] // 2, 0), axis=2
    ).reshape(-1)
    slot_live = jnp.any(chosen_slot, axis=2).reshape(-1)
    outgoing = pick_rows(normed_rows, slot_source, slot_live)
    arrived = exchange(
        outgoing.reshape(groups, -1, outgoing.shape[-1]), "req", groups, False, 1
    ).reshape(outgoing.shape)
    rows_full = lax.all_gather(arrived, "exp", axis=1, tiled=True)
    gate_h = jnp.dot(rows_full, w_gate[0], preferred_element_type=jnp.float32)
    up_h = jnp.dot(rows_full, w_up[0], preferred_element_type=jnp.float32)
    active = (jax.nn.silu(gate_h) * up_h).astype(jnp.bfloat16)
    partial_value = lax.optimization_barrier(
        jnp.dot(active, w_down[0], preferred_element_type=jnp.float32).astype(jnp.bfloat16)
    )
    partial_value, page_pool = lax.optimization_barrier((partial_value, page_pool))
    summed_value = lax.psum_scatter(partial_value, "exp", scatter_dimension=1, tiled=True)
    page_rows = jnp.take(page_pool, page_table.reshape(-1), axis=0).reshape(
        row_req, pages_req, page_len, kv_slice
    )
    position = (
        jnp.arange(pages_req, dtype=jnp.int32)[:, None] * page_len
        + jnp.arange(page_len, dtype=jnp.int32)[None, :]
    )
    kept_mask = position[None, :, :] < cache_len[:, None, None]
    page_rows = jnp.where(kept_mask[..., None], page_rows, jnp.zeros((), page_rows.dtype)).reshape(
        row_req, -1
    )
    moved_pages = lax.all_to_all(
        pick_rows(page_rows, send_index, send_live), "req", split_axis=0, concat_axis=0, tiled=True
    )
    new_pages = jnp.take(
        jnp.concatenate([page_rows, moved_pages], axis=0), arrival, axis=0
    ).reshape(row_req, pages_req, page_len, kv_slice)
    lookup = target_dev * CAP + slot_index
    returned = exchange(
        summed_value.reshape(groups, -1, summed_value.shape[-1]), "req", groups, False, 2
    ).reshape(summed_value.shape)
    taken_rows = jnp.take(returned, lookup, axis=0).reshape(row_req, 2, -1).astype(jnp.float32)
    expert_part = gate_first[:, None] * taken_rows[:, 0] + gate_second[:, None] * taken_rows[:, 1]
    mixed = hidden + expert_part
    return (mixed, new_pages)


def solution(mesh):
    in_specs = (
        P("req", None),
        P("req", "exp"),
        P("req", "exp"),
        P("exp", None),
        P("exp"),
        P("req", None, "exp"),
        P("req", None),
        P("req"),
        P(),
        P("req", None),
        P("req", None, "exp"),
        P("req", None, "exp"),
        P("req", "exp", None),
    )
    out_specs = (P("req", "exp"), P("req", None, None, "exp"))
    return jax.shard_map(body, mesh=mesh, in_specs=in_specs, out_specs=out_specs, check_vma=False)
```

```python
import jax
import jax.numpy as jnp
from jax import lax
from jax.experimental import pallas as pl
from jax.experimental.pallas import tpu as pltpu
from jax.sharding import PartitionSpec as P
import functools

D = 4096
CAP = 32
MIG_PAIR = 4


EPSILON = 1e-05

MESH = pl.DeviceIdType.MESH


def exchange_kernel(axis, n, gather, x_ref, y_ref, send_sems, recv_sems):
    me = lax.axis_index(axis)
    barrier = pltpu.get_barrier_semaphore()
    for k in range(1, n):
        pl.semaphore_signal(
            barrier, inc=1, device_id={axis: lax.rem(me + k, n)}, device_id_type=MESH
        )
    pl.semaphore_wait(barrier, n - 1)
    copies = []
    for k in range(1, n):
        peer = lax.rem(me + k, n)
        copy = pltpu.make_async_remote_copy(
            src_ref=x_ref if gather else x_ref.at[peer],
            dst_ref=y_ref.at[me],
            send_sem=send_sems.at[k],
            recv_sem=recv_sems.at[k],
            device_id={axis: peer},
            device_id_type=MESH,
        )
        copy.start()
        copies.append(copy)
    if gather:
        y_ref[me] = x_ref[...]
    else:
        y_ref[me] = x_ref[me]
    for k in range(1, n):
        copies[k - 1].wait_send()
        source = lax.rem(me + n - k, n)
        pltpu.make_async_remote_copy(
            src_ref=x_ref if gather else x_ref.at[source],
            dst_ref=y_ref.at[source],
            send_sem=send_sems.at[k],
            recv_sem=recv_sems.at[k],
            device_id={axis: source},
            device_id_type=MESH,
        ).wait_recv()


def exchange(x, axis, n, gather, collective_id):
    out_shape = (n,) + x.shape if gather else x.shape
    return pl.pallas_call(
        functools.partial(exchange_kernel, axis, n, gather),
        out_shape=jax.ShapeDtypeStruct(out_shape, x.dtype),
        in_specs=[pl.BlockSpec(memory_space=pltpu.VMEM)],
        out_specs=pl.BlockSpec(memory_space=pltpu.VMEM),
        scratch_shapes=[pltpu.SemaphoreType.DMA((n,)), pltpu.SemaphoreType.DMA((n,))],
        compiler_params=pltpu.CompilerParams(collective_id=collective_id, has_side_effects=True),
    )(x)


def exp_gather_kernel(n, x_ref, y_ref, send_sems, recv_sems):
    chips = n // 2
    width = x_ref.shape[1]
    half = x_ref.shape[0] // 2
    me = lax.axis_index("exp")
    z, core = me // 2, me % 2
    sib = 2 * z + 1 - core
    up = 2 * lax.rem(z + 1, chips) + core
    dn = 2 * lax.rem(z + chips - 1, chips) + core
    far = 2 * lax.rem(z + 2, chips) + core

    def cols(block):
        return pl.ds(pl.multiple_of(block * width, width), width)

    def rows(part):
        return pl.ds(part * half, half)

    barrier = pltpu.get_barrier_semaphore()
    for peer in (sib, up, dn):
        pl.semaphore_signal(barrier, inc=1, device_id={"exp": peer}, device_id_type=MESH)
    pl.semaphore_wait(barrier, 3)

    def remote(src, dst, slot, peer):
        return pltpu.make_async_remote_copy(
            src_ref=src, dst_ref=dst, send_sem=send_sems.at[slot],
            recv_sem=recv_sems.at[slot], device_id={"exp": peer}, device_id_type=MESH,
        )

    own_cols = cols(me)
    first = [
        remote(x_ref, y_ref.at[:, own_cols], 0, up),
        remote(x_ref, y_ref.at[:, own_cols], 1, dn),
        remote(x_ref, y_ref.at[:, own_cols], 2, sib),
    ]
    for copy in first:
        copy.start()
    y_ref[:, own_cols] = x_ref[...]
    remote(x_ref, y_ref.at[:, cols(dn)], 0, dn).wait_recv()
    remote(x_ref, y_ref.at[:, cols(up)], 1, up).wait_recv()
    second = [
        remote(y_ref.at[rows(1), cols(dn)], y_ref.at[rows(1), cols(dn)], 3, up),
        remote(y_ref.at[rows(0), cols(up)], y_ref.at[rows(0), cols(up)], 4, dn),
        remote(y_ref.at[:, cols(dn)], y_ref.at[:, cols(dn)], 5, sib),
        remote(y_ref.at[:, cols(up)], y_ref.at[:, cols(up)], 6, sib),
    ]
    for copy in second:
        copy.start()
    remote(y_ref.at[rows(1), cols(far)], y_ref.at[rows(1), cols(far)], 3, dn).wait_recv()
    remote(y_ref.at[rows(0), cols(far)], y_ref.at[rows(0), cols(far)], 4, up).wait_recv()
    third = remote(y_ref.at[:, cols(far)], y_ref.at[:, cols(far)], 7, sib)
    third.start()
    sib_z = 2 * z + 1 - core
    sib_up = 2 * lax.rem(z + 1, chips) + 1 - core
    sib_dn = 2 * lax.rem(z + chips - 1, chips) + 1 - core
    sib_far = 2 * lax.rem(z + 2, chips) + 1 - core
    remote(x_ref, y_ref.at[:, cols(sib_z)], 2, sib).wait_recv()
    remote(y_ref.at[:, cols(sib_dn)], y_ref.at[:, cols(sib_dn)], 5, sib).wait_recv()
    remote(y_ref.at[:, cols(sib_up)], y_ref.at[:, cols(sib_up)], 6, sib).wait_recv()
    remote(y_ref.at[:, cols(sib_far)], y_ref.at[:, cols(sib_far)], 7, sib).wait_recv()
    for copy in first + second + [third]:
        copy.wait_send()


def exp_gather(x, n, collective_id):
    return pl.pallas_call(
        functools.partial(exp_gather_kernel, n),
        out_shape=jax.ShapeDtypeStruct((x.shape[0], n * x.shape[1]), x.dtype),
        in_specs=[pl.BlockSpec(memory_space=pltpu.VMEM)],
        out_specs=pl.BlockSpec(memory_space=pltpu.VMEM),
        scratch_shapes=[pltpu.SemaphoreType.DMA((8,)), pltpu.SemaphoreType.DMA((8,))],
        compiler_params=pltpu.CompilerParams(collective_id=collective_id, has_side_effects=True),
    )(x)


def pick_rows(source, row_index, live_slot):
    taken_rows = jnp.take(source, row_index, axis=0)
    return jnp.where(live_slot[:, None], taken_rows, jnp.zeros((), source.dtype))


def body(
    attention_out,
    residual,
    w_out,
    router_w,
    norm_gain,
    page_pool,
    page_table,
    cache_len,
    came_from,
    routes,
    w_gate,
    w_up,
    w_down,
):
    groups = lax.axis_size("req")
    own_group = lax.axis_index("req")
    row_req = attention_out.shape[0]
    rows_all = came_from.shape[0]
    pages_req = page_table.shape[1]
    page_len = page_pool.shape[1]
    kv_slice = page_pool.shape[2]
    experts = groups // 2
    targets = jnp.arange(groups, dtype=jnp.int32)
    local_ids = jnp.arange(row_req, dtype=jnp.int32)
    dest_of = (
        jnp.zeros((rows_all,), jnp.int32).at[came_from].set(jnp.arange(rows_all, dtype=jnp.int32))
    )
    dest_group = dest_of // row_req
    dest_hot = (
        (dest_group[:, None] == targets[None, :]).astype(jnp.int32).reshape(groups, row_req, groups)
    )
    pair_rank = jnp.sum((jnp.cumsum(dest_hot, axis=1) - dest_hot) * dest_hot, axis=2).reshape(
        rows_all
    )
    own_dest = lax.dynamic_slice_in_dim(dest_group, own_group * row_req, row_req)
    own_rank = lax.dynamic_slice_in_dim(pair_rank, own_group * row_req, row_req)
    chosen_send = (
        (own_dest[None, None, :] == targets[:, None, None])
        & (own_rank[None, None, :] == jnp.arange(MIG_PAIR, dtype=jnp.int32)[None, :, None])
        & (targets[:, None, None] != own_group)
    )
    send_index = jnp.sum(jnp.where(chosen_send, local_ids[None, None, :], 0), axis=2).reshape(-1)
    send_live = jnp.any(chosen_send, axis=2).reshape(-1)
    moved_attn, moved_resid = (
        lax.all_to_all(
            pick_rows(attention_out, send_index, send_live),
            "req",
            split_axis=0,
            concat_axis=0,
            tiled=True,
        ),
        lax.all_to_all(
            pick_rows(residual, send_index, send_live),
            "req",
            split_axis=0,
            concat_axis=0,
            tiled=True,
        ),
    )
    new_source = lax.dynamic_slice_in_dim(came_from, own_group * row_req, row_req)
    source_group = new_source // row_req
    stays_home = source_group == own_group
    arrival = jnp.where(
        stays_home,
        new_source - own_group * row_req,
        row_req + source_group * MIG_PAIR + jnp.take(pair_rank, new_source),
    )
    attn_new = jnp.take(jnp.concatenate([attention_out, moved_attn], axis=0), arrival, axis=0)
    resid_new = jnp.take(jnp.concatenate([residual, moved_resid], axis=0), arrival, axis=0)
    projected = jnp.dot(
        attn_new,
        lax.all_gather(w_out, "req", axis=0, tiled=True),
        preferred_element_type=jnp.float32,
    )
    hidden = resid_new.astype(jnp.float32) + projected
    squares = jnp.sum(hidden * hidden, axis=1)
    scaled = hidden * norm_gain[None, :]
    raw_logits = jnp.dot(scaled, router_w, precision=lax.Precision.HIGHEST)
    stats_t = jnp.concatenate([squares[None, :], raw_logits.T], axis=0)
    stats_t = jnp.pad(stats_t, ((0, 16 - stats_t.shape[0]), (0, 0)))
    n_exp = lax.axis_size("exp")
    row_stats = jnp.sum(exchange(stats_t, "exp", n_exp, True, 0), axis=0)[:9].T
    total_sq = row_stats[:, 0]
    inverse = lax.rsqrt(total_sq / D + EPSILON)
    normed = scaled * inverse[:, None]
    logits = row_stats[:, 1:] * inverse[:, None]
    normed_rows = normed.astype(jnp.bfloat16)
    expert_ids = jnp.arange(experts, dtype=jnp.int32)
    chosen = jnp.sum(
        jnp.where(routes[:, :, None] == expert_ids[None, None, :], logits[:, None, :], 0.0), axis=2
    )
    gate_first = jax.nn.sigmoid(chosen[:, 0] - chosen[:, 1])
    gate_second = jax.nn.sigmoid(chosen[:, 1] - chosen[:, 0])
    flat_routes = routes.reshape(-1)
    expert_hot = (flat_routes[:, None] == expert_ids[None, :]).astype(jnp.int32)
    expert_rank = jnp.sum((jnp.cumsum(expert_hot, axis=0) - expert_hot) * expert_hot, axis=1)
    target_dev = flat_routes + experts * (expert_rank % 2)
    slot_index = expert_rank // 2
    assign_ids = jnp.arange(flat_routes.shape[0], dtype=jnp.int32)
    chosen_slot = (target_dev[None, None, :] == targets[:, None, None]) & (
        slot_index[None, None, :] == jnp.arange(CAP, dtype=jnp.int32)[None, :, None]
    )
    slot_source = jnp.sum(
        jnp.where(chosen_slot, assign_ids[None, None, :] // 2, 0), axis=2
    ).reshape(-1)
    slot_live = jnp.any(chosen_slot, axis=2).reshape(-1)
    outgoing = pick_rows(normed_rows, slot_source, slot_live)
    arrived = exchange(
        outgoing.reshape(groups, -1, outgoing.shape[-1]), "req", groups, False, 1
    ).reshape(outgoing.shape)
    rows_full = exp_gather(arrived, lax.axis_size("exp"), 3)
    gate_h = jnp.dot(rows_full, w_gate[0], preferred_element_type=jnp.float32)
    up_h = jnp.dot(rows_full, w_up[0], preferred_element_type=jnp.float32)
    active = (jax.nn.silu(gate_h) * up_h).astype(jnp.bfloat16)
    partial_value = lax.optimization_barrier(
        jnp.dot(active, w_down[0], preferred_element_type=jnp.float32).astype(jnp.bfloat16)
    )
    partial_value, page_pool = lax.optimization_barrier((partial_value, page_pool))
    summed_value = lax.psum_scatter(partial_value, "exp", scatter_dimension=1, tiled=True)
    page_rows = jnp.take(page_pool, page_table.reshape(-1), axis=0).reshape(
        row_req, pages_req, page_len, kv_slice
    )
    position = (
        jnp.arange(pages_req, dtype=jnp.int32)[:, None] * page_len
        + jnp.arange(page_len, dtype=jnp.int32)[None, :]
    )
    kept_mask = position[None, :, :] < cache_len[:, None, None]
    page_rows = jnp.where(kept_mask[..., None], page_rows, jnp.zeros((), page_rows.dtype)).reshape(
        row_req, -1
    )
    moved_pages = lax.all_to_all(
        pick_rows(page_rows, send_index, send_live), "req", split_axis=0, concat_axis=0, tiled=True
    )
    new_pages = jnp.take(
        jnp.concatenate([page_rows, moved_pages], axis=0), arrival, axis=0
    ).reshape(row_req, pages_req, page_len, kv_slice)
    lookup = target_dev * CAP + slot_index
    returned = exchange(
        summed_value.reshape(groups, -1, summed_value.shape[-1]), "req", groups, False, 2
    ).reshape(summed_value.shape)
    taken_rows = jnp.take(returned, lookup, axis=0).reshape(row_req, 2, -1).astype(jnp.float32)
    expert_part = gate_first[:, None] * taken_rows[:, 0] + gate_second[:, None] * taken_rows[:, 1]
    mixed = hidden + expert_part
    return (mixed, new_pages)


def solution(mesh):
    in_specs = (
        P("req", None),
        P("req", "exp"),
        P("req", "exp"),
        P("exp", None),
        P("exp"),
        P("req", None, "exp"),
        P("req", None),
        P("req"),
        P(),
        P("req", None),
        P("req", None, "exp"),
        P("req", None, "exp"),
        P("req", "exp", None),
    )
    out_specs = (P("req", "exp"), P("req", None, None, "exp"))
    return jax.shard_map(body, mesh=mesh, in_specs=in_specs, out_specs=out_specs, check_vma=False)
```

```python
import jax
import jax.numpy as jnp
from jax import lax
from jax.experimental import pallas as pl
from jax.experimental.pallas import tpu as pltpu
from jax.sharding import PartitionSpec as P
import functools

D = 4096
CAP = 32
MIG_PAIR = 4


EPSILON = 1e-05

MESH = pl.DeviceIdType.MESH


def exchange_kernel(axis, n, gather, x_ref, y_ref, send_sems, recv_sems):
    me = lax.axis_index(axis)
    barrier = pltpu.get_barrier_semaphore()
    for k in range(1, n):
        pl.semaphore_signal(
            barrier, inc=1, device_id={axis: lax.rem(me + k, n)}, device_id_type=MESH
        )
    pl.semaphore_wait(barrier, n - 1)
    copies = []
    for k in range(1, n):
        peer = lax.rem(me + k, n)
        copy = pltpu.make_async_remote_copy(
            src_ref=x_ref if gather else x_ref.at[peer],
            dst_ref=y_ref.at[me],
            send_sem=send_sems.at[k],
            recv_sem=recv_sems.at[k],
            device_id={axis: peer},
            device_id_type=MESH,
        )
        copy.start()
        copies.append(copy)
    if gather:
        y_ref[me] = x_ref[...]
    else:
        y_ref[me] = x_ref[me]
    for k in range(1, n):
        copies[k - 1].wait_send()
        source = lax.rem(me + n - k, n)
        pltpu.make_async_remote_copy(
            src_ref=x_ref if gather else x_ref.at[source],
            dst_ref=y_ref.at[source],
            send_sem=send_sems.at[k],
            recv_sem=recv_sems.at[k],
            device_id={axis: source},
            device_id_type=MESH,
        ).wait_recv()


def exchange(x, axis, n, gather, collective_id):
    out_shape = (n,) + x.shape if gather else x.shape
    return pl.pallas_call(
        functools.partial(exchange_kernel, axis, n, gather),
        out_shape=jax.ShapeDtypeStruct(out_shape, x.dtype),
        in_specs=[pl.BlockSpec(memory_space=pltpu.VMEM)],
        out_specs=pl.BlockSpec(memory_space=pltpu.VMEM),
        scratch_shapes=[pltpu.SemaphoreType.DMA((n,)), pltpu.SemaphoreType.DMA((n,))],
        compiler_params=pltpu.CompilerParams(collective_id=collective_id, has_side_effects=True),
    )(x)


def exp_gather_kernel(n, x_ref, y_ref, send_sems, recv_sems):
    chips = n // 2
    width = x_ref.shape[1]
    half = x_ref.shape[0] // 2
    me = lax.axis_index("exp")
    z, core = me // 2, me % 2
    sib = 2 * z + 1 - core
    up = 2 * lax.rem(z + 1, chips) + core
    dn = 2 * lax.rem(z + chips - 1, chips) + core
    far = 2 * lax.rem(z + 2, chips) + core

    def cols(block):
        return pl.ds(pl.multiple_of(block * width, width), width)

    def rows(part):
        return pl.ds(part * half, half)

    barrier = pltpu.get_barrier_semaphore()
    for peer in (sib, up, dn):
        pl.semaphore_signal(barrier, inc=1, device_id={"exp": peer}, device_id_type=MESH)
    pl.semaphore_wait(barrier, 3)

    def remote(src, dst, slot, peer):
        return pltpu.make_async_remote_copy(
            src_ref=src, dst_ref=dst, send_sem=send_sems.at[slot],
            recv_sem=recv_sems.at[slot], device_id={"exp": peer}, device_id_type=MESH,
        )

    own_cols = cols(me)
    first = [
        remote(x_ref, y_ref.at[:, own_cols], 0, up),
        remote(x_ref, y_ref.at[:, own_cols], 1, dn),
        remote(x_ref, y_ref.at[:, own_cols], 2, sib),
    ]
    for copy in first:
        copy.start()
    y_ref[:, own_cols] = x_ref[...]
    remote(x_ref, y_ref.at[:, cols(dn)], 0, dn).wait_recv()
    remote(x_ref, y_ref.at[:, cols(up)], 1, up).wait_recv()
    second = [
        remote(y_ref.at[rows(1), cols(dn)], y_ref.at[rows(1), cols(dn)], 3, up),
        remote(y_ref.at[rows(0), cols(up)], y_ref.at[rows(0), cols(up)], 4, dn),
        remote(y_ref.at[:, cols(dn)], y_ref.at[:, cols(dn)], 5, sib),
        remote(y_ref.at[:, cols(up)], y_ref.at[:, cols(up)], 6, sib),
    ]
    for copy in second:
        copy.start()
    remote(y_ref.at[rows(1), cols(far)], y_ref.at[rows(1), cols(far)], 3, dn).wait_recv()
    remote(y_ref.at[rows(0), cols(far)], y_ref.at[rows(0), cols(far)], 4, up).wait_recv()
    third = remote(y_ref.at[:, cols(far)], y_ref.at[:, cols(far)], 7, sib)
    third.start()
    sib_z = 2 * z + 1 - core
    sib_up = 2 * lax.rem(z + 1, chips) + 1 - core
    sib_dn = 2 * lax.rem(z + chips - 1, chips) + 1 - core
    sib_far = 2 * lax.rem(z + 2, chips) + 1 - core
    remote(x_ref, y_ref.at[:, cols(sib_z)], 2, sib).wait_recv()
    remote(y_ref.at[:, cols(sib_dn)], y_ref.at[:, cols(sib_dn)], 5, sib).wait_recv()
    remote(y_ref.at[:, cols(sib_up)], y_ref.at[:, cols(sib_up)], 6, sib).wait_recv()
    remote(y_ref.at[:, cols(sib_far)], y_ref.at[:, cols(sib_far)], 7, sib).wait_recv()
    for copy in first + second + [third]:
        copy.wait_send()


def exp_gather(x, n, collective_id):
    return pl.pallas_call(
        functools.partial(exp_gather_kernel, n),
        out_shape=jax.ShapeDtypeStruct((x.shape[0], n * x.shape[1]), x.dtype),
        in_specs=[pl.BlockSpec(memory_space=pltpu.VMEM)],
        out_specs=pl.BlockSpec(memory_space=pltpu.VMEM),
        scratch_shapes=[pltpu.SemaphoreType.DMA((8,)), pltpu.SemaphoreType.DMA((8,))],
        compiler_params=pltpu.CompilerParams(collective_id=collective_id, has_side_effects=True),
    )(x)


def exp_scatter_kernel(n, p_ref, o_ref, sib_buf, acc, stage, half_buf, near_buf, send_sems, recv_sems):
    chips = n // 2
    width = o_ref.shape[1]
    half = o_ref.shape[0] // 2
    me = lax.axis_index("exp")
    z, core = me // 2, me % 2
    sib = 2 * z + 1 - core
    up = 2 * lax.rem(z + 1, chips) + core
    dn = 2 * lax.rem(z + chips - 1, chips) + core
    far = 2 * lax.rem(z + 2, chips) + core

    def cols(block):
        return pl.ds(pl.multiple_of(block * width, width), width)

    def rows(part):
        return pl.ds(part * half, half)

    barrier = pltpu.get_barrier_semaphore()
    for peer in (sib, up, dn):
        pl.semaphore_signal(barrier, inc=1, device_id={"exp": peer}, device_id_type=MESH)
    pl.semaphore_wait(barrier, 3)

    def remote(src, dst, slot, peer):
        return pltpu.make_async_remote_copy(
            src_ref=src, dst_ref=dst, send_sem=send_sems.at[slot],
            recv_sem=recv_sems.at[slot], device_id={"exp": peer}, device_id_type=MESH,
        )

    mine = (me, up, dn, far)
    theirs = tuple(block + 1 - 2 * core for block in mine)
    sends = []
    for k in range(4):
        copy = remote(p_ref.at[:, cols(theirs[k])], sib_buf.at[k], k, sib)
        copy.start()
        sends.append(copy)
    for k in range(4):
        remote(p_ref.at[:, cols(mine[k])], sib_buf.at[k], k, sib).wait_recv()
        acc[k] = p_ref[:, cols(mine[k])].astype(jnp.float32) + sib_buf[k].astype(jnp.float32)
    stage[0] = acc[3].astype(stage.dtype)
    for part, peer, slot in ((0, up, 4), (1, dn, 5)):
        copy = remote(stage.at[0, rows(part)], half_buf.at[part], slot, peer)
        copy.start()
        sends.append(copy)
    remote(stage.at[0, rows(0)], half_buf.at[0], 4, dn).wait_recv()
    acc[1, rows(0)] = acc[1, rows(0)] + half_buf[0].astype(jnp.float32)
    stage[1] = acc[1].astype(stage.dtype)
    copy = remote(stage.at[1], near_buf.at[0], 6, up)
    copy.start()
    sends.append(copy)
    remote(stage.at[0, rows(1)], half_buf.at[1], 5, up).wait_recv()
    acc[2, rows(1)] = acc[2, rows(1)] + half_buf[1].astype(jnp.float32)
    stage[2] = acc[2].astype(stage.dtype)
    copy = remote(stage.at[2], near_buf.at[1], 7, dn)
    copy.start()
    sends.append(copy)
    remote(stage.at[1], near_buf.at[0], 6, dn).wait_recv()
    remote(stage.at[2], near_buf.at[1], 7, up).wait_recv()
    o_ref[...] = (
        acc[0] + near_buf[0].astype(jnp.float32) + near_buf[1].astype(jnp.float32)
    ).astype(o_ref.dtype)
    for copy in sends:
        copy.wait_send()


def exp_scatter(p, n, collective_id):
    rows_n, width = p.shape[0], p.shape[1] // n
    return pl.pallas_call(
        functools.partial(exp_scatter_kernel, n),
        out_shape=jax.ShapeDtypeStruct((rows_n, width), p.dtype),
        in_specs=[pl.BlockSpec(memory_space=pltpu.VMEM)],
        out_specs=pl.BlockSpec(memory_space=pltpu.VMEM),
        scratch_shapes=[
            pltpu.VMEM((4, rows_n, width), p.dtype),
            pltpu.VMEM((4, rows_n, width), jnp.float32),
            pltpu.VMEM((3, rows_n, width), p.dtype),
            pltpu.VMEM((2, rows_n // 2, width), p.dtype),
            pltpu.VMEM((2, rows_n, width), p.dtype),
            pltpu.SemaphoreType.DMA((8,)),
            pltpu.SemaphoreType.DMA((8,)),
        ],
        compiler_params=pltpu.CompilerParams(collective_id=collective_id, has_side_effects=True),
    )(p)


def pick_rows(source, row_index, live_slot):
    taken_rows = jnp.take(source, row_index, axis=0)
    return jnp.where(live_slot[:, None], taken_rows, jnp.zeros((), source.dtype))


def body(
    attention_out,
    residual,
    w_out,
    router_w,
    norm_gain,
    page_pool,
    page_table,
    cache_len,
    came_from,
    routes,
    w_gate,
    w_up,
    w_down,
):
    groups = lax.axis_size("req")
    own_group = lax.axis_index("req")
    row_req = attention_out.shape[0]
    rows_all = came_from.shape[0]
    pages_req = page_table.shape[1]
    page_len = page_pool.shape[1]
    kv_slice = page_pool.shape[2]
    experts = groups // 2
    targets = jnp.arange(groups, dtype=jnp.int32)
    local_ids = jnp.arange(row_req, dtype=jnp.int32)
    dest_of = (
        jnp.zeros((rows_all,), jnp.int32).at[came_from].set(jnp.arange(rows_all, dtype=jnp.int32))
    )
    dest_group = dest_of // row_req
    dest_hot = (
        (dest_group[:, None] == targets[None, :]).astype(jnp.int32).reshape(groups, row_req, groups)
    )
    pair_rank = jnp.sum((jnp.cumsum(dest_hot, axis=1) - dest_hot) * dest_hot, axis=2).reshape(
        rows_all
    )
    own_dest = lax.dynamic_slice_in_dim(dest_group, own_group * row_req, row_req)
    own_rank = lax.dynamic_slice_in_dim(pair_rank, own_group * row_req, row_req)
    chosen_send = (
        (own_dest[None, None, :] == targets[:, None, None])
        & (own_rank[None, None, :] == jnp.arange(MIG_PAIR, dtype=jnp.int32)[None, :, None])
        & (targets[:, None, None] != own_group)
    )
    send_index = jnp.sum(jnp.where(chosen_send, local_ids[None, None, :], 0), axis=2).reshape(-1)
    send_live = jnp.any(chosen_send, axis=2).reshape(-1)
    page_rows = jnp.take(page_pool, page_table.reshape(-1), axis=0).reshape(
        row_req, pages_req, page_len, kv_slice
    )
    position = (
        jnp.arange(pages_req, dtype=jnp.int32)[:, None] * page_len
        + jnp.arange(page_len, dtype=jnp.int32)[None, :]
    )
    kept_mask = position[None, :, :] < cache_len[:, None, None]
    page_rows = jnp.where(kept_mask[..., None], page_rows, jnp.zeros((), page_rows.dtype)).reshape(
        row_req, -1
    )
    payload = jnp.concatenate([attention_out, page_rows, residual], axis=1)
    moved = exchange(
        pick_rows(payload, send_index, send_live).reshape(groups, MIG_PAIR, -1),
        "req",
        groups,
        False,
        5,
    ).reshape(groups * MIG_PAIR, -1)
    new_source = lax.dynamic_slice_in_dim(came_from, own_group * row_req, row_req)
    source_group = new_source // row_req
    stays_home = source_group == own_group
    arrival = jnp.where(
        stays_home,
        new_source - own_group * row_req,
        row_req + source_group * MIG_PAIR + jnp.take(pair_rank, new_source),
    )
    payload_new = jnp.take(jnp.concatenate([payload, moved], axis=0), arrival, axis=0)
    d_attn, d_page = attention_out.shape[1], page_rows.shape[1]
    attn_new = payload_new[:, :d_attn]
    new_pages = payload_new[:, d_attn:d_attn + d_page].reshape(
        row_req, pages_req, page_len, kv_slice
    )
    resid_new = payload_new[:, d_attn + d_page:]
    projected = jnp.dot(
        attn_new,
        lax.all_gather(w_out, "req", axis=0, tiled=True),
        preferred_element_type=jnp.float32,
    )
    hidden = resid_new.astype(jnp.float32) + projected
    squares = jnp.sum(hidden * hidden, axis=1)
    scaled = hidden * norm_gain[None, :]
    raw_logits = jnp.dot(scaled, router_w, precision=lax.Precision.HIGHEST)
    stats_t = jnp.concatenate([squares[None, :], raw_logits.T], axis=0)
    stats_t = jnp.pad(stats_t, ((0, 16 - stats_t.shape[0]), (0, 0)))
    n_exp = lax.axis_size("exp")
    row_stats = jnp.sum(exchange(stats_t, "exp", n_exp, True, 0), axis=0)[:9].T
    total_sq = row_stats[:, 0]
    inverse = lax.rsqrt(total_sq / D + EPSILON)
    normed = scaled * inverse[:, None]
    logits = row_stats[:, 1:] * inverse[:, None]
    normed_rows = normed.astype(jnp.bfloat16)
    expert_ids = jnp.arange(experts, dtype=jnp.int32)
    chosen = jnp.sum(
        jnp.where(routes[:, :, None] == expert_ids[None, None, :], logits[:, None, :], 0.0), axis=2
    )
    gate_first = jax.nn.sigmoid(chosen[:, 0] - chosen[:, 1])
    gate_second = jax.nn.sigmoid(chosen[:, 1] - chosen[:, 0])
    flat_routes = routes.reshape(-1)
    expert_hot = (flat_routes[:, None] == expert_ids[None, :]).astype(jnp.int32)
    expert_rank = jnp.sum((jnp.cumsum(expert_hot, axis=0) - expert_hot) * expert_hot, axis=1)
    target_dev = flat_routes + experts * (expert_rank % 2)
    slot_index = expert_rank // 2
    assign_ids = jnp.arange(flat_routes.shape[0], dtype=jnp.int32)
    chosen_slot = (target_dev[None, None, :] == targets[:, None, None]) & (
        slot_index[None, None, :] == jnp.arange(CAP, dtype=jnp.int32)[None, :, None]
    )
    slot_source = jnp.sum(
        jnp.where(chosen_slot, assign_ids[None, None, :] // 2, 0), axis=2
    ).reshape(-1)
    slot_live = jnp.any(chosen_slot, axis=2).reshape(-1)
    outgoing = pick_rows(normed_rows, slot_source, slot_live)
    arrived = exchange(
        outgoing.reshape(groups, -1, outgoing.shape[-1]), "req", groups, False, 1
    ).reshape(outgoing.shape)
    rows_full = exp_gather(arrived, lax.axis_size("exp"), 3)
    gate_h = jnp.dot(rows_full, w_gate[0], preferred_element_type=jnp.float32)
    up_h = jnp.dot(rows_full, w_up[0], preferred_element_type=jnp.float32)
    active = (jax.nn.silu(gate_h) * up_h).astype(jnp.bfloat16)
    partial_value = lax.optimization_barrier(
        jnp.dot(active, w_down[0], preferred_element_type=jnp.float32).astype(jnp.bfloat16)
    )
    summed_value = exp_scatter(partial_value, lax.axis_size("exp"), 4)
    lookup = target_dev * CAP + slot_index
    returned = exchange(
        summed_value.reshape(groups, -1, summed_value.shape[-1]), "req", groups, False, 2
    ).reshape(summed_value.shape)
    taken_rows = jnp.take(returned, lookup, axis=0).reshape(row_req, 2, -1).astype(jnp.float32)
    expert_part = gate_first[:, None] * taken_rows[:, 0] + gate_second[:, None] * taken_rows[:, 1]
    mixed = hidden + expert_part
    return (mixed, new_pages)


def solution(mesh):
    in_specs = (
        P("req", None),
        P("req", "exp"),
        P("req", "exp"),
        P("exp", None),
        P("exp"),
        P("req", None, "exp"),
        P("req", None),
        P("req"),
        P(),
        P("req", None),
        P("req", None, "exp"),
        P("req", None, "exp"),
        P("req", "exp", None),
    )
    out_specs = (P("req", "exp"), P("req", None, None, "exp"))
    return jax.shard_map(body, mesh=mesh, in_specs=in_specs, out_specs=out_specs, check_vma=False)
```

```python
import jax
import jax.numpy as jnp
from jax import lax
from jax.experimental import pallas as pl
from jax.experimental.pallas import tpu as pltpu
from jax.sharding import PartitionSpec as P
import functools

D = 4096
CAP = 32
MIG_PAIR = 4


EPSILON = 1e-05

MESH = pl.DeviceIdType.MESH


def exchange_kernel(axis, n, gather, x_ref, y_ref, send_sems, recv_sems):
    me = lax.axis_index(axis)
    barrier = pltpu.get_barrier_semaphore()
    for k in range(1, n):
        pl.semaphore_signal(
            barrier, inc=1, device_id={axis: lax.rem(me + k, n)}, device_id_type=MESH
        )
    pl.semaphore_wait(barrier, n - 1)
    copies = []
    for k in range(1, n):
        peer = lax.rem(me + k, n)
        copy = pltpu.make_async_remote_copy(
            src_ref=x_ref if gather else x_ref.at[peer],
            dst_ref=y_ref.at[me],
            send_sem=send_sems.at[k],
            recv_sem=recv_sems.at[k],
            device_id={axis: peer},
            device_id_type=MESH,
        )
        copy.start()
        copies.append(copy)
    if gather:
        y_ref[me] = x_ref[...]
    else:
        y_ref[me] = x_ref[me]
    for k in range(1, n):
        copies[k - 1].wait_send()
        source = lax.rem(me + n - k, n)
        pltpu.make_async_remote_copy(
            src_ref=x_ref if gather else x_ref.at[source],
            dst_ref=y_ref.at[source],
            send_sem=send_sems.at[k],
            recv_sem=recv_sems.at[k],
            device_id={axis: source},
            device_id_type=MESH,
        ).wait_recv()


def exchange(x, axis, n, gather, collective_id):
    out_shape = (n,) + x.shape if gather else x.shape
    return pl.pallas_call(
        functools.partial(exchange_kernel, axis, n, gather),
        out_shape=jax.ShapeDtypeStruct(out_shape, x.dtype),
        in_specs=[pl.BlockSpec(memory_space=pltpu.VMEM)],
        out_specs=pl.BlockSpec(memory_space=pltpu.VMEM),
        scratch_shapes=[pltpu.SemaphoreType.DMA((n,)), pltpu.SemaphoreType.DMA((n,))],
        compiler_params=pltpu.CompilerParams(collective_id=collective_id, has_side_effects=True),
    )(x)


def exp_gather_kernel(n, x_ref, y_ref, send_sems, recv_sems):
    chips = n // 2
    width = x_ref.shape[1]
    half = x_ref.shape[0] // 2
    me = lax.axis_index("exp")
    z, core = me // 2, me % 2
    sib = 2 * z + 1 - core
    up = 2 * lax.rem(z + 1, chips) + core
    dn = 2 * lax.rem(z + chips - 1, chips) + core
    far = 2 * lax.rem(z + 2, chips) + core

    def cols(block):
        return pl.ds(pl.multiple_of(block * width, width), width)

    def rows(part):
        return pl.ds(part * half, half)

    barrier = pltpu.get_barrier_semaphore()
    for peer in (sib, up, dn):
        pl.semaphore_signal(barrier, inc=1, device_id={"exp": peer}, device_id_type=MESH)
    pl.semaphore_wait(barrier, 3)

    def remote(src, dst, slot, peer):
        return pltpu.make_async_remote_copy(
            src_ref=src, dst_ref=dst, send_sem=send_sems.at[slot],
            recv_sem=recv_sems.at[slot], device_id={"exp": peer}, device_id_type=MESH,
        )

    own_cols = cols(me)
    first = [
        remote(x_ref, y_ref.at[:, own_cols], 0, up),
        remote(x_ref, y_ref.at[:, own_cols], 1, dn),
        remote(x_ref, y_ref.at[:, own_cols], 2, sib),
    ]
    for copy in first:
        copy.start()
    y_ref[:, own_cols] = x_ref[...]
    remote(x_ref, y_ref.at[:, cols(dn)], 0, dn).wait_recv()
    remote(x_ref, y_ref.at[:, cols(up)], 1, up).wait_recv()
    second = [
        remote(y_ref.at[rows(1), cols(dn)], y_ref.at[rows(1), cols(dn)], 3, up),
        remote(y_ref.at[rows(0), cols(up)], y_ref.at[rows(0), cols(up)], 4, dn),
        remote(y_ref.at[:, cols(dn)], y_ref.at[:, cols(dn)], 5, sib),
        remote(y_ref.at[:, cols(up)], y_ref.at[:, cols(up)], 6, sib),
    ]
    for copy in second:
        copy.start()
    remote(y_ref.at[rows(1), cols(far)], y_ref.at[rows(1), cols(far)], 3, dn).wait_recv()
    remote(y_ref.at[rows(0), cols(far)], y_ref.at[rows(0), cols(far)], 4, up).wait_recv()
    third = remote(y_ref.at[:, cols(far)], y_ref.at[:, cols(far)], 7, sib)
    third.start()
    sib_z = 2 * z + 1 - core
    sib_up = 2 * lax.rem(z + 1, chips) + 1 - core
    sib_dn = 2 * lax.rem(z + chips - 1, chips) + 1 - core
    sib_far = 2 * lax.rem(z + 2, chips) + 1 - core
    remote(x_ref, y_ref.at[:, cols(sib_z)], 2, sib).wait_recv()
    remote(y_ref.at[:, cols(sib_dn)], y_ref.at[:, cols(sib_dn)], 5, sib).wait_recv()
    remote(y_ref.at[:, cols(sib_up)], y_ref.at[:, cols(sib_up)], 6, sib).wait_recv()
    remote(y_ref.at[:, cols(sib_far)], y_ref.at[:, cols(sib_far)], 7, sib).wait_recv()
    for copy in first + second + [third]:
        copy.wait_send()


def exp_gather(x, n, collective_id):
    return pl.pallas_call(
        functools.partial(exp_gather_kernel, n),
        out_shape=jax.ShapeDtypeStruct((x.shape[0], n * x.shape[1]), x.dtype),
        in_specs=[pl.BlockSpec(memory_space=pltpu.VMEM)],
        out_specs=pl.BlockSpec(memory_space=pltpu.VMEM),
        scratch_shapes=[pltpu.SemaphoreType.DMA((8,)), pltpu.SemaphoreType.DMA((8,))],
        compiler_params=pltpu.CompilerParams(collective_id=collective_id, has_side_effects=True),
    )(x)


def ffn_kernel(x_ref, wg_ref, wu_ref, wd_ref, o_ref, g_acc, u_acc):
    step = pl.program_id(0)

    @pl.when(step == 0)
    def _():
        g_acc[...] = jnp.zeros_like(g_acc)
        u_acc[...] = jnp.zeros_like(u_acc)

    x = x_ref[...]
    g_acc[...] += jnp.dot(x, wg_ref[...], preferred_element_type=jnp.float32)
    u_acc[...] += jnp.dot(x, wu_ref[...], preferred_element_type=jnp.float32)

    @pl.when(step == pl.num_programs(0) - 1)
    def _():
        g = g_acc[...]
        act = (g / (1.0 + jnp.exp(-g)) * u_acc[...]).astype(wd_ref.dtype)
        o_ref[...] = jnp.dot(act, wd_ref[...], preferred_element_type=jnp.float32).astype(
            o_ref.dtype
        )


def expert_ffn(x, wg, wu, wd, tk=512):
    rows_n, d = x.shape
    ff = wg.shape[1]
    return pl.pallas_call(
        ffn_kernel,
        out_shape=jax.ShapeDtypeStruct((rows_n, wd.shape[1]), x.dtype),
        grid=(d // tk,),
        in_specs=[
            pl.BlockSpec((rows_n, tk), lambda k: (0, k)),
            pl.BlockSpec((tk, ff), lambda k: (k, 0)),
            pl.BlockSpec((tk, ff), lambda k: (k, 0)),
            pl.BlockSpec((ff, wd.shape[1]), lambda k: (0, 0)),
        ],
        out_specs=pl.BlockSpec((rows_n, wd.shape[1]), lambda k: (0, 0)),
        scratch_shapes=[
            pltpu.VMEM((rows_n, ff), jnp.float32),
            pltpu.VMEM((rows_n, ff), jnp.float32),
        ],
        compiler_params=pltpu.CompilerParams(
            dimension_semantics=("arbitrary",), vmem_limit_bytes=56 * 1024 * 1024
        ),
        cost_estimate=pl.CostEstimate(
            flops=2 * rows_n * d * ff * 2 + 2 * rows_n * ff * wd.shape[1],
            transcendentals=rows_n * ff,
            bytes_accessed=2 * (rows_n * d + 2 * d * ff + ff * wd.shape[1] + rows_n * wd.shape[1]),
        ),
    )(x, wg, wu, wd)


def pick_rows(source, row_index, live_slot):
    taken_rows = jnp.take(source, row_index, axis=0)
    return jnp.where(live_slot[:, None], taken_rows, jnp.zeros((), source.dtype))


def body(
    attention_out,
    residual,
    w_out,
    router_w,
    norm_gain,
    page_pool,
    page_table,
    cache_len,
    came_from,
    routes,
    w_gate,
    w_up,
    w_down,
):
    groups = lax.axis_size("req")
    own_group = lax.axis_index("req")
    row_req = attention_out.shape[0]
    rows_all = came_from.shape[0]
    pages_req = page_table.shape[1]
    page_len = page_pool.shape[1]
    kv_slice = page_pool.shape[2]
    experts = groups // 2
    targets = jnp.arange(groups, dtype=jnp.int32)
    local_ids = jnp.arange(row_req, dtype=jnp.int32)
    dest_of = (
        jnp.zeros((rows_all,), jnp.int32).at[came_from].set(jnp.arange(rows_all, dtype=jnp.int32))
    )
    dest_group = dest_of // row_req
    dest_hot = (
        (dest_group[:, None] == targets[None, :]).astype(jnp.int32).reshape(groups, row_req, groups)
    )
    pair_rank = jnp.sum((jnp.cumsum(dest_hot, axis=1) - dest_hot) * dest_hot, axis=2).reshape(
        rows_all
    )
    own_dest = lax.dynamic_slice_in_dim(dest_group, own_group * row_req, row_req)
    own_rank = lax.dynamic_slice_in_dim(pair_rank, own_group * row_req, row_req)
    chosen_send = (
        (own_dest[None, None, :] == targets[:, None, None])
        & (own_rank[None, None, :] == jnp.arange(MIG_PAIR, dtype=jnp.int32)[None, :, None])
        & (targets[:, None, None] != own_group)
    )
    send_index = jnp.sum(jnp.where(chosen_send, local_ids[None, None, :], 0), axis=2).reshape(-1)
    send_live = jnp.any(chosen_send, axis=2).reshape(-1)
    moved_attn, moved_resid = (
        lax.all_to_all(
            pick_rows(attention_out, send_index, send_live),
            "req",
            split_axis=0,
            concat_axis=0,
            tiled=True,
        ),
        lax.all_to_all(
            pick_rows(residual, send_index, send_live),
            "req",
            split_axis=0,
            concat_axis=0,
            tiled=True,
        ),
    )
    new_source = lax.dynamic_slice_in_dim(came_from, own_group * row_req, row_req)
    source_group = new_source // row_req
    stays_home = source_group == own_group
    arrival = jnp.where(
        stays_home,
        new_source - own_group * row_req,
        row_req + source_group * MIG_PAIR + jnp.take(pair_rank, new_source),
    )
    attn_new = jnp.take(jnp.concatenate([attention_out, moved_attn], axis=0), arrival, axis=0)
    resid_new = jnp.take(jnp.concatenate([residual, moved_resid], axis=0), arrival, axis=0)
    projected = jnp.dot(
        attn_new,
        lax.all_gather(w_out, "req", axis=0, tiled=True),
        preferred_element_type=jnp.float32,
    )
    hidden = resid_new.astype(jnp.float32) + projected
    squares = jnp.sum(hidden * hidden, axis=1)
    scaled = hidden * norm_gain[None, :]
    raw_logits = jnp.dot(scaled, router_w, precision=lax.Precision.HIGHEST)
    stats_t = jnp.concatenate([squares[None, :], raw_logits.T], axis=0)
    stats_t = jnp.pad(stats_t, ((0, 16 - stats_t.shape[0]), (0, 0)))
    n_exp = lax.axis_size("exp")
    row_stats = jnp.sum(exchange(stats_t, "exp", n_exp, True, 0), axis=0)[:9].T
    total_sq = row_stats[:, 0]
    inverse = lax.rsqrt(total_sq / D + EPSILON)
    normed = scaled * inverse[:, None]
    logits = row_stats[:, 1:] * inverse[:, None]
    normed_rows = normed.astype(jnp.bfloat16)
    expert_ids = jnp.arange(experts, dtype=jnp.int32)
    chosen = jnp.sum(
        jnp.where(routes[:, :, None] == expert_ids[None, None, :], logits[:, None, :], 0.0), axis=2
    )
    gate_first = jax.nn.sigmoid(chosen[:, 0] - chosen[:, 1])
    gate_second = jax.nn.sigmoid(chosen[:, 1] - chosen[:, 0])
    flat_routes = routes.reshape(-1)
    expert_hot = (flat_routes[:, None] == expert_ids[None, :]).astype(jnp.int32)
    expert_rank = jnp.sum((jnp.cumsum(expert_hot, axis=0) - expert_hot) * expert_hot, axis=1)
    target_dev = flat_routes + experts * (expert_rank % 2)
    slot_index = expert_rank // 2
    assign_ids = jnp.arange(flat_routes.shape[0], dtype=jnp.int32)
    chosen_slot = (target_dev[None, None, :] == targets[:, None, None]) & (
        slot_index[None, None, :] == jnp.arange(CAP, dtype=jnp.int32)[None, :, None]
    )
    slot_source = jnp.sum(
        jnp.where(chosen_slot, assign_ids[None, None, :] // 2, 0), axis=2
    ).reshape(-1)
    slot_live = jnp.any(chosen_slot, axis=2).reshape(-1)
    outgoing = pick_rows(normed_rows, slot_source, slot_live)
    arrived = exchange(
        outgoing.reshape(groups, -1, outgoing.shape[-1]), "req", groups, False, 1
    ).reshape(outgoing.shape)
    rows_full = exp_gather(arrived, lax.axis_size("exp"), 3)
    partial_value = expert_ffn(rows_full, w_gate[0], w_up[0], w_down[0])
    partial_value, page_pool = lax.optimization_barrier((partial_value, page_pool))
    summed_value = lax.psum_scatter(partial_value, "exp", scatter_dimension=1, tiled=True)
    page_rows = jnp.take(page_pool, page_table.reshape(-1), axis=0).reshape(
        row_req, pages_req, page_len, kv_slice
    )
    position = (
        jnp.arange(pages_req, dtype=jnp.int32)[:, None] * page_len
        + jnp.arange(page_len, dtype=jnp.int32)[None, :]
    )
    kept_mask = position[None, :, :] < cache_len[:, None, None]
    page_rows = jnp.where(kept_mask[..., None], page_rows, jnp.zeros((), page_rows.dtype)).reshape(
        row_req, -1
    )
    moved_pages = lax.all_to_all(
        pick_rows(page_rows, send_index, send_live), "req", split_axis=0, concat_axis=0, tiled=True
    )
    new_pages = jnp.take(
        jnp.concatenate([page_rows, moved_pages], axis=0), arrival, axis=0
    ).reshape(row_req, pages_req, page_len, kv_slice)
    lookup = target_dev * CAP + slot_index
    returned = exchange(
        summed_value.reshape(groups, -1, summed_value.shape[-1]), "req", groups, False, 2
    ).reshape(summed_value.shape)
    taken_rows = jnp.take(returned, lookup, axis=0).reshape(row_req, 2, -1).astype(jnp.float32)
    expert_part = gate_first[:, None] * taken_rows[:, 0] + gate_second[:, None] * taken_rows[:, 1]
    mixed = hidden + expert_part
    return (mixed, new_pages)


def solution(mesh):
    in_specs = (
        P("req", None),
        P("req", "exp"),
        P("req", "exp"),
        P("exp", None),
        P("exp"),
        P("req", None, "exp"),
        P("req", None),
        P("req"),
        P(),
        P("req", None),
        P("req", None, "exp"),
        P("req", None, "exp"),
        P("req", "exp", None),
    )
    out_specs = (P("req", "exp"), P("req", None, None, "exp"))
    return jax.shard_map(body, mesh=mesh, in_specs=in_specs, out_specs=out_specs, check_vma=False)
```

```python
import jax
import jax.numpy as jnp
from jax import lax
from jax.experimental import pallas as pl
from jax.experimental.pallas import tpu as pltpu
from jax.sharding import PartitionSpec as P
import functools

D = 4096
CAP = 32
MIG_PAIR = 4


EPSILON = 1e-05

MESH = pl.DeviceIdType.MESH


def exchange_kernel(axis, n, gather, x_ref, y_ref, send_sems, recv_sems):
    me = lax.axis_index(axis)
    barrier = pltpu.get_barrier_semaphore()
    for k in range(1, n):
        pl.semaphore_signal(
            barrier, inc=1, device_id={axis: lax.rem(me + k, n)}, device_id_type=MESH
        )
    pl.semaphore_wait(barrier, n - 1)
    copies = []
    for k in range(1, n):
        peer = lax.rem(me + k, n)
        copy = pltpu.make_async_remote_copy(
            src_ref=x_ref if gather else x_ref.at[peer],
            dst_ref=y_ref.at[me],
            send_sem=send_sems.at[k],
            recv_sem=recv_sems.at[k],
            device_id={axis: peer},
            device_id_type=MESH,
        )
        copy.start()
        copies.append(copy)
    if gather:
        y_ref[me] = x_ref[...]
    else:
        y_ref[me] = x_ref[me]
    for k in range(1, n):
        copies[k - 1].wait_send()
        source = lax.rem(me + n - k, n)
        pltpu.make_async_remote_copy(
            src_ref=x_ref if gather else x_ref.at[source],
            dst_ref=y_ref.at[source],
            send_sem=send_sems.at[k],
            recv_sem=recv_sems.at[k],
            device_id={axis: source},
            device_id_type=MESH,
        ).wait_recv()


def exchange(x, axis, n, gather, collective_id):
    out_shape = (n,) + x.shape if gather else x.shape
    return pl.pallas_call(
        functools.partial(exchange_kernel, axis, n, gather),
        out_shape=jax.ShapeDtypeStruct(out_shape, x.dtype),
        in_specs=[pl.BlockSpec(memory_space=pltpu.VMEM)],
        out_specs=pl.BlockSpec(memory_space=pltpu.VMEM),
        scratch_shapes=[pltpu.SemaphoreType.DMA((n,)), pltpu.SemaphoreType.DMA((n,))],
        compiler_params=pltpu.CompilerParams(collective_id=collective_id, has_side_effects=True),
    )(x)


def exp_gather_kernel(n, x_ref, y_ref, send_sems, recv_sems):
    chips = n // 2
    width = x_ref.shape[1]
    half = x_ref.shape[0] // 2
    me = lax.axis_index("exp")
    z, core = me // 2, me % 2
    sib = 2 * z + 1 - core
    up = 2 * lax.rem(z + 1, chips) + core
    dn = 2 * lax.rem(z + chips - 1, chips) + core
    far = 2 * lax.rem(z + 2, chips) + core

    def cols(block):
        return pl.ds(pl.multiple_of(block * width, width), width)

    def rows(part):
        return pl.ds(part * half, half)

    barrier = pltpu.get_barrier_semaphore()
    for peer in (sib, up, dn):
        pl.semaphore_signal(barrier, inc=1, device_id={"exp": peer}, device_id_type=MESH)
    pl.semaphore_wait(barrier, 3)

    def remote(src, dst, slot, peer):
        return pltpu.make_async_remote_copy(
            src_ref=src, dst_ref=dst, send_sem=send_sems.at[slot],
            recv_sem=recv_sems.at[slot], device_id={"exp": peer}, device_id_type=MESH,
        )

    own_cols = cols(me)
    first = [
        remote(x_ref, y_ref.at[:, own_cols], 0, up),
        remote(x_ref, y_ref.at[:, own_cols], 1, dn),
        remote(x_ref, y_ref.at[:, own_cols], 2, sib),
    ]
    for copy in first:
        copy.start()
    y_ref[:, own_cols] = x_ref[...]
    remote(x_ref, y_ref.at[:, cols(dn)], 0, dn).wait_recv()
    remote(x_ref, y_ref.at[:, cols(up)], 1, up).wait_recv()
    second = [
        remote(y_ref.at[rows(1), cols(dn)], y_ref.at[rows(1), cols(dn)], 3, up),
        remote(y_ref.at[rows(0), cols(up)], y_ref.at[rows(0), cols(up)], 4, dn),
        remote(y_ref.at[:, cols(dn)], y_ref.at[:, cols(dn)], 5, sib),
        remote(y_ref.at[:, cols(up)], y_ref.at[:, cols(up)], 6, sib),
    ]
    for copy in second:
        copy.start()
    remote(y_ref.at[rows(1), cols(far)], y_ref.at[rows(1), cols(far)], 3, dn).wait_recv()
    remote(y_ref.at[rows(0), cols(far)], y_ref.at[rows(0), cols(far)], 4, up).wait_recv()
    third = remote(y_ref.at[:, cols(far)], y_ref.at[:, cols(far)], 7, sib)
    third.start()
    sib_z = 2 * z + 1 - core
    sib_up = 2 * lax.rem(z + 1, chips) + 1 - core
    sib_dn = 2 * lax.rem(z + chips - 1, chips) + 1 - core
    sib_far = 2 * lax.rem(z + 2, chips) + 1 - core
    remote(x_ref, y_ref.at[:, cols(sib_z)], 2, sib).wait_recv()
    remote(y_ref.at[:, cols(sib_dn)], y_ref.at[:, cols(sib_dn)], 5, sib).wait_recv()
    remote(y_ref.at[:, cols(sib_up)], y_ref.at[:, cols(sib_up)], 6, sib).wait_recv()
    remote(y_ref.at[:, cols(sib_far)], y_ref.at[:, cols(sib_far)], 7, sib).wait_recv()
    for copy in first + second + [third]:
        copy.wait_send()


def exp_gather(x, n, collective_id):
    return pl.pallas_call(
        functools.partial(exp_gather_kernel, n),
        out_shape=jax.ShapeDtypeStruct((x.shape[0], n * x.shape[1]), x.dtype),
        in_specs=[pl.BlockSpec(memory_space=pltpu.VMEM)],
        out_specs=pl.BlockSpec(memory_space=pltpu.VMEM),
        scratch_shapes=[pltpu.SemaphoreType.DMA((8,)), pltpu.SemaphoreType.DMA((8,))],
        compiler_params=pltpu.CompilerParams(collective_id=collective_id, has_side_effects=True),
    )(x)


def ffn_kernel(x_ref, wg_ref, wu_ref, wd_ref, o_ref, g_acc, u_acc):
    step = pl.program_id(0)

    @pl.when(step == 0)
    def _():
        g_acc[...] = jnp.zeros_like(g_acc)
        u_acc[...] = jnp.zeros_like(u_acc)

    x = x_ref[...]
    g_acc[...] += jnp.dot(x, wg_ref[...], preferred_element_type=jnp.float32)
    u_acc[...] += jnp.dot(x, wu_ref[...], preferred_element_type=jnp.float32)

    @pl.when(step == pl.num_programs(0) - 1)
    def _():
        g = g_acc[...]
        act = (g / (1.0 + jnp.exp(-g)) * u_acc[...]).astype(wd_ref.dtype)
        o_ref[...] = jnp.dot(act, wd_ref[...], preferred_element_type=jnp.float32).astype(
            o_ref.dtype
        )


def expert_ffn(x, wg, wu, wd, tk=512):
    rows_n, d = x.shape
    ff = wg.shape[1]
    return pl.pallas_call(
        ffn_kernel,
        out_shape=jax.ShapeDtypeStruct((rows_n, wd.shape[1]), x.dtype),
        grid=(d // tk,),
        in_specs=[
            pl.BlockSpec((rows_n, tk), lambda k: (0, k)),
            pl.BlockSpec((tk, ff), lambda k: (k, 0)),
            pl.BlockSpec((tk, ff), lambda k: (k, 0)),
            pl.BlockSpec((ff, wd.shape[1]), lambda k: (0, 0)),
        ],
        out_specs=pl.BlockSpec((rows_n, wd.shape[1]), lambda k: (0, 0)),
        scratch_shapes=[
            pltpu.VMEM((rows_n, ff), jnp.float32),
            pltpu.VMEM((rows_n, ff), jnp.float32),
        ],
        compiler_params=pltpu.CompilerParams(
            dimension_semantics=("arbitrary",), vmem_limit_bytes=56 * 1024 * 1024
        ),
        cost_estimate=pl.CostEstimate(
            flops=2 * rows_n * d * ff * 2 + 2 * rows_n * ff * wd.shape[1],
            transcendentals=rows_n * ff,
            bytes_accessed=2 * (rows_n * d + 2 * d * ff + ff * wd.shape[1] + rows_n * wd.shape[1]),
        ),
    )(x, wg, wu, wd)


def gather_ffn_kernel(
    n, x_ref, wg_hbm, wu_hbm, wd_hbm, o_ref,
    y_ref, wg_v, wu_v, wd_v, g_acc, u_acc, send_sems, recv_sems, w_sems,
):
    chips = n // 2
    width = x_ref.shape[1]
    half = x_ref.shape[0] // 2
    me = lax.axis_index("exp")
    z, core = me // 2, me % 2
    sib = 2 * z + 1 - core
    up = 2 * lax.rem(z + 1, chips) + core
    dn = 2 * lax.rem(z + chips - 1, chips) + core
    far = 2 * lax.rem(z + 2, chips) + core

    weight_copies = [
        pltpu.make_async_copy(src.at[0], dst, w_sems.at[i])
        for i, (src, dst) in enumerate(((wg_hbm, wg_v), (wu_hbm, wu_v), (wd_hbm, wd_v)))
    ]
    for copy in weight_copies:
        copy.start()

    def cols(block):
        return pl.ds(pl.multiple_of(block * width, width), width)

    def rows(part):
        return pl.ds(part * half, half)

    barrier = pltpu.get_barrier_semaphore()
    for peer in (sib, up, dn):
        pl.semaphore_signal(barrier, inc=1, device_id={"exp": peer}, device_id_type=MESH)
    pl.semaphore_wait(barrier, 3)

    def remote(src, dst, slot, peer):
        return pltpu.make_async_remote_copy(
            src_ref=src, dst_ref=dst, send_sem=send_sems.at[slot],
            recv_sem=recv_sems.at[slot], device_id={"exp": peer}, device_id_type=MESH,
        )

    def consume(block, first=False):
        rows_in = x_ref[...] if first else y_ref[:, cols(block)]
        w_rows = pl.ds(pl.multiple_of(block * width, width), width)
        g_part = jnp.dot(rows_in, wg_v[w_rows, :], preferred_element_type=jnp.float32)
        u_part = jnp.dot(rows_in, wu_v[w_rows, :], preferred_element_type=jnp.float32)
        if first:
            g_acc[...] = g_part
            u_acc[...] = u_part
        else:
            g_acc[...] += g_part
            u_acc[...] += u_part

    own_cols = cols(me)
    sends = [
        remote(x_ref, y_ref.at[:, own_cols], 0, up),
        remote(x_ref, y_ref.at[:, own_cols], 1, dn),
        remote(x_ref, y_ref.at[:, own_cols], 2, sib),
    ]
    for copy in sends:
        copy.start()
    weight_copies[0].wait()
    weight_copies[1].wait()
    consume(me, first=True)
    remote(x_ref, y_ref.at[:, cols(dn)], 0, dn).wait_recv()
    remote(x_ref, y_ref.at[:, cols(up)], 1, up).wait_recv()
    second = [
        remote(y_ref.at[rows(1), cols(dn)], y_ref.at[rows(1), cols(dn)], 3, up),
        remote(y_ref.at[rows(0), cols(up)], y_ref.at[rows(0), cols(up)], 4, dn),
        remote(y_ref.at[:, cols(dn)], y_ref.at[:, cols(dn)], 5, sib),
        remote(y_ref.at[:, cols(up)], y_ref.at[:, cols(up)], 6, sib),
    ]
    for copy in second:
        copy.start()
    sends += second
    consume(dn)
    consume(up)
    remote(y_ref.at[rows(1), cols(far)], y_ref.at[rows(1), cols(far)], 3, dn).wait_recv()
    remote(y_ref.at[rows(0), cols(far)], y_ref.at[rows(0), cols(far)], 4, up).wait_recv()
    third = remote(y_ref.at[:, cols(far)], y_ref.at[:, cols(far)], 7, sib)
    third.start()
    sends.append(third)
    consume(far)
    sib_up = 2 * lax.rem(z + 1, chips) + 1 - core
    sib_dn = 2 * lax.rem(z + chips - 1, chips) + 1 - core
    sib_far = 2 * lax.rem(z + 2, chips) + 1 - core
    for block, slot in ((sib, 2), (sib_dn, 5), (sib_up, 6), (sib_far, 7)):
        remote(y_ref.at[:, cols(block)], y_ref.at[:, cols(block)], slot, sib).wait_recv()
        consume(block)
    g = g_acc[...]
    act = (g / (1.0 + jnp.exp(-g)) * u_acc[...]).astype(wd_v.dtype)
    weight_copies[2].wait()
    out_cols = o_ref.shape[1]
    chunk = out_cols // 8
    for c in range(8):
        span = pl.ds(c * chunk, chunk)
        o_ref[:, span] = jnp.dot(act, wd_v[:, span], preferred_element_type=jnp.float32).astype(
            o_ref.dtype
        )
    for copy in sends:
        copy.wait_send()


def gather_ffn(x, w_gate, w_up, w_down, n, collective_id):
    rows_n, width = x.shape
    d, ff = w_gate.shape[1], w_gate.shape[2]
    return pl.pallas_call(
        functools.partial(gather_ffn_kernel, n),
        out_shape=jax.ShapeDtypeStruct((rows_n, w_down.shape[2]), x.dtype),
        in_specs=[pl.BlockSpec(memory_space=pltpu.VMEM)] + [pl.BlockSpec(memory_space=pl.ANY)] * 3,
        out_specs=pl.BlockSpec(memory_space=pltpu.VMEM),
        scratch_shapes=[
            pltpu.VMEM((rows_n, n * width), x.dtype),
            pltpu.VMEM((d, ff), w_gate.dtype),
            pltpu.VMEM((d, ff), w_up.dtype),
            pltpu.VMEM((ff, w_down.shape[2]), w_down.dtype),
            pltpu.VMEM((rows_n, ff), jnp.float32),
            pltpu.VMEM((rows_n, ff), jnp.float32),
            pltpu.SemaphoreType.DMA((8,)),
            pltpu.SemaphoreType.DMA((8,)),
            pltpu.SemaphoreType.DMA((3,)),
        ],
        compiler_params=pltpu.CompilerParams(
            collective_id=collective_id, has_side_effects=True, vmem_limit_bytes=60 * 1024 * 1024
        ),
    )(x, w_gate, w_up, w_down)


def pick_rows(source, row_index, live_slot):
    taken_rows = jnp.take(source, row_index, axis=0)
    return jnp.where(live_slot[:, None], taken_rows, jnp.zeros((), source.dtype))


def body(
    attention_out,
    residual,
    w_out,
    router_w,
    norm_gain,
    page_pool,
    page_table,
    cache_len,
    came_from,
    routes,
    w_gate,
    w_up,
    w_down,
):
    groups = lax.axis_size("req")
    own_group = lax.axis_index("req")
    row_req = attention_out.shape[0]
    rows_all = came_from.shape[0]
    pages_req = page_table.shape[1]
    page_len = page_pool.shape[1]
    kv_slice = page_pool.shape[2]
    experts = groups // 2
    targets = jnp.arange(groups, dtype=jnp.int32)
    local_ids = jnp.arange(row_req, dtype=jnp.int32)
    dest_of = (
        jnp.zeros((rows_all,), jnp.int32).at[came_from].set(jnp.arange(rows_all, dtype=jnp.int32))
    )
    dest_group = dest_of // row_req
    dest_hot = (
        (dest_group[:, None] == targets[None, :]).astype(jnp.int32).reshape(groups, row_req, groups)
    )
    pair_rank = jnp.sum((jnp.cumsum(dest_hot, axis=1) - dest_hot) * dest_hot, axis=2).reshape(
        rows_all
    )
    own_dest = lax.dynamic_slice_in_dim(dest_group, own_group * row_req, row_req)
    own_rank = lax.dynamic_slice_in_dim(pair_rank, own_group * row_req, row_req)
    chosen_send = (
        (own_dest[None, None, :] == targets[:, None, None])
        & (own_rank[None, None, :] == jnp.arange(MIG_PAIR, dtype=jnp.int32)[None, :, None])
        & (targets[:, None, None] != own_group)
    )
    send_index = jnp.sum(jnp.where(chosen_send, local_ids[None, None, :], 0), axis=2).reshape(-1)
    send_live = jnp.any(chosen_send, axis=2).reshape(-1)
    moved_attn, moved_resid = (
        lax.all_to_all(
            pick_rows(attention_out, send_index, send_live),
            "req",
            split_axis=0,
            concat_axis=0,
            tiled=True,
        ),
        lax.all_to_all(
            pick_rows(residual, send_index, send_live),
            "req",
            split_axis=0,
            concat_axis=0,
            tiled=True,
        ),
    )
    new_source = lax.dynamic_slice_in_dim(came_from, own_group * row_req, row_req)
    source_group = new_source // row_req
    stays_home = source_group == own_group
    arrival = jnp.where(
        stays_home,
        new_source - own_group * row_req,
        row_req + source_group * MIG_PAIR + jnp.take(pair_rank, new_source),
    )
    attn_new = jnp.take(jnp.concatenate([attention_out, moved_attn], axis=0), arrival, axis=0)
    resid_new = jnp.take(jnp.concatenate([residual, moved_resid], axis=0), arrival, axis=0)
    projected = jnp.dot(
        attn_new,
        lax.all_gather(w_out, "req", axis=0, tiled=True),
        preferred_element_type=jnp.float32,
    )
    hidden = resid_new.astype(jnp.float32) + projected
    squares = jnp.sum(hidden * hidden, axis=1)
    scaled = hidden * norm_gain[None, :]
    raw_logits = jnp.dot(scaled, router_w, precision=lax.Precision.HIGHEST)
    stats_t = jnp.concatenate([squares[None, :], raw_logits.T], axis=0)
    stats_t = jnp.pad(stats_t, ((0, 16 - stats_t.shape[0]), (0, 0)))
    n_exp = lax.axis_size("exp")
    row_stats = jnp.sum(exchange(stats_t, "exp", n_exp, True, 0), axis=0)[:9].T
    total_sq = row_stats[:, 0]
    inverse = lax.rsqrt(total_sq / D + EPSILON)
    normed = scaled * inverse[:, None]
    logits = row_stats[:, 1:] * inverse[:, None]
    normed_rows = normed.astype(jnp.bfloat16)
    expert_ids = jnp.arange(experts, dtype=jnp.int32)
    chosen = jnp.sum(
        jnp.where(routes[:, :, None] == expert_ids[None, None, :], logits[:, None, :], 0.0), axis=2
    )
    gate_first = jax.nn.sigmoid(chosen[:, 0] - chosen[:, 1])
    gate_second = jax.nn.sigmoid(chosen[:, 1] - chosen[:, 0])
    flat_routes = routes.reshape(-1)
    expert_hot = (flat_routes[:, None] == expert_ids[None, :]).astype(jnp.int32)
    expert_rank = jnp.sum((jnp.cumsum(expert_hot, axis=0) - expert_hot) * expert_hot, axis=1)
    target_dev = flat_routes + experts * (expert_rank % 2)
    slot_index = expert_rank // 2
    assign_ids = jnp.arange(flat_routes.shape[0], dtype=jnp.int32)
    chosen_slot = (target_dev[None, None, :] == targets[:, None, None]) & (
        slot_index[None, None, :] == jnp.arange(CAP, dtype=jnp.int32)[None, :, None]
    )
    slot_source = jnp.sum(
        jnp.where(chosen_slot, assign_ids[None, None, :] // 2, 0), axis=2
    ).reshape(-1)
    slot_live = jnp.any(chosen_slot, axis=2).reshape(-1)
    outgoing = pick_rows(normed_rows, slot_source, slot_live)
    arrived = exchange(
        outgoing.reshape(groups, -1, outgoing.shape[-1]), "req", groups, False, 1
    ).reshape(outgoing.shape)
    partial_value = gather_ffn(arrived, w_gate, w_up, w_down, lax.axis_size("exp"), 3)
    partial_value, page_pool = lax.optimization_barrier((partial_value, page_pool))
    summed_value = lax.psum_scatter(partial_value, "exp", scatter_dimension=1, tiled=True)
    page_rows = jnp.take(page_pool, page_table.reshape(-1), axis=0).reshape(
        row_req, pages_req, page_len, kv_slice
    )
    position = (
        jnp.arange(pages_req, dtype=jnp.int32)[:, None] * page_len
        + jnp.arange(page_len, dtype=jnp.int32)[None, :]
    )
    kept_mask = position[None, :, :] < cache_len[:, None, None]
    page_rows = jnp.where(kept_mask[..., None], page_rows, jnp.zeros((), page_rows.dtype)).reshape(
        row_req, -1
    )
    moved_pages = lax.all_to_all(
        pick_rows(page_rows, send_index, send_live), "req", split_axis=0, concat_axis=0, tiled=True
    )
    new_pages = jnp.take(
        jnp.concatenate([page_rows, moved_pages], axis=0), arrival, axis=0
    ).reshape(row_req, pages_req, page_len, kv_slice)
    lookup = target_dev * CAP + slot_index
    returned = exchange(
        summed_value.reshape(groups, -1, summed_value.shape[-1]), "req", groups, False, 2
    ).reshape(summed_value.shape)
    taken_rows = jnp.take(returned, lookup, axis=0).reshape(row_req, 2, -1).astype(jnp.float32)
    expert_part = gate_first[:, None] * taken_rows[:, 0] + gate_second[:, None] * taken_rows[:, 1]
    mixed = hidden + expert_part
    return (mixed, new_pages)


def solution(mesh):
    in_specs = (
        P("req", None),
        P("req", "exp"),
        P("req", "exp"),
        P("exp", None),
        P("exp"),
        P("req", None, "exp"),
        P("req", None),
        P("req"),
        P(),
        P("req", None),
        P("req", None, "exp"),
        P("req", None, "exp"),
        P("req", "exp", None),
    )
    out_specs = (P("req", "exp"), P("req", None, None, "exp"))
    return jax.shard_map(body, mesh=mesh, in_specs=in_specs, out_specs=out_specs, check_vma=False)
```

```python
import jax
import jax.numpy as jnp
from jax import lax
from jax.experimental import pallas as pl
from jax.experimental.pallas import tpu as pltpu
from jax.sharding import PartitionSpec as P
import functools

D = 4096
CAP = 32
MIG_PAIR = 4


EPSILON = 1e-05

MESH = pl.DeviceIdType.MESH


def exchange_kernel(axis, n, gather, x_ref, y_ref, send_sems, recv_sems):
    me = lax.axis_index(axis)
    barrier = pltpu.get_barrier_semaphore()
    for k in range(1, n):
        pl.semaphore_signal(
            barrier, inc=1, device_id={axis: lax.rem(me + k, n)}, device_id_type=MESH
        )
    pl.semaphore_wait(barrier, n - 1)
    copies = []
    for k in range(1, n):
        peer = lax.rem(me + k, n)
        copy = pltpu.make_async_remote_copy(
            src_ref=x_ref if gather else x_ref.at[peer],
            dst_ref=y_ref.at[me],
            send_sem=send_sems.at[k],
            recv_sem=recv_sems.at[k],
            device_id={axis: peer},
            device_id_type=MESH,
        )
        copy.start()
        copies.append(copy)
    if gather:
        y_ref[me] = x_ref[...]
    else:
        y_ref[me] = x_ref[me]
    for k in range(1, n):
        copies[k - 1].wait_send()
        source = lax.rem(me + n - k, n)
        pltpu.make_async_remote_copy(
            src_ref=x_ref if gather else x_ref.at[source],
            dst_ref=y_ref.at[source],
            send_sem=send_sems.at[k],
            recv_sem=recv_sems.at[k],
            device_id={axis: source},
            device_id_type=MESH,
        ).wait_recv()


def exchange(x, axis, n, gather, collective_id):
    out_shape = (n,) + x.shape if gather else x.shape
    return pl.pallas_call(
        functools.partial(exchange_kernel, axis, n, gather),
        out_shape=jax.ShapeDtypeStruct(out_shape, x.dtype),
        in_specs=[pl.BlockSpec(memory_space=pltpu.VMEM)],
        out_specs=pl.BlockSpec(memory_space=pltpu.VMEM),
        scratch_shapes=[pltpu.SemaphoreType.DMA((n,)), pltpu.SemaphoreType.DMA((n,))],
        compiler_params=pltpu.CompilerParams(collective_id=collective_id, has_side_effects=True),
    )(x)


def exp_gather_kernel(n, x_ref, y_ref, send_sems, recv_sems):
    chips = n // 2
    width = x_ref.shape[1]
    half = x_ref.shape[0] // 2
    me = lax.axis_index("exp")
    z, core = me // 2, me % 2
    sib = 2 * z + 1 - core
    up = 2 * lax.rem(z + 1, chips) + core
    dn = 2 * lax.rem(z + chips - 1, chips) + core
    far = 2 * lax.rem(z + 2, chips) + core

    def cols(block):
        return pl.ds(pl.multiple_of(block * width, width), width)

    def rows(part):
        return pl.ds(part * half, half)

    barrier = pltpu.get_barrier_semaphore()
    for peer in (sib, up, dn):
        pl.semaphore_signal(barrier, inc=1, device_id={"exp": peer}, device_id_type=MESH)
    pl.semaphore_wait(barrier, 3)

    def remote(src, dst, slot, peer):
        return pltpu.make_async_remote_copy(
            src_ref=src, dst_ref=dst, send_sem=send_sems.at[slot],
            recv_sem=recv_sems.at[slot], device_id={"exp": peer}, device_id_type=MESH,
        )

    own_cols = cols(me)
    first = [
        remote(x_ref, y_ref.at[:, own_cols], 0, up),
        remote(x_ref, y_ref.at[:, own_cols], 1, dn),
        remote(x_ref, y_ref.at[:, own_cols], 2, sib),
    ]
    for copy in first:
        copy.start()
    y_ref[:, own_cols] = x_ref[...]
    remote(x_ref, y_ref.at[:, cols(dn)], 0, dn).wait_recv()
    remote(x_ref, y_ref.at[:, cols(up)], 1, up).wait_recv()
    second = [
        remote(y_ref.at[rows(1), cols(dn)], y_ref.at[rows(1), cols(dn)], 3, up),
        remote(y_ref.at[rows(0), cols(up)], y_ref.at[rows(0), cols(up)], 4, dn),
        remote(y_ref.at[:, cols(dn)], y_ref.at[:, cols(dn)], 5, sib),
        remote(y_ref.at[:, cols(up)], y_ref.at[:, cols(up)], 6, sib),
    ]
    for copy in second:
        copy.start()
    remote(y_ref.at[rows(1), cols(far)], y_ref.at[rows(1), cols(far)], 3, dn).wait_recv()
    remote(y_ref.at[rows(0), cols(far)], y_ref.at[rows(0), cols(far)], 4, up).wait_recv()
    third = remote(y_ref.at[:, cols(far)], y_ref.at[:, cols(far)], 7, sib)
    third.start()
    sib_z = 2 * z + 1 - core
    sib_up = 2 * lax.rem(z + 1, chips) + 1 - core
    sib_dn = 2 * lax.rem(z + chips - 1, chips) + 1 - core
    sib_far = 2 * lax.rem(z + 2, chips) + 1 - core
    remote(x_ref, y_ref.at[:, cols(sib_z)], 2, sib).wait_recv()
    remote(y_ref.at[:, cols(sib_dn)], y_ref.at[:, cols(sib_dn)], 5, sib).wait_recv()
    remote(y_ref.at[:, cols(sib_up)], y_ref.at[:, cols(sib_up)], 6, sib).wait_recv()
    remote(y_ref.at[:, cols(sib_far)], y_ref.at[:, cols(sib_far)], 7, sib).wait_recv()
    for copy in first + second + [third]:
        copy.wait_send()


def exp_gather(x, n, collective_id):
    return pl.pallas_call(
        functools.partial(exp_gather_kernel, n),
        out_shape=jax.ShapeDtypeStruct((x.shape[0], n * x.shape[1]), x.dtype),
        in_specs=[pl.BlockSpec(memory_space=pltpu.VMEM)],
        out_specs=pl.BlockSpec(memory_space=pltpu.VMEM),
        scratch_shapes=[pltpu.SemaphoreType.DMA((8,)), pltpu.SemaphoreType.DMA((8,))],
        compiler_params=pltpu.CompilerParams(collective_id=collective_id, has_side_effects=True),
    )(x)


def ffn_kernel(x_ref, wg_ref, wu_ref, wd_ref, o_ref, g_acc, u_acc):
    step = pl.program_id(0)

    @pl.when(step == 0)
    def _():
        g_acc[...] = jnp.zeros_like(g_acc)
        u_acc[...] = jnp.zeros_like(u_acc)

    x = x_ref[...]
    g_acc[...] += jnp.dot(x, wg_ref[...], preferred_element_type=jnp.float32)
    u_acc[...] += jnp.dot(x, wu_ref[...], preferred_element_type=jnp.float32)

    @pl.when(step == pl.num_programs(0) - 1)
    def _():
        g = g_acc[...]
        act = (g / (1.0 + jnp.exp(-g)) * u_acc[...]).astype(wd_ref.dtype)
        o_ref[...] = jnp.dot(act, wd_ref[...], preferred_element_type=jnp.float32).astype(
            o_ref.dtype
        )


def expert_ffn(x, wg, wu, wd, tk=512):
    rows_n, d = x.shape
    ff = wg.shape[1]
    return pl.pallas_call(
        ffn_kernel,
        out_shape=jax.ShapeDtypeStruct((rows_n, wd.shape[1]), x.dtype),
        grid=(d // tk,),
        in_specs=[
            pl.BlockSpec((rows_n, tk), lambda k: (0, k)),
            pl.BlockSpec((tk, ff), lambda k: (k, 0)),
            pl.BlockSpec((tk, ff), lambda k: (k, 0)),
            pl.BlockSpec((ff, wd.shape[1]), lambda k: (0, 0)),
        ],
        out_specs=pl.BlockSpec((rows_n, wd.shape[1]), lambda k: (0, 0)),
        scratch_shapes=[
            pltpu.VMEM((rows_n, ff), jnp.float32),
            pltpu.VMEM((rows_n, ff), jnp.float32),
        ],
        compiler_params=pltpu.CompilerParams(
            dimension_semantics=("arbitrary",), vmem_limit_bytes=56 * 1024 * 1024
        ),
        cost_estimate=pl.CostEstimate(
            flops=2 * rows_n * d * ff * 2 + 2 * rows_n * ff * wd.shape[1],
            transcendentals=rows_n * ff,
            bytes_accessed=2 * (rows_n * d + 2 * d * ff + ff * wd.shape[1] + rows_n * wd.shape[1]),
        ),
    )(x, wg, wu, wd)


def gather_ffn_kernel(
    n, x_ref, wg_hbm, wu_hbm, wd_hbm, o_ref,
    y_ref, wg_v, wu_v, wd_v, g_acc, u_acc, send_sems, recv_sems, w_sems,
    sib_out, sib_buf, acc, stage, half_buf, near_buf, rs_send, rs_recv,
):
    chips = n // 2
    width = x_ref.shape[1]
    half = x_ref.shape[0] // 2
    me = lax.axis_index("exp")
    z, core = me // 2, me % 2
    sib = 2 * z + 1 - core
    up = 2 * lax.rem(z + 1, chips) + core
    dn = 2 * lax.rem(z + chips - 1, chips) + core
    far = 2 * lax.rem(z + 2, chips) + core

    weight_copies = [
        pltpu.make_async_copy(src.at[0], dst, w_sems.at[i])
        for i, (src, dst) in enumerate(((wg_hbm, wg_v), (wu_hbm, wu_v), (wd_hbm, wd_v)))
    ]
    for copy in weight_copies:
        copy.start()

    def cols(block):
        return pl.ds(pl.multiple_of(block * width, width), width)

    def rows(part):
        return pl.ds(part * half, half)

    barrier = pltpu.get_barrier_semaphore()
    for peer in (sib, up, dn):
        pl.semaphore_signal(barrier, inc=1, device_id={"exp": peer}, device_id_type=MESH)
    pl.semaphore_wait(barrier, 3)

    def remote(src, dst, slot, peer):
        return pltpu.make_async_remote_copy(
            src_ref=src, dst_ref=dst, send_sem=send_sems.at[slot],
            recv_sem=recv_sems.at[slot], device_id={"exp": peer}, device_id_type=MESH,
        )

    def consume(block, first=False):
        rows_in = x_ref[...] if first else y_ref[:, cols(block)]
        w_rows = pl.ds(pl.multiple_of(block * width, width), width)
        g_part = jnp.dot(rows_in, wg_v[w_rows, :], preferred_element_type=jnp.float32)
        u_part = jnp.dot(rows_in, wu_v[w_rows, :], preferred_element_type=jnp.float32)
        if first:
            g_acc[...] = g_part
            u_acc[...] = u_part
        else:
            g_acc[...] += g_part
            u_acc[...] += u_part

    own_cols = cols(me)
    sends = [
        remote(x_ref, y_ref.at[:, own_cols], 0, up),
        remote(x_ref, y_ref.at[:, own_cols], 1, dn),
        remote(x_ref, y_ref.at[:, own_cols], 2, sib),
    ]
    for copy in sends:
        copy.start()
    weight_copies[0].wait()
    weight_copies[1].wait()
    consume(me, first=True)
    remote(x_ref, y_ref.at[:, cols(dn)], 0, dn).wait_recv()
    remote(x_ref, y_ref.at[:, cols(up)], 1, up).wait_recv()
    second = [
        remote(y_ref.at[rows(1), cols(dn)], y_ref.at[rows(1), cols(dn)], 3, up),
        remote(y_ref.at[rows(0), cols(up)], y_ref.at[rows(0), cols(up)], 4, dn),
        remote(y_ref.at[:, cols(dn)], y_ref.at[:, cols(dn)], 5, sib),
        remote(y_ref.at[:, cols(up)], y_ref.at[:, cols(up)], 6, sib),
    ]
    for copy in second:
        copy.start()
    sends += second
    consume(dn)
    consume(up)
    remote(y_ref.at[rows(1), cols(far)], y_ref.at[rows(1), cols(far)], 3, dn).wait_recv()
    remote(y_ref.at[rows(0), cols(far)], y_ref.at[rows(0), cols(far)], 4, up).wait_recv()
    third = remote(y_ref.at[:, cols(far)], y_ref.at[:, cols(far)], 7, sib)
    third.start()
    sends.append(third)
    consume(far)
    sib_up = 2 * lax.rem(z + 1, chips) + 1 - core
    sib_dn = 2 * lax.rem(z + chips - 1, chips) + 1 - core
    sib_far = 2 * lax.rem(z + 2, chips) + 1 - core
    for block, slot in ((sib, 2), (sib_dn, 5), (sib_up, 6), (sib_far, 7)):
        remote(y_ref.at[:, cols(block)], y_ref.at[:, cols(block)], slot, sib).wait_recv()
        consume(block)
    g = g_acc[...]
    act = (g / (1.0 + jnp.exp(-g)) * u_acc[...]).astype(wd_v.dtype)
    weight_copies[2].wait()

    def down(block):
        return jnp.dot(act, wd_v[:, cols(block)], preferred_element_type=jnp.float32).astype(
            sib_out.dtype
        )

    def rs_remote(src, dst, slot, peer):
        return pltpu.make_async_remote_copy(
            src_ref=src, dst_ref=dst, send_sem=rs_send.at[slot],
            recv_sem=rs_recv.at[slot], device_id={"exp": peer}, device_id_type=MESH,
        )

    mine = (me, up, dn, far)
    theirs = tuple(block + 1 - 2 * core for block in mine)
    for k in range(4):
        sib_out[k] = down(theirs[k])
        copy = rs_remote(sib_out.at[k], sib_buf.at[k], k, sib)
        copy.start()
        sends.append(copy)
    for k in (3, 1, 2, 0):
        own_part = down(mine[k]).astype(jnp.float32)
        rs_remote(sib_out.at[k], sib_buf.at[k], k, sib).wait_recv()
        acc[k] = own_part + sib_buf[k].astype(jnp.float32)
        if k == 3:
            stage[0] = acc[3].astype(stage.dtype)
            for part, peer, slot in ((0, up, 4), (1, dn, 5)):
                copy = rs_remote(stage.at[0, rows(part)], half_buf.at[part], slot, peer)
                copy.start()
                sends.append(copy)
    rs_remote(stage.at[0, rows(0)], half_buf.at[0], 4, dn).wait_recv()
    acc[1, rows(0)] = acc[1, rows(0)] + half_buf[0].astype(jnp.float32)
    stage[1] = acc[1].astype(stage.dtype)
    copy = rs_remote(stage.at[1], near_buf.at[0], 6, up)
    copy.start()
    sends.append(copy)
    rs_remote(stage.at[0, rows(1)], half_buf.at[1], 5, up).wait_recv()
    acc[2, rows(1)] = acc[2, rows(1)] + half_buf[1].astype(jnp.float32)
    stage[2] = acc[2].astype(stage.dtype)
    copy = rs_remote(stage.at[2], near_buf.at[1], 7, dn)
    copy.start()
    sends.append(copy)
    rs_remote(stage.at[1], near_buf.at[0], 6, dn).wait_recv()
    rs_remote(stage.at[2], near_buf.at[1], 7, up).wait_recv()
    o_ref[...] = (
        acc[0] + near_buf[0].astype(jnp.float32) + near_buf[1].astype(jnp.float32)
    ).astype(o_ref.dtype)
    for copy in sends:
        copy.wait_send()


def gather_ffn(x, w_gate, w_up, w_down, n, collective_id):
    rows_n, width = x.shape
    d, ff = w_gate.shape[1], w_gate.shape[2]
    return pl.pallas_call(
        functools.partial(gather_ffn_kernel, n),
        out_shape=jax.ShapeDtypeStruct((rows_n, w_down.shape[2] // n), x.dtype),
        in_specs=[pl.BlockSpec(memory_space=pltpu.VMEM)] + [pl.BlockSpec(memory_space=pl.ANY)] * 3,
        out_specs=pl.BlockSpec(memory_space=pltpu.VMEM),
        scratch_shapes=[
            pltpu.VMEM((rows_n, n * width), x.dtype),
            pltpu.VMEM((d, ff), w_gate.dtype),
            pltpu.VMEM((d, ff), w_up.dtype),
            pltpu.VMEM((ff, w_down.shape[2]), w_down.dtype),
            pltpu.VMEM((rows_n, ff), jnp.float32),
            pltpu.VMEM((rows_n, ff), jnp.float32),
            pltpu.SemaphoreType.DMA((8,)),
            pltpu.SemaphoreType.DMA((8,)),
            pltpu.SemaphoreType.DMA((3,)),
            pltpu.VMEM((4, rows_n, width), x.dtype),
            pltpu.VMEM((4, rows_n, width), x.dtype),
            pltpu.VMEM((4, rows_n, width), jnp.float32),
            pltpu.VMEM((3, rows_n, width), x.dtype),
            pltpu.VMEM((2, rows_n // 2, width), x.dtype),
            pltpu.VMEM((2, rows_n, width), x.dtype),
            pltpu.SemaphoreType.DMA((8,)),
            pltpu.SemaphoreType.DMA((8,)),
        ],
        compiler_params=pltpu.CompilerParams(
            collective_id=collective_id, has_side_effects=True, vmem_limit_bytes=60 * 1024 * 1024
        ),
    )(x, w_gate, w_up, w_down)

def pick_rows(source, row_index, live_slot):
    taken_rows = jnp.take(source, row_index, axis=0)
    return jnp.where(live_slot[:, None], taken_rows, jnp.zeros((), source.dtype))


def body(
    attention_out,
    residual,
    w_out,
    router_w,
    norm_gain,
    page_pool,
    page_table,
    cache_len,
    came_from,
    routes,
    w_gate,
    w_up,
    w_down,
):
    groups = lax.axis_size("req")
    own_group = lax.axis_index("req")
    row_req = attention_out.shape[0]
    rows_all = came_from.shape[0]
    pages_req = page_table.shape[1]
    page_len = page_pool.shape[1]
    kv_slice = page_pool.shape[2]
    experts = groups // 2
    targets = jnp.arange(groups, dtype=jnp.int32)
    local_ids = jnp.arange(row_req, dtype=jnp.int32)
    dest_of = (
        jnp.zeros((rows_all,), jnp.int32).at[came_from].set(jnp.arange(rows_all, dtype=jnp.int32))
    )
    dest_group = dest_of // row_req
    dest_hot = (
        (dest_group[:, None] == targets[None, :]).astype(jnp.int32).reshape(groups, row_req, groups)
    )
    pair_rank = jnp.sum((jnp.cumsum(dest_hot, axis=1) - dest_hot) * dest_hot, axis=2).reshape(
        rows_all
    )
    own_dest = lax.dynamic_slice_in_dim(dest_group, own_group * row_req, row_req)
    own_rank = lax.dynamic_slice_in_dim(pair_rank, own_group * row_req, row_req)
    chosen_send = (
        (own_dest[None, None, :] == targets[:, None, None])
        & (own_rank[None, None, :] == jnp.arange(MIG_PAIR, dtype=jnp.int32)[None, :, None])
        & (targets[:, None, None] != own_group)
    )
    send_index = jnp.sum(jnp.where(chosen_send, local_ids[None, None, :], 0), axis=2).reshape(-1)
    send_live = jnp.any(chosen_send, axis=2).reshape(-1)
    moved_attn, moved_resid = (
        lax.all_to_all(
            pick_rows(attention_out, send_index, send_live),
            "req",
            split_axis=0,
            concat_axis=0,
            tiled=True,
        ),
        lax.all_to_all(
            pick_rows(residual, send_index, send_live),
            "req",
            split_axis=0,
            concat_axis=0,
            tiled=True,
        ),
    )
    new_source = lax.dynamic_slice_in_dim(came_from, own_group * row_req, row_req)
    source_group = new_source // row_req
    stays_home = source_group == own_group
    arrival = jnp.where(
        stays_home,
        new_source - own_group * row_req,
        row_req + source_group * MIG_PAIR + jnp.take(pair_rank, new_source),
    )
    attn_new = jnp.take(jnp.concatenate([attention_out, moved_attn], axis=0), arrival, axis=0)
    resid_new = jnp.take(jnp.concatenate([residual, moved_resid], axis=0), arrival, axis=0)
    projected = jnp.dot(
        attn_new,
        lax.all_gather(w_out, "req", axis=0, tiled=True),
        preferred_element_type=jnp.float32,
    )
    hidden = resid_new.astype(jnp.float32) + projected
    squares = jnp.sum(hidden * hidden, axis=1)
    scaled = hidden * norm_gain[None, :]
    raw_logits = jnp.dot(scaled, router_w, precision=lax.Precision.HIGHEST)
    stats_t = jnp.concatenate([squares[None, :], raw_logits.T], axis=0)
    stats_t = jnp.pad(stats_t, ((0, 16 - stats_t.shape[0]), (0, 0)))
    n_exp = lax.axis_size("exp")
    row_stats = jnp.sum(exchange(stats_t, "exp", n_exp, True, 0), axis=0)[:9].T
    total_sq = row_stats[:, 0]
    inverse = lax.rsqrt(total_sq / D + EPSILON)
    normed = scaled * inverse[:, None]
    logits = row_stats[:, 1:] * inverse[:, None]
    normed_rows = normed.astype(jnp.bfloat16)
    expert_ids = jnp.arange(experts, dtype=jnp.int32)
    chosen = jnp.sum(
        jnp.where(routes[:, :, None] == expert_ids[None, None, :], logits[:, None, :], 0.0), axis=2
    )
    gate_first = jax.nn.sigmoid(chosen[:, 0] - chosen[:, 1])
    gate_second = jax.nn.sigmoid(chosen[:, 1] - chosen[:, 0])
    flat_routes = routes.reshape(-1)
    expert_hot = (flat_routes[:, None] == expert_ids[None, :]).astype(jnp.int32)
    expert_rank = jnp.sum((jnp.cumsum(expert_hot, axis=0) - expert_hot) * expert_hot, axis=1)
    target_dev = flat_routes + experts * (expert_rank % 2)
    slot_index = expert_rank // 2
    assign_ids = jnp.arange(flat_routes.shape[0], dtype=jnp.int32)
    chosen_slot = (target_dev[None, None, :] == targets[:, None, None]) & (
        slot_index[None, None, :] == jnp.arange(CAP, dtype=jnp.int32)[None, :, None]
    )
    slot_source = jnp.sum(
        jnp.where(chosen_slot, assign_ids[None, None, :] // 2, 0), axis=2
    ).reshape(-1)
    slot_live = jnp.any(chosen_slot, axis=2).reshape(-1)
    outgoing = pick_rows(normed_rows, slot_source, slot_live)
    arrived = exchange(
        outgoing.reshape(groups, -1, outgoing.shape[-1]), "req", groups, False, 1
    ).reshape(outgoing.shape)
    partial_value = gather_ffn(arrived, w_gate, w_up, w_down, lax.axis_size("exp"), 3)
    summed_value = partial_value
    lookup = target_dev * CAP + slot_index
    page_rows = jnp.take(page_pool, page_table.reshape(-1), axis=0).reshape(
        row_req, pages_req, page_len, kv_slice
    )
    position = (
        jnp.arange(pages_req, dtype=jnp.int32)[:, None] * page_len
        + jnp.arange(page_len, dtype=jnp.int32)[None, :]
    )
    kept_mask = position[None, :, :] < cache_len[:, None, None]
    page_rows = jnp.where(kept_mask[..., None], page_rows, jnp.zeros((), page_rows.dtype)).reshape(
        row_req, -1
    )
    page_send = pick_rows(page_rows, send_index, send_live).reshape(groups, summed_value.shape[0] // groups, -1)
    both = exchange(
        jnp.concatenate(
            [summed_value.reshape(groups, -1, summed_value.shape[-1]), page_send], axis=2
        ),
        "req",
        groups,
        False,
        2,
    )
    returned = both[:, :, :summed_value.shape[-1]].reshape(summed_value.shape)
    moved_pages = both[:, :, summed_value.shape[-1]:].reshape(groups * MIG_PAIR, -1)
    new_pages = jnp.take(
        jnp.concatenate([page_rows, moved_pages], axis=0), arrival, axis=0
    ).reshape(row_req, pages_req, page_len, kv_slice)
    taken_rows = jnp.take(returned, lookup, axis=0).reshape(row_req, 2, -1).astype(jnp.float32)
    expert_part = gate_first[:, None] * taken_rows[:, 0] + gate_second[:, None] * taken_rows[:, 1]
    mixed = hidden + expert_part
    return (mixed, new_pages)


def solution(mesh):
    in_specs = (
        P("req", None),
        P("req", "exp"),
        P("req", "exp"),
        P("exp", None),
        P("exp"),
        P("req", None, "exp"),
        P("req", None),
        P("req"),
        P(),
        P("req", None),
        P("req", None, "exp"),
        P("req", None, "exp"),
        P("req", "exp", None),
    )
    out_specs = (P("req", "exp"), P("req", None, None, "exp"))
    return jax.shard_map(body, mesh=mesh, in_specs=in_specs, out_specs=out_specs, check_vma=False)
```

```python
import jax
import jax.numpy as jnp
from jax import lax
from jax.experimental import pallas as pl
from jax.experimental.pallas import tpu as pltpu
from jax.sharding import PartitionSpec as P
import functools

D = 4096
CAP = 32
MIG_PAIR = 4


EPSILON = 1e-05

MESH = pl.DeviceIdType.MESH


def exchange_kernel(axis, n, gather, x_ref, y_ref, send_sems, recv_sems):
    me = lax.axis_index(axis)
    barrier = pltpu.get_barrier_semaphore()
    for k in range(1, n):
        pl.semaphore_signal(
            barrier, inc=1, device_id={axis: lax.rem(me + k, n)}, device_id_type=MESH
        )
    pl.semaphore_wait(barrier, n - 1)
    copies = []
    for k in range(1, n):
        peer = lax.rem(me + k, n)
        copy = pltpu.make_async_remote_copy(
            src_ref=x_ref if gather else x_ref.at[peer],
            dst_ref=y_ref.at[me],
            send_sem=send_sems.at[k],
            recv_sem=recv_sems.at[k],
            device_id={axis: peer},
            device_id_type=MESH,
        )
        copy.start()
        copies.append(copy)
    if gather:
        y_ref[me] = x_ref[...]
    else:
        y_ref[me] = x_ref[me]
    for k in range(1, n):
        copies[k - 1].wait_send()
        source = lax.rem(me + n - k, n)
        pltpu.make_async_remote_copy(
            src_ref=x_ref if gather else x_ref.at[source],
            dst_ref=y_ref.at[source],
            send_sem=send_sems.at[k],
            recv_sem=recv_sems.at[k],
            device_id={axis: source},
            device_id_type=MESH,
        ).wait_recv()


def exchange(x, axis, n, gather, collective_id):
    out_shape = (n,) + x.shape if gather else x.shape
    return pl.pallas_call(
        functools.partial(exchange_kernel, axis, n, gather),
        out_shape=jax.ShapeDtypeStruct(out_shape, x.dtype),
        in_specs=[pl.BlockSpec(memory_space=pltpu.VMEM)],
        out_specs=pl.BlockSpec(memory_space=pltpu.VMEM),
        scratch_shapes=[pltpu.SemaphoreType.DMA((n,)), pltpu.SemaphoreType.DMA((n,))],
        compiler_params=pltpu.CompilerParams(collective_id=collective_id, has_side_effects=True),
    )(x)


def exp_gather_kernel(n, x_ref, y_ref, send_sems, recv_sems):
    chips = n // 2
    width = x_ref.shape[1]
    half = x_ref.shape[0] // 2
    me = lax.axis_index("exp")
    z, core = me // 2, me % 2
    sib = 2 * z + 1 - core
    up = 2 * lax.rem(z + 1, chips) + core
    dn = 2 * lax.rem(z + chips - 1, chips) + core
    far = 2 * lax.rem(z + 2, chips) + core

    def cols(block):
        return pl.ds(pl.multiple_of(block * width, width), width)

    def rows(part):
        return pl.ds(part * half, half)

    barrier = pltpu.get_barrier_semaphore()
    for peer in (sib, up, dn):
        pl.semaphore_signal(barrier, inc=1, device_id={"exp": peer}, device_id_type=MESH)
    pl.semaphore_wait(barrier, 3)

    def remote(src, dst, slot, peer):
        return pltpu.make_async_remote_copy(
            src_ref=src, dst_ref=dst, send_sem=send_sems.at[slot],
            recv_sem=recv_sems.at[slot], device_id={"exp": peer}, device_id_type=MESH,
        )

    own_cols = cols(me)
    first = [
        remote(x_ref, y_ref.at[:, own_cols], 0, up),
        remote(x_ref, y_ref.at[:, own_cols], 1, dn),
        remote(x_ref, y_ref.at[:, own_cols], 2, sib),
    ]
    for copy in first:
        copy.start()
    y_ref[:, own_cols] = x_ref[...]
    remote(x_ref, y_ref.at[:, cols(dn)], 0, dn).wait_recv()
    remote(x_ref, y_ref.at[:, cols(up)], 1, up).wait_recv()
    second = [
        remote(y_ref.at[rows(1), cols(dn)], y_ref.at[rows(1), cols(dn)], 3, up),
        remote(y_ref.at[rows(0), cols(up)], y_ref.at[rows(0), cols(up)], 4, dn),
        remote(y_ref.at[:, cols(dn)], y_ref.at[:, cols(dn)], 5, sib),
        remote(y_ref.at[:, cols(up)], y_ref.at[:, cols(up)], 6, sib),
    ]
    for copy in second:
        copy.start()
    remote(y_ref.at[rows(1), cols(far)], y_ref.at[rows(1), cols(far)], 3, dn).wait_recv()
    remote(y_ref.at[rows(0), cols(far)], y_ref.at[rows(0), cols(far)], 4, up).wait_recv()
    third = remote(y_ref.at[:, cols(far)], y_ref.at[:, cols(far)], 7, sib)
    third.start()
    sib_z = 2 * z + 1 - core
    sib_up = 2 * lax.rem(z + 1, chips) + 1 - core
    sib_dn = 2 * lax.rem(z + chips - 1, chips) + 1 - core
    sib_far = 2 * lax.rem(z + 2, chips) + 1 - core
    remote(x_ref, y_ref.at[:, cols(sib_z)], 2, sib).wait_recv()
    remote(y_ref.at[:, cols(sib_dn)], y_ref.at[:, cols(sib_dn)], 5, sib).wait_recv()
    remote(y_ref.at[:, cols(sib_up)], y_ref.at[:, cols(sib_up)], 6, sib).wait_recv()
    remote(y_ref.at[:, cols(sib_far)], y_ref.at[:, cols(sib_far)], 7, sib).wait_recv()
    for copy in first + second + [third]:
        copy.wait_send()


def exp_gather(x, n, collective_id):
    return pl.pallas_call(
        functools.partial(exp_gather_kernel, n),
        out_shape=jax.ShapeDtypeStruct((x.shape[0], n * x.shape[1]), x.dtype),
        in_specs=[pl.BlockSpec(memory_space=pltpu.VMEM)],
        out_specs=pl.BlockSpec(memory_space=pltpu.VMEM),
        scratch_shapes=[pltpu.SemaphoreType.DMA((8,)), pltpu.SemaphoreType.DMA((8,))],
        compiler_params=pltpu.CompilerParams(collective_id=collective_id, has_side_effects=True),
    )(x)


def ffn_kernel(x_ref, wg_ref, wu_ref, wd_ref, o_ref, g_acc, u_acc):
    step = pl.program_id(0)

    @pl.when(step == 0)
    def _():
        g_acc[...] = jnp.zeros_like(g_acc)
        u_acc[...] = jnp.zeros_like(u_acc)

    x = x_ref[...]
    g_acc[...] += jnp.dot(x, wg_ref[...], preferred_element_type=jnp.float32)
    u_acc[...] += jnp.dot(x, wu_ref[...], preferred_element_type=jnp.float32)

    @pl.when(step == pl.num_programs(0) - 1)
    def _():
        g = g_acc[...]
        act = (g / (1.0 + jnp.exp(-g)) * u_acc[...]).astype(wd_ref.dtype)
        o_ref[...] = jnp.dot(act, wd_ref[...], preferred_element_type=jnp.float32).astype(
            o_ref.dtype
        )


def expert_ffn(x, wg, wu, wd, tk=512):
    rows_n, d = x.shape
    ff = wg.shape[1]
    return pl.pallas_call(
        ffn_kernel,
        out_shape=jax.ShapeDtypeStruct((rows_n, wd.shape[1]), x.dtype),
        grid=(d // tk,),
        in_specs=[
            pl.BlockSpec((rows_n, tk), lambda k: (0, k)),
            pl.BlockSpec((tk, ff), lambda k: (k, 0)),
            pl.BlockSpec((tk, ff), lambda k: (k, 0)),
            pl.BlockSpec((ff, wd.shape[1]), lambda k: (0, 0)),
        ],
        out_specs=pl.BlockSpec((rows_n, wd.shape[1]), lambda k: (0, 0)),
        scratch_shapes=[
            pltpu.VMEM((rows_n, ff), jnp.float32),
            pltpu.VMEM((rows_n, ff), jnp.float32),
        ],
        compiler_params=pltpu.CompilerParams(
            dimension_semantics=("arbitrary",), vmem_limit_bytes=56 * 1024 * 1024
        ),
        cost_estimate=pl.CostEstimate(
            flops=2 * rows_n * d * ff * 2 + 2 * rows_n * ff * wd.shape[1],
            transcendentals=rows_n * ff,
            bytes_accessed=2 * (rows_n * d + 2 * d * ff + ff * wd.shape[1] + rows_n * wd.shape[1]),
        ),
    )(x, wg, wu, wd)


def gather_ffn_kernel(
    n, x_ref, wg_hbm, wu_hbm, wd_hbm, o_ref,
    y_ref, wg_v, wu_v, wd_v, g_acc, u_acc, send_sems, recv_sems, w_sems,
    sib_out, sib_buf, acc, stage, half_buf, near_buf, rs_send, rs_recv,
):
    chips = n // 2
    width = x_ref.shape[1]
    half = x_ref.shape[0] // 2
    me = lax.axis_index("exp")
    z, core = me // 2, me % 2
    sib = 2 * z + 1 - core
    up = 2 * lax.rem(z + 1, chips) + core
    dn = 2 * lax.rem(z + chips - 1, chips) + core
    far = 2 * lax.rem(z + 2, chips) + core

    weight_copies = [
        pltpu.make_async_copy(src.at[0], dst, w_sems.at[i])
        for i, (src, dst) in enumerate(((wg_hbm, wg_v), (wu_hbm, wu_v), (wd_hbm, wd_v)))
    ]
    for copy in weight_copies:
        copy.start()

    def cols(block):
        return pl.ds(pl.multiple_of(block * width, width), width)

    def rows(part):
        return pl.ds(part * half, half)

    barrier = pltpu.get_barrier_semaphore()
    for peer in (sib, up, dn):
        pl.semaphore_signal(barrier, inc=1, device_id={"exp": peer}, device_id_type=MESH)
    pl.semaphore_wait(barrier, 3)

    def remote(src, dst, slot, peer):
        return pltpu.make_async_remote_copy(
            src_ref=src, dst_ref=dst, send_sem=send_sems.at[slot],
            recv_sem=recv_sems.at[slot], device_id={"exp": peer}, device_id_type=MESH,
        )

    def consume(block, first=False):
        rows_in = x_ref[...] if first else y_ref[:, cols(block)]
        w_rows = pl.ds(pl.multiple_of(block * width, width), width)
        g_part = jnp.dot(rows_in, wg_v[w_rows, :], preferred_element_type=jnp.float32)
        u_part = jnp.dot(rows_in, wu_v[w_rows, :], preferred_element_type=jnp.float32)
        if first:
            g_acc[...] = g_part
            u_acc[...] = u_part
        else:
            g_acc[...] += g_part
            u_acc[...] += u_part

    own_cols = cols(me)
    sends = [
        remote(x_ref, y_ref.at[:, own_cols], 0, up),
        remote(x_ref, y_ref.at[:, own_cols], 1, dn),
        remote(x_ref, y_ref.at[:, own_cols], 2, sib),
    ]
    for copy in sends:
        copy.start()
    weight_copies[0].wait()
    weight_copies[1].wait()
    consume(me, first=True)
    remote(x_ref, y_ref.at[:, cols(dn)], 0, dn).wait_recv()
    remote(x_ref, y_ref.at[:, cols(up)], 1, up).wait_recv()
    second = [
        remote(y_ref.at[rows(1), cols(dn)], y_ref.at[rows(1), cols(dn)], 3, up),
        remote(y_ref.at[rows(0), cols(up)], y_ref.at[rows(0), cols(up)], 4, dn),
        remote(y_ref.at[:, cols(dn)], y_ref.at[:, cols(dn)], 5, sib),
        remote(y_ref.at[:, cols(up)], y_ref.at[:, cols(up)], 6, sib),
    ]
    for copy in second:
        copy.start()
    sends += second
    consume(dn)
    consume(up)
    remote(y_ref.at[rows(1), cols(far)], y_ref.at[rows(1), cols(far)], 3, dn).wait_recv()
    remote(y_ref.at[rows(0), cols(far)], y_ref.at[rows(0), cols(far)], 4, up).wait_recv()
    third = remote(y_ref.at[:, cols(far)], y_ref.at[:, cols(far)], 7, sib)
    third.start()
    sends.append(third)
    consume(far)
    sib_up = 2 * lax.rem(z + 1, chips) + 1 - core
    sib_dn = 2 * lax.rem(z + chips - 1, chips) + 1 - core
    sib_far = 2 * lax.rem(z + 2, chips) + 1 - core
    for block, slot in ((sib, 2), (sib_dn, 5), (sib_up, 6), (sib_far, 7)):
        remote(y_ref.at[:, cols(block)], y_ref.at[:, cols(block)], slot, sib).wait_recv()
        consume(block)
    g = g_acc[...]
    act = (g / (1.0 + jnp.exp(-g)) * u_acc[...]).astype(wd_v.dtype)
    weight_copies[2].wait()

    def down(block):
        return jnp.dot(act, wd_v[:, cols(block)], preferred_element_type=jnp.float32).astype(
            sib_out.dtype
        )

    def rs_remote(src, dst, slot, peer):
        return pltpu.make_async_remote_copy(
            src_ref=src, dst_ref=dst, send_sem=rs_send.at[slot],
            recv_sem=rs_recv.at[slot], device_id={"exp": peer}, device_id_type=MESH,
        )

    mine = (me, up, dn, far)
    theirs = tuple(block + 1 - 2 * core for block in mine)
    for k in range(4):
        sib_out[k] = down(theirs[k])
        copy = rs_remote(sib_out.at[k], sib_buf.at[k], k, sib)
        copy.start()
        sends.append(copy)
    for k in (3, 1, 2, 0):
        own_part = down(mine[k]).astype(jnp.float32)
        rs_remote(sib_out.at[k], sib_buf.at[k], k, sib).wait_recv()
        acc[k] = own_part + sib_buf[k].astype(jnp.float32)
        if k == 3:
            stage[0] = acc[3].astype(stage.dtype)
            for part, peer, slot in ((0, up, 4), (1, dn, 5)):
                copy = rs_remote(stage.at[0, rows(part)], half_buf.at[part], slot, peer)
                copy.start()
                sends.append(copy)
    rs_remote(stage.at[0, rows(0)], half_buf.at[0], 4, dn).wait_recv()
    acc[1, rows(0)] = acc[1, rows(0)] + half_buf[0].astype(jnp.float32)
    stage[1] = acc[1].astype(stage.dtype)
    copy = rs_remote(stage.at[1], near_buf.at[0], 6, up)
    copy.start()
    sends.append(copy)
    rs_remote(stage.at[0, rows(1)], half_buf.at[1], 5, up).wait_recv()
    acc[2, rows(1)] = acc[2, rows(1)] + half_buf[1].astype(jnp.float32)
    stage[2] = acc[2].astype(stage.dtype)
    copy = rs_remote(stage.at[2], near_buf.at[1], 7, dn)
    copy.start()
    sends.append(copy)
    rs_remote(stage.at[1], near_buf.at[0], 6, dn).wait_recv()
    rs_remote(stage.at[2], near_buf.at[1], 7, up).wait_recv()
    o_ref[...] = (
        acc[0] + near_buf[0].astype(jnp.float32) + near_buf[1].astype(jnp.float32)
    ).astype(o_ref.dtype)
    for copy in sends:
        copy.wait_send()


def gather_ffn(x, w_gate, w_up, w_down, n, collective_id):
    rows_n, width = x.shape
    d, ff = w_gate.shape[1], w_gate.shape[2]
    return pl.pallas_call(
        functools.partial(gather_ffn_kernel, n),
        out_shape=jax.ShapeDtypeStruct((rows_n, w_down.shape[2] // n), x.dtype),
        in_specs=[pl.BlockSpec(memory_space=pltpu.VMEM)] + [pl.BlockSpec(memory_space=pl.ANY)] * 3,
        out_specs=pl.BlockSpec(memory_space=pltpu.VMEM),
        scratch_shapes=[
            pltpu.VMEM((rows_n, n * width), x.dtype),
            pltpu.VMEM((d, ff), w_gate.dtype),
            pltpu.VMEM((d, ff), w_up.dtype),
            pltpu.VMEM((ff, w_down.shape[2]), w_down.dtype),
            pltpu.VMEM((rows_n, ff), jnp.float32),
            pltpu.VMEM((rows_n, ff), jnp.float32),
            pltpu.SemaphoreType.DMA((8,)),
            pltpu.SemaphoreType.DMA((8,)),
            pltpu.SemaphoreType.DMA((3,)),
            pltpu.VMEM((4, rows_n, width), x.dtype),
            pltpu.VMEM((4, rows_n, width), x.dtype),
            pltpu.VMEM((4, rows_n, width), jnp.float32),
            pltpu.VMEM((3, rows_n, width), x.dtype),
            pltpu.VMEM((2, rows_n // 2, width), x.dtype),
            pltpu.VMEM((2, rows_n, width), x.dtype),
            pltpu.SemaphoreType.DMA((8,)),
            pltpu.SemaphoreType.DMA((8,)),
        ],
        compiler_params=pltpu.CompilerParams(
            collective_id=collective_id, has_side_effects=True, vmem_limit_bytes=60 * 1024 * 1024
        ),
        cost_estimate=pl.CostEstimate(
            flops=2 * rows_n * d * ff * 3,
            transcendentals=rows_n * ff,
            bytes_accessed=2 * (3 * d * ff + 2 * rows_n * d),
        ),
    )(x, w_gate, w_up, w_down)

def pick_rows(source, row_index, live_slot):
    taken_rows = jnp.take(source, row_index, axis=0)
    return jnp.where(live_slot[:, None], taken_rows, jnp.zeros((), source.dtype))


def body(
    attention_out,
    residual,
    w_out,
    router_w,
    norm_gain,
    page_pool,
    page_table,
    cache_len,
    came_from,
    routes,
    w_gate,
    w_up,
    w_down,
):
    groups = lax.axis_size("req")
    own_group = lax.axis_index("req")
    row_req = attention_out.shape[0]
    rows_all = came_from.shape[0]
    pages_req = page_table.shape[1]
    page_len = page_pool.shape[1]
    kv_slice = page_pool.shape[2]
    experts = groups // 2
    targets = jnp.arange(groups, dtype=jnp.int32)
    local_ids = jnp.arange(row_req, dtype=jnp.int32)
    dest_of = (
        jnp.zeros((rows_all,), jnp.int32).at[came_from].set(jnp.arange(rows_all, dtype=jnp.int32))
    )
    dest_group = dest_of // row_req
    dest_hot = (
        (dest_group[:, None] == targets[None, :]).astype(jnp.int32).reshape(groups, row_req, groups)
    )
    pair_rank = jnp.sum((jnp.cumsum(dest_hot, axis=1) - dest_hot) * dest_hot, axis=2).reshape(
        rows_all
    )
    own_dest = lax.dynamic_slice_in_dim(dest_group, own_group * row_req, row_req)
    own_rank = lax.dynamic_slice_in_dim(pair_rank, own_group * row_req, row_req)
    chosen_send = (
        (own_dest[None, None, :] == targets[:, None, None])
        & (own_rank[None, None, :] == jnp.arange(MIG_PAIR, dtype=jnp.int32)[None, :, None])
        & (targets[:, None, None] != own_group)
    )
    send_index = jnp.sum(jnp.where(chosen_send, local_ids[None, None, :], 0), axis=2).reshape(-1)
    send_live = jnp.any(chosen_send, axis=2).reshape(-1)
    moved_attn, moved_resid = (
        lax.all_to_all(
            pick_rows(attention_out, send_index, send_live),
            "req",
            split_axis=0,
            concat_axis=0,
            tiled=True,
        ),
        lax.all_to_all(
            pick_rows(residual, send_index, send_live),
            "req",
            split_axis=0,
            concat_axis=0,
            tiled=True,
        ),
    )
    new_source = lax.dynamic_slice_in_dim(came_from, own_group * row_req, row_req)
    source_group = new_source // row_req
    stays_home = source_group == own_group
    arrival = jnp.where(
        stays_home,
        new_source - own_group * row_req,
        row_req + source_group * MIG_PAIR + jnp.take(pair_rank, new_source),
    )
    attn_new = jnp.take(jnp.concatenate([attention_out, moved_attn], axis=0), arrival, axis=0)
    resid_new = jnp.take(jnp.concatenate([residual, moved_resid], axis=0), arrival, axis=0)
    projected = jnp.dot(
        attn_new,
        lax.all_gather(w_out, "req", axis=0, tiled=True),
        preferred_element_type=jnp.float32,
    )
    hidden = resid_new.astype(jnp.float32) + projected
    squares = jnp.sum(hidden * hidden, axis=1)
    scaled = hidden * norm_gain[None, :]
    raw_logits = jnp.dot(scaled, router_w, precision=lax.Precision.HIGHEST)
    stats_t = jnp.concatenate([squares[None, :], raw_logits.T], axis=0)
    stats_t = jnp.pad(stats_t, ((0, 16 - stats_t.shape[0]), (0, 0)))
    n_exp = lax.axis_size("exp")
    row_stats = jnp.sum(exchange(stats_t, "exp", n_exp, True, 0), axis=0)[:9].T
    total_sq = row_stats[:, 0]
    inverse = lax.rsqrt(total_sq / D + EPSILON)
    normed = scaled * inverse[:, None]
    logits = row_stats[:, 1:] * inverse[:, None]
    normed_rows = normed.astype(jnp.bfloat16)
    expert_ids = jnp.arange(experts, dtype=jnp.int32)
    chosen = jnp.sum(
        jnp.where(routes[:, :, None] == expert_ids[None, None, :], logits[:, None, :], 0.0), axis=2
    )
    gate_first = jax.nn.sigmoid(chosen[:, 0] - chosen[:, 1])
    gate_second = jax.nn.sigmoid(chosen[:, 1] - chosen[:, 0])
    flat_routes = routes.reshape(-1)
    expert_hot = (flat_routes[:, None] == expert_ids[None, :]).astype(jnp.int32)
    expert_rank = jnp.sum((jnp.cumsum(expert_hot, axis=0) - expert_hot) * expert_hot, axis=1)
    target_dev = flat_routes + experts * (expert_rank % 2)
    slot_index = expert_rank // 2
    assign_ids = jnp.arange(flat_routes.shape[0], dtype=jnp.int32)
    chosen_slot = (target_dev[None, None, :] == targets[:, None, None]) & (
        slot_index[None, None, :] == jnp.arange(CAP, dtype=jnp.int32)[None, :, None]
    )
    slot_source = jnp.sum(
        jnp.where(chosen_slot, assign_ids[None, None, :] // 2, 0), axis=2
    ).reshape(-1)
    slot_live = jnp.any(chosen_slot, axis=2).reshape(-1)
    outgoing = pick_rows(normed_rows, slot_source, slot_live)
    arrived = exchange(
        outgoing.reshape(groups, -1, outgoing.shape[-1]), "req", groups, False, 1
    ).reshape(outgoing.shape)
    page_rows = jnp.take(page_pool, page_table.reshape(-1), axis=0).reshape(
        row_req, pages_req, page_len, kv_slice
    )
    position = (
        jnp.arange(pages_req, dtype=jnp.int32)[:, None] * page_len
        + jnp.arange(page_len, dtype=jnp.int32)[None, :]
    )
    kept_mask = position[None, :, :] < cache_len[:, None, None]
    page_rows = jnp.where(kept_mask[..., None], page_rows, jnp.zeros((), page_rows.dtype)).reshape(
        row_req, -1
    )
    page_send, arrived = lax.optimization_barrier(
        (pick_rows(page_rows, send_index, send_live), arrived)
    )
    moved_pages = lax.all_to_all(page_send, "req", split_axis=0, concat_axis=0, tiled=True)
    partial_value = gather_ffn(arrived, w_gate, w_up, w_down, lax.axis_size("exp"), 3)
    summed_value = partial_value
    lookup = target_dev * CAP + slot_index
    new_pages = jnp.take(
        jnp.concatenate([page_rows, moved_pages], axis=0), arrival, axis=0
    ).reshape(row_req, pages_req, page_len, kv_slice)
    returned = exchange(
        summed_value.reshape(groups, -1, summed_value.shape[-1]), "req", groups, False, 2
    ).reshape(summed_value.shape)
    taken_rows = jnp.take(returned, lookup, axis=0).reshape(row_req, 2, -1).astype(jnp.float32)
    expert_part = gate_first[:, None] * taken_rows[:, 0] + gate_second[:, None] * taken_rows[:, 1]
    mixed = hidden + expert_part
    return (mixed, new_pages)


def solution(mesh):
    in_specs = (
        P("req", None),
        P("req", "exp"),
        P("req", "exp"),
        P("exp", None),
        P("exp"),
        P("req", None, "exp"),
        P("req", None),
        P("req"),
        P(),
        P("req", None),
        P("req", None, "exp"),
        P("req", None, "exp"),
        P("req", "exp", None),
    )
    out_specs = (P("req", "exp"), P("req", None, None, "exp"))
    return jax.shard_map(body, mesh=mesh, in_specs=in_specs, out_specs=out_specs, check_vma=False)
```

```python
import jax
import jax.numpy as jnp
from jax import lax
from jax.experimental import pallas as pl
from jax.experimental.pallas import tpu as pltpu
from jax.sharding import PartitionSpec as P
import functools

D = 4096
CAP = 32
MIG_PAIR = 4


EPSILON = 1e-05

MESH = pl.DeviceIdType.MESH


def exchange_kernel(axis, n, gather, x_ref, y_ref, send_sems, recv_sems):
    me = lax.axis_index(axis)
    barrier = pltpu.get_barrier_semaphore()
    for k in range(1, n):
        pl.semaphore_signal(
            barrier, inc=1, device_id={axis: lax.rem(me + k, n)}, device_id_type=MESH
        )
    pl.semaphore_wait(barrier, n - 1)
    copies = []
    for k in range(1, n):
        peer = lax.rem(me + k, n)
        copy = pltpu.make_async_remote_copy(
            src_ref=x_ref if gather else x_ref.at[peer],
            dst_ref=y_ref.at[me],
            send_sem=send_sems.at[k],
            recv_sem=recv_sems.at[k],
            device_id={axis: peer},
            device_id_type=MESH,
        )
        copy.start()
        copies.append(copy)
    if gather:
        y_ref[me] = x_ref[...]
    else:
        y_ref[me] = x_ref[me]
    for k in range(1, n):
        copies[k - 1].wait_send()
        source = lax.rem(me + n - k, n)
        pltpu.make_async_remote_copy(
            src_ref=x_ref if gather else x_ref.at[source],
            dst_ref=y_ref.at[source],
            send_sem=send_sems.at[k],
            recv_sem=recv_sems.at[k],
            device_id={axis: source},
            device_id_type=MESH,
        ).wait_recv()


def exchange(x, axis, n, gather, collective_id):
    out_shape = (n,) + x.shape if gather else x.shape
    return pl.pallas_call(
        functools.partial(exchange_kernel, axis, n, gather),
        out_shape=jax.ShapeDtypeStruct(out_shape, x.dtype),
        in_specs=[pl.BlockSpec(memory_space=pltpu.VMEM)],
        out_specs=pl.BlockSpec(memory_space=pltpu.VMEM),
        scratch_shapes=[pltpu.SemaphoreType.DMA((n,)), pltpu.SemaphoreType.DMA((n,))],
        compiler_params=pltpu.CompilerParams(collective_id=collective_id, has_side_effects=True),
    )(x)


def exp_gather_kernel(n, x_ref, y_ref, send_sems, recv_sems):
    chips = n // 2
    width = x_ref.shape[1]
    half = x_ref.shape[0] // 2
    me = lax.axis_index("exp")
    z, core = me // 2, me % 2
    sib = 2 * z + 1 - core
    up = 2 * lax.rem(z + 1, chips) + core
    dn = 2 * lax.rem(z + chips - 1, chips) + core
    far = 2 * lax.rem(z + 2, chips) + core

    def cols(block):
        return pl.ds(pl.multiple_of(block * width, width), width)

    def rows(part):
        return pl.ds(part * half, half)

    barrier = pltpu.get_barrier_semaphore()
    for peer in (sib, up, dn):
        pl.semaphore_signal(barrier, inc=1, device_id={"exp": peer}, device_id_type=MESH)
    pl.semaphore_wait(barrier, 3)

    def remote(src, dst, slot, peer):
        return pltpu.make_async_remote_copy(
            src_ref=src, dst_ref=dst, send_sem=send_sems.at[slot],
            recv_sem=recv_sems.at[slot], device_id={"exp": peer}, device_id_type=MESH,
        )

    own_cols = cols(me)
    first = [
        remote(x_ref, y_ref.at[:, own_cols], 0, up),
        remote(x_ref, y_ref.at[:, own_cols], 1, dn),
        remote(x_ref, y_ref.at[:, own_cols], 2, sib),
    ]
    for copy in first:
        copy.start()
    y_ref[:, own_cols] = x_ref[...]
    remote(x_ref, y_ref.at[:, cols(dn)], 0, dn).wait_recv()
    remote(x_ref, y_ref.at[:, cols(up)], 1, up).wait_recv()
    second = [
        remote(y_ref.at[rows(1), cols(dn)], y_ref.at[rows(1), cols(dn)], 3, up),
        remote(y_ref.at[rows(0), cols(up)], y_ref.at[rows(0), cols(up)], 4, dn),
        remote(y_ref.at[:, cols(dn)], y_ref.at[:, cols(dn)], 5, sib),
        remote(y_ref.at[:, cols(up)], y_ref.at[:, cols(up)], 6, sib),
    ]
    for copy in second:
        copy.start()
    remote(y_ref.at[rows(1), cols(far)], y_ref.at[rows(1), cols(far)], 3, dn).wait_recv()
    remote(y_ref.at[rows(0), cols(far)], y_ref.at[rows(0), cols(far)], 4, up).wait_recv()
    third = remote(y_ref.at[:, cols(far)], y_ref.at[:, cols(far)], 7, sib)
    third.start()
    sib_z = 2 * z + 1 - core
    sib_up = 2 * lax.rem(z + 1, chips) + 1 - core
    sib_dn = 2 * lax.rem(z + chips - 1, chips) + 1 - core
    sib_far = 2 * lax.rem(z + 2, chips) + 1 - core
    remote(x_ref, y_ref.at[:, cols(sib_z)], 2, sib).wait_recv()
    remote(y_ref.at[:, cols(sib_dn)], y_ref.at[:, cols(sib_dn)], 5, sib).wait_recv()
    remote(y_ref.at[:, cols(sib_up)], y_ref.at[:, cols(sib_up)], 6, sib).wait_recv()
    remote(y_ref.at[:, cols(sib_far)], y_ref.at[:, cols(sib_far)], 7, sib).wait_recv()
    for copy in first + second + [third]:
        copy.wait_send()


def exp_gather(x, n, collective_id):
    return pl.pallas_call(
        functools.partial(exp_gather_kernel, n),
        out_shape=jax.ShapeDtypeStruct((x.shape[0], n * x.shape[1]), x.dtype),
        in_specs=[pl.BlockSpec(memory_space=pltpu.VMEM)],
        out_specs=pl.BlockSpec(memory_space=pltpu.VMEM),
        scratch_shapes=[pltpu.SemaphoreType.DMA((8,)), pltpu.SemaphoreType.DMA((8,))],
        compiler_params=pltpu.CompilerParams(collective_id=collective_id, has_side_effects=True),
    )(x)


def ffn_kernel(x_ref, wg_ref, wu_ref, wd_ref, o_ref, g_acc, u_acc):
    step = pl.program_id(0)

    @pl.when(step == 0)
    def _():
        g_acc[...] = jnp.zeros_like(g_acc)
        u_acc[...] = jnp.zeros_like(u_acc)

    x = x_ref[...]
    g_acc[...] += jnp.dot(x, wg_ref[...], preferred_element_type=jnp.float32)
    u_acc[...] += jnp.dot(x, wu_ref[...], preferred_element_type=jnp.float32)

    @pl.when(step == pl.num_programs(0) - 1)
    def _():
        g = g_acc[...]
        act = (g / (1.0 + jnp.exp(-g)) * u_acc[...]).astype(wd_ref.dtype)
        o_ref[...] = jnp.dot(act, wd_ref[...], preferred_element_type=jnp.float32).astype(
            o_ref.dtype
        )


def expert_ffn(x, wg, wu, wd, tk=512):
    rows_n, d = x.shape
    ff = wg.shape[1]
    return pl.pallas_call(
        ffn_kernel,
        out_shape=jax.ShapeDtypeStruct((rows_n, wd.shape[1]), x.dtype),
        grid=(d // tk,),
        in_specs=[
            pl.BlockSpec((rows_n, tk), lambda k: (0, k)),
            pl.BlockSpec((tk, ff), lambda k: (k, 0)),
            pl.BlockSpec((tk, ff), lambda k: (k, 0)),
            pl.BlockSpec((ff, wd.shape[1]), lambda k: (0, 0)),
        ],
        out_specs=pl.BlockSpec((rows_n, wd.shape[1]), lambda k: (0, 0)),
        scratch_shapes=[
            pltpu.VMEM((rows_n, ff), jnp.float32),
            pltpu.VMEM((rows_n, ff), jnp.float32),
        ],
        compiler_params=pltpu.CompilerParams(
            dimension_semantics=("arbitrary",), vmem_limit_bytes=56 * 1024 * 1024
        ),
        cost_estimate=pl.CostEstimate(
            flops=2 * rows_n * d * ff * 2 + 2 * rows_n * ff * wd.shape[1],
            transcendentals=rows_n * ff,
            bytes_accessed=2 * (rows_n * d + 2 * d * ff + ff * wd.shape[1] + rows_n * wd.shape[1]),
        ),
    )(x, wg, wu, wd)


def gather_ffn_kernel(
    n, x_ref, wg_hbm, wu_hbm, wd_hbm, o_ref,
    y_ref, wg_v, wu_v, wd_v, g_acc, u_acc, send_sems, recv_sems, w_sems,
    sib_out, sib_buf, acc, stage, half_buf, near_buf, rs_send, rs_recv,
):
    chips = n // 2
    width = x_ref.shape[1]
    half = x_ref.shape[0] // 2
    me = lax.axis_index("exp")
    z, core = me // 2, me % 2
    sib = 2 * z + 1 - core
    up = 2 * lax.rem(z + 1, chips) + core
    dn = 2 * lax.rem(z + chips - 1, chips) + core
    far = 2 * lax.rem(z + 2, chips) + core

    weight_copies = [
        pltpu.make_async_copy(src.at[0], dst, w_sems.at[i])
        for i, (src, dst) in enumerate(((wg_hbm, wg_v), (wu_hbm, wu_v), (wd_hbm, wd_v)))
    ]
    for copy in weight_copies:
        copy.start()

    def cols(block):
        return pl.ds(pl.multiple_of(block * width, width), width)

    def rows(part):
        return pl.ds(part * half, half)

    barrier = pltpu.get_barrier_semaphore()
    for peer in (sib, up, dn):
        pl.semaphore_signal(barrier, inc=1, device_id={"exp": peer}, device_id_type=MESH)
    pl.semaphore_wait(barrier, 3)

    def remote(src, dst, slot, peer):
        return pltpu.make_async_remote_copy(
            src_ref=src, dst_ref=dst, send_sem=send_sems.at[slot],
            recv_sem=recv_sems.at[slot], device_id={"exp": peer}, device_id_type=MESH,
        )

    def consume(block, first=False):
        rows_in = x_ref[...] if first else y_ref[:, cols(block)]
        w_rows = pl.ds(pl.multiple_of(block * width, width), width)
        g_part = jnp.dot(rows_in, wg_v[w_rows, :], preferred_element_type=jnp.float32)
        u_part = jnp.dot(rows_in, wu_v[w_rows, :], preferred_element_type=jnp.float32)
        if first:
            g_acc[...] = g_part
            u_acc[...] = u_part
        else:
            g_acc[...] += g_part
            u_acc[...] += u_part

    own_cols = cols(me)
    sends = [
        remote(x_ref, y_ref.at[:, own_cols], 0, up),
        remote(x_ref, y_ref.at[:, own_cols], 1, dn),
        remote(x_ref, y_ref.at[:, own_cols], 2, sib),
    ]
    for copy in sends:
        copy.start()
    weight_copies[0].wait()
    weight_copies[1].wait()
    consume(me, first=True)
    remote(x_ref, y_ref.at[:, cols(dn)], 0, dn).wait_recv()
    remote(x_ref, y_ref.at[:, cols(up)], 1, up).wait_recv()
    second = [
        remote(y_ref.at[rows(1), cols(dn)], y_ref.at[rows(1), cols(dn)], 3, up),
        remote(y_ref.at[rows(0), cols(up)], y_ref.at[rows(0), cols(up)], 4, dn),
        remote(y_ref.at[:, cols(dn)], y_ref.at[:, cols(dn)], 5, sib),
        remote(y_ref.at[:, cols(up)], y_ref.at[:, cols(up)], 6, sib),
    ]
    for copy in second:
        copy.start()
    sends += second
    consume(dn)
    consume(up)
    remote(y_ref.at[rows(1), cols(far)], y_ref.at[rows(1), cols(far)], 3, dn).wait_recv()
    remote(y_ref.at[rows(0), cols(far)], y_ref.at[rows(0), cols(far)], 4, up).wait_recv()
    third = remote(y_ref.at[:, cols(far)], y_ref.at[:, cols(far)], 7, sib)
    third.start()
    sends.append(third)
    consume(far)
    sib_up = 2 * lax.rem(z + 1, chips) + 1 - core
    sib_dn = 2 * lax.rem(z + chips - 1, chips) + 1 - core
    sib_far = 2 * lax.rem(z + 2, chips) + 1 - core
    for block, slot in ((sib, 2), (sib_dn, 5), (sib_up, 6), (sib_far, 7)):
        remote(y_ref.at[:, cols(block)], y_ref.at[:, cols(block)], slot, sib).wait_recv()
        consume(block)
    g = g_acc[...]
    act = (g / (1.0 + jnp.exp(-g)) * u_acc[...]).astype(wd_v.dtype)
    weight_copies[2].wait()

    def down(block):
        return jnp.dot(act, wd_v[:, cols(block)], preferred_element_type=jnp.float32).astype(
            sib_out.dtype
        )

    def rs_remote(src, dst, slot, peer):
        return pltpu.make_async_remote_copy(
            src_ref=src, dst_ref=dst, send_sem=rs_send.at[slot],
            recv_sem=rs_recv.at[slot], device_id={"exp": peer}, device_id_type=MESH,
        )

    mine = (me, up, dn, far)
    theirs = tuple(block + 1 - 2 * core for block in mine)
    for k in range(4):
        sib_out[k] = down(theirs[k])
        copy = rs_remote(sib_out.at[k], sib_buf.at[k], k, sib)
        copy.start()
        sends.append(copy)
    for k in (3, 1, 2, 0):
        own_part = down(mine[k]).astype(jnp.float32)
        rs_remote(sib_out.at[k], sib_buf.at[k], k, sib).wait_recv()
        acc[k] = own_part + sib_buf[k].astype(jnp.float32)
        if k == 3:
            stage[0] = acc[3].astype(stage.dtype)
            for part, peer, slot in ((0, up, 4), (1, dn, 5)):
                copy = rs_remote(stage.at[0, rows(part)], half_buf.at[part], slot, peer)
                copy.start()
                sends.append(copy)
    rs_remote(stage.at[0, rows(0)], half_buf.at[0], 4, dn).wait_recv()
    acc[1, rows(0)] = acc[1, rows(0)] + half_buf[0].astype(jnp.float32)
    stage[1] = acc[1].astype(stage.dtype)
    copy = rs_remote(stage.at[1], near_buf.at[0], 6, up)
    copy.start()
    sends.append(copy)
    rs_remote(stage.at[0, rows(1)], half_buf.at[1], 5, up).wait_recv()
    acc[2, rows(1)] = acc[2, rows(1)] + half_buf[1].astype(jnp.float32)
    stage[2] = acc[2].astype(stage.dtype)
    copy = rs_remote(stage.at[2], near_buf.at[1], 7, dn)
    copy.start()
    sends.append(copy)
    rs_remote(stage.at[1], near_buf.at[0], 6, dn).wait_recv()
    rs_remote(stage.at[2], near_buf.at[1], 7, up).wait_recv()
    o_ref[...] = (
        acc[0] + near_buf[0].astype(jnp.float32) + near_buf[1].astype(jnp.float32)
    ).astype(o_ref.dtype)
    for copy in sends:
        copy.wait_send()


def gather_ffn(x, w_gate, w_up, w_down, n, collective_id):
    rows_n, width = x.shape
    d, ff = w_gate.shape[1], w_gate.shape[2]
    return pl.pallas_call(
        functools.partial(gather_ffn_kernel, n),
        out_shape=jax.ShapeDtypeStruct((rows_n, w_down.shape[2] // n), x.dtype),
        in_specs=[pl.BlockSpec(memory_space=pltpu.VMEM)] + [pl.BlockSpec(memory_space=pl.ANY)] * 3,
        out_specs=pl.BlockSpec(memory_space=pltpu.VMEM),
        scratch_shapes=[
            pltpu.VMEM((rows_n, n * width), x.dtype),
            pltpu.VMEM((d, ff), w_gate.dtype),
            pltpu.VMEM((d, ff), w_up.dtype),
            pltpu.VMEM((ff, w_down.shape[2]), w_down.dtype),
            pltpu.VMEM((rows_n, ff), jnp.float32),
            pltpu.VMEM((rows_n, ff), jnp.float32),
            pltpu.SemaphoreType.DMA((8,)),
            pltpu.SemaphoreType.DMA((8,)),
            pltpu.SemaphoreType.DMA((3,)),
            pltpu.VMEM((4, rows_n, width), x.dtype),
            pltpu.VMEM((4, rows_n, width), x.dtype),
            pltpu.VMEM((4, rows_n, width), jnp.float32),
            pltpu.VMEM((3, rows_n, width), x.dtype),
            pltpu.VMEM((2, rows_n // 2, width), x.dtype),
            pltpu.VMEM((2, rows_n, width), x.dtype),
            pltpu.SemaphoreType.DMA((8,)),
            pltpu.SemaphoreType.DMA((8,)),
        ],
        compiler_params=pltpu.CompilerParams(
            collective_id=collective_id, has_side_effects=True, vmem_limit_bytes=60 * 1024 * 1024
        ),
        cost_estimate=pl.CostEstimate(
            flops=2 * rows_n * d * ff * 3,
            transcendentals=rows_n * ff,
            bytes_accessed=2 * (3 * d * ff + 2 * rows_n * d),
        ),
    )(x, w_gate, w_up, w_down)

def pick_rows(source, row_index, live_slot):
    taken_rows = jnp.take(source, row_index, axis=0)
    return jnp.where(live_slot[:, None], taken_rows, jnp.zeros((), source.dtype))


def body(
    attention_out,
    residual,
    w_out,
    router_w,
    norm_gain,
    page_pool,
    page_table,
    cache_len,
    came_from,
    routes,
    w_gate,
    w_up,
    w_down,
):
    groups = lax.axis_size("req")
    own_group = lax.axis_index("req")
    row_req = attention_out.shape[0]
    rows_all = came_from.shape[0]
    pages_req = page_table.shape[1]
    page_len = page_pool.shape[1]
    kv_slice = page_pool.shape[2]
    experts = groups // 2
    targets = jnp.arange(groups, dtype=jnp.int32)
    local_ids = jnp.arange(row_req, dtype=jnp.int32)
    dest_of = (
        jnp.zeros((rows_all,), jnp.int32).at[came_from].set(jnp.arange(rows_all, dtype=jnp.int32))
    )
    dest_group = dest_of // row_req
    dest_hot = (
        (dest_group[:, None] == targets[None, :]).astype(jnp.int32).reshape(groups, row_req, groups)
    )
    pair_rank = jnp.sum((jnp.cumsum(dest_hot, axis=1) - dest_hot) * dest_hot, axis=2).reshape(
        rows_all
    )
    own_dest = lax.dynamic_slice_in_dim(dest_group, own_group * row_req, row_req)
    own_rank = lax.dynamic_slice_in_dim(pair_rank, own_group * row_req, row_req)
    chosen_send = (
        (own_dest[None, None, :] == targets[:, None, None])
        & (own_rank[None, None, :] == jnp.arange(MIG_PAIR, dtype=jnp.int32)[None, :, None])
        & (targets[:, None, None] != own_group)
    )
    send_index = jnp.sum(jnp.where(chosen_send, local_ids[None, None, :], 0), axis=2).reshape(-1)
    send_live = jnp.any(chosen_send, axis=2).reshape(-1)
    moved_attn, moved_resid = (
        lax.all_to_all(
            pick_rows(attention_out, send_index, send_live),
            "req",
            split_axis=0,
            concat_axis=0,
            tiled=True,
        ),
        lax.all_to_all(
            pick_rows(residual, send_index, send_live),
            "req",
            split_axis=0,
            concat_axis=0,
            tiled=True,
        ),
    )
    new_source = lax.dynamic_slice_in_dim(came_from, own_group * row_req, row_req)
    source_group = new_source // row_req
    stays_home = source_group == own_group
    arrival = jnp.where(
        stays_home,
        new_source - own_group * row_req,
        row_req + source_group * MIG_PAIR + jnp.take(pair_rank, new_source),
    )
    attn_new = jnp.take(jnp.concatenate([attention_out, moved_attn], axis=0), arrival, axis=0)
    resid_new = jnp.take(jnp.concatenate([residual, moved_resid], axis=0), arrival, axis=0)
    projected = jnp.dot(
        attn_new,
        lax.all_gather(w_out, "req", axis=0, tiled=True),
        preferred_element_type=jnp.float32,
    )
    hidden = resid_new.astype(jnp.float32) + projected
    squares = jnp.sum(hidden * hidden, axis=1)
    scaled = hidden * norm_gain[None, :]
    raw_logits = jnp.dot(scaled, router_w, precision=lax.Precision.HIGHEST)
    stats_t = jnp.concatenate([squares[None, :], raw_logits.T], axis=0)
    stats_t = jnp.pad(stats_t, ((0, 16 - stats_t.shape[0]), (0, 0)))
    n_exp = lax.axis_size("exp")
    row_stats = jnp.sum(exchange(stats_t, "exp", n_exp, True, 0), axis=0)[:9].T
    total_sq = row_stats[:, 0]
    inverse = lax.rsqrt(total_sq / D + EPSILON)
    normed = scaled * inverse[:, None]
    logits = row_stats[:, 1:] * inverse[:, None]
    normed_rows = normed.astype(jnp.bfloat16)
    expert_ids = jnp.arange(experts, dtype=jnp.int32)
    chosen = jnp.sum(
        jnp.where(routes[:, :, None] == expert_ids[None, None, :], logits[:, None, :], 0.0), axis=2
    )
    gate_first = jax.nn.sigmoid(chosen[:, 0] - chosen[:, 1])
    gate_second = jax.nn.sigmoid(chosen[:, 1] - chosen[:, 0])
    flat_routes = routes.reshape(-1)
    expert_hot = (flat_routes[:, None] == expert_ids[None, :]).astype(jnp.int32)
    expert_rank = jnp.sum((jnp.cumsum(expert_hot, axis=0) - expert_hot) * expert_hot, axis=1)
    target_dev = flat_routes + experts * (expert_rank % 2)
    slot_index = expert_rank // 2
    assign_ids = jnp.arange(flat_routes.shape[0], dtype=jnp.int32)
    chosen_slot = (target_dev[None, None, :] == targets[:, None, None]) & (
        slot_index[None, None, :] == jnp.arange(CAP, dtype=jnp.int32)[None, :, None]
    )
    slot_source = jnp.sum(
        jnp.where(chosen_slot, assign_ids[None, None, :] // 2, 0), axis=2
    ).reshape(-1)
    slot_live = jnp.any(chosen_slot, axis=2).reshape(-1)
    outgoing = pick_rows(normed_rows, slot_source, slot_live)
    arrived = exchange(
        outgoing.reshape(groups, -1, outgoing.shape[-1]), "req", groups, False, 1
    ).reshape(outgoing.shape)
    page_pool, attn_new = lax.optimization_barrier((page_pool, attn_new))
    page_rows = jnp.take(page_pool, page_table.reshape(-1), axis=0).reshape(
        row_req, pages_req, page_len, kv_slice
    )
    position = (
        jnp.arange(pages_req, dtype=jnp.int32)[:, None] * page_len
        + jnp.arange(page_len, dtype=jnp.int32)[None, :]
    )
    kept_mask = position[None, :, :] < cache_len[:, None, None]
    page_rows = jnp.where(kept_mask[..., None], page_rows, jnp.zeros((), page_rows.dtype)).reshape(
        row_req, -1
    )
    page_send, arrived = lax.optimization_barrier(
        (pick_rows(page_rows, send_index, send_live), arrived)
    )
    moved_pages = lax.all_to_all(page_send, "req", split_axis=0, concat_axis=0, tiled=True)
    partial_value = gather_ffn(arrived, w_gate, w_up, w_down, lax.axis_size("exp"), 3)
    summed_value = partial_value
    lookup = target_dev * CAP + slot_index
    new_pages = jnp.take(
        jnp.concatenate([page_rows, moved_pages], axis=0), arrival, axis=0
    ).reshape(row_req, pages_req, page_len, kv_slice)
    returned = exchange(
        summed_value.reshape(groups, -1, summed_value.shape[-1]), "req", groups, False, 2
    ).reshape(summed_value.shape)
    taken_rows = jnp.take(returned, lookup, axis=0).reshape(row_req, 2, -1).astype(jnp.float32)
    expert_part = gate_first[:, None] * taken_rows[:, 0] + gate_second[:, None] * taken_rows[:, 1]
    mixed = hidden + expert_part
    return (mixed, new_pages)


def solution(mesh):
    in_specs = (
        P("req", None),
        P("req", "exp"),
        P("req", "exp"),
        P("exp", None),
        P("exp"),
        P("req", None, "exp"),
        P("req", None),
        P("req"),
        P(),
        P("req", None),
        P("req", None, "exp"),
        P("req", None, "exp"),
        P("req", "exp", None),
    )
    out_specs = (P("req", "exp"), P("req", None, None, "exp"))
    return jax.shard_map(body, mesh=mesh, in_specs=in_specs, out_specs=out_specs, check_vma=False)
```

```python
import jax
import jax.numpy as jnp
from jax import lax
from jax.experimental import pallas as pl
from jax.experimental.pallas import tpu as pltpu
from jax.sharding import PartitionSpec as P
import functools

D = 4096
CAP = 32
MIG_PAIR = 4


EPSILON = 1e-05

MESH = pl.DeviceIdType.MESH


def exchange_kernel(axis, n, gather, x_ref, y_ref, send_sems, recv_sems):
    me = lax.axis_index(axis)
    barrier = pltpu.get_barrier_semaphore()
    for k in range(1, n):
        pl.semaphore_signal(
            barrier, inc=1, device_id={axis: lax.rem(me + k, n)}, device_id_type=MESH
        )
    pl.semaphore_wait(barrier, n - 1)
    copies = []
    for k in range(1, n):
        peer = lax.rem(me + k, n)
        copy = pltpu.make_async_remote_copy(
            src_ref=x_ref if gather else x_ref.at[peer],
            dst_ref=y_ref.at[me],
            send_sem=send_sems.at[k],
            recv_sem=recv_sems.at[k],
            device_id={axis: peer},
            device_id_type=MESH,
        )
        copy.start()
        copies.append(copy)
    if gather:
        y_ref[me] = x_ref[...]
    else:
        y_ref[me] = x_ref[me]
    for k in range(1, n):
        copies[k - 1].wait_send()
        source = lax.rem(me + n - k, n)
        pltpu.make_async_remote_copy(
            src_ref=x_ref if gather else x_ref.at[source],
            dst_ref=y_ref.at[source],
            send_sem=send_sems.at[k],
            recv_sem=recv_sems.at[k],
            device_id={axis: source},
            device_id_type=MESH,
        ).wait_recv()


def exchange(x, axis, n, gather, collective_id):
    out_shape = (n,) + x.shape if gather else x.shape
    return pl.pallas_call(
        functools.partial(exchange_kernel, axis, n, gather),
        out_shape=jax.ShapeDtypeStruct(out_shape, x.dtype),
        in_specs=[pl.BlockSpec(memory_space=pltpu.VMEM)],
        out_specs=pl.BlockSpec(memory_space=pltpu.VMEM),
        scratch_shapes=[pltpu.SemaphoreType.DMA((n,)), pltpu.SemaphoreType.DMA((n,))],
        compiler_params=pltpu.CompilerParams(collective_id=collective_id, has_side_effects=True),
    )(x)


def exp_gather_kernel(n, x_ref, y_ref, send_sems, recv_sems):
    chips = n // 2
    width = x_ref.shape[1]
    half = x_ref.shape[0] // 2
    me = lax.axis_index("exp")
    z, core = me // 2, me % 2
    sib = 2 * z + 1 - core
    up = 2 * lax.rem(z + 1, chips) + core
    dn = 2 * lax.rem(z + chips - 1, chips) + core
    far = 2 * lax.rem(z + 2, chips) + core

    def cols(block):
        return pl.ds(pl.multiple_of(block * width, width), width)

    def rows(part):
        return pl.ds(part * half, half)

    barrier = pltpu.get_barrier_semaphore()
    for peer in (sib, up, dn):
        pl.semaphore_signal(barrier, inc=1, device_id={"exp": peer}, device_id_type=MESH)
    pl.semaphore_wait(barrier, 3)

    def remote(src, dst, slot, peer):
        return pltpu.make_async_remote_copy(
            src_ref=src, dst_ref=dst, send_sem=send_sems.at[slot],
            recv_sem=recv_sems.at[slot], device_id={"exp": peer}, device_id_type=MESH,
        )

    own_cols = cols(me)
    first = [
        remote(x_ref, y_ref.at[:, own_cols], 0, up),
        remote(x_ref, y_ref.at[:, own_cols], 1, dn),
        remote(x_ref, y_ref.at[:, own_cols], 2, sib),
    ]
    for copy in first:
        copy.start()
    y_ref[:, own_cols] = x_ref[...]
    remote(x_ref, y_ref.at[:, cols(dn)], 0, dn).wait_recv()
    remote(x_ref, y_ref.at[:, cols(up)], 1, up).wait_recv()
    second = [
        remote(y_ref.at[rows(1), cols(dn)], y_ref.at[rows(1), cols(dn)], 3, up),
        remote(y_ref.at[rows(0), cols(up)], y_ref.at[rows(0), cols(up)], 4, dn),
        remote(y_ref.at[:, cols(dn)], y_ref.at[:, cols(dn)], 5, sib),
        remote(y_ref.at[:, cols(up)], y_ref.at[:, cols(up)], 6, sib),
    ]
    for copy in second:
        copy.start()
    remote(y_ref.at[rows(1), cols(far)], y_ref.at[rows(1), cols(far)], 3, dn).wait_recv()
    remote(y_ref.at[rows(0), cols(far)], y_ref.at[rows(0), cols(far)], 4, up).wait_recv()
    third = remote(y_ref.at[:, cols(far)], y_ref.at[:, cols(far)], 7, sib)
    third.start()
    sib_z = 2 * z + 1 - core
    sib_up = 2 * lax.rem(z + 1, chips) + 1 - core
    sib_dn = 2 * lax.rem(z + chips - 1, chips) + 1 - core
    sib_far = 2 * lax.rem(z + 2, chips) + 1 - core
    remote(x_ref, y_ref.at[:, cols(sib_z)], 2, sib).wait_recv()
    remote(y_ref.at[:, cols(sib_dn)], y_ref.at[:, cols(sib_dn)], 5, sib).wait_recv()
    remote(y_ref.at[:, cols(sib_up)], y_ref.at[:, cols(sib_up)], 6, sib).wait_recv()
    remote(y_ref.at[:, cols(sib_far)], y_ref.at[:, cols(sib_far)], 7, sib).wait_recv()
    for copy in first + second + [third]:
        copy.wait_send()


def exp_gather(x, n, collective_id):
    return pl.pallas_call(
        functools.partial(exp_gather_kernel, n),
        out_shape=jax.ShapeDtypeStruct((x.shape[0], n * x.shape[1]), x.dtype),
        in_specs=[pl.BlockSpec(memory_space=pltpu.VMEM)],
        out_specs=pl.BlockSpec(memory_space=pltpu.VMEM),
        scratch_shapes=[pltpu.SemaphoreType.DMA((8,)), pltpu.SemaphoreType.DMA((8,))],
        compiler_params=pltpu.CompilerParams(collective_id=collective_id, has_side_effects=True),
    )(x)


def ffn_kernel(x_ref, wg_ref, wu_ref, wd_ref, o_ref, g_acc, u_acc):
    step = pl.program_id(0)

    @pl.when(step == 0)
    def _():
        g_acc[...] = jnp.zeros_like(g_acc)
        u_acc[...] = jnp.zeros_like(u_acc)

    x = x_ref[...]
    g_acc[...] += jnp.dot(x, wg_ref[...], preferred_element_type=jnp.float32)
    u_acc[...] += jnp.dot(x, wu_ref[...], preferred_element_type=jnp.float32)

    @pl.when(step == pl.num_programs(0) - 1)
    def _():
        g = g_acc[...]
        act = (g / (1.0 + jnp.exp(-g)) * u_acc[...]).astype(wd_ref.dtype)
        o_ref[...] = jnp.dot(act, wd_ref[...], preferred_element_type=jnp.float32).astype(
            o_ref.dtype
        )


def expert_ffn(x, wg, wu, wd, tk=512):
    rows_n, d = x.shape
    ff = wg.shape[1]
    return pl.pallas_call(
        ffn_kernel,
        out_shape=jax.ShapeDtypeStruct((rows_n, wd.shape[1]), x.dtype),
        grid=(d // tk,),
        in_specs=[
            pl.BlockSpec((rows_n, tk), lambda k: (0, k)),
            pl.BlockSpec((tk, ff), lambda k: (k, 0)),
            pl.BlockSpec((tk, ff), lambda k: (k, 0)),
            pl.BlockSpec((ff, wd.shape[1]), lambda k: (0, 0)),
        ],
        out_specs=pl.BlockSpec((rows_n, wd.shape[1]), lambda k: (0, 0)),
        scratch_shapes=[
            pltpu.VMEM((rows_n, ff), jnp.float32),
            pltpu.VMEM((rows_n, ff), jnp.float32),
        ],
        compiler_params=pltpu.CompilerParams(
            dimension_semantics=("arbitrary",), vmem_limit_bytes=56 * 1024 * 1024
        ),
        cost_estimate=pl.CostEstimate(
            flops=2 * rows_n * d * ff * 2 + 2 * rows_n * ff * wd.shape[1],
            transcendentals=rows_n * ff,
            bytes_accessed=2 * (rows_n * d + 2 * d * ff + ff * wd.shape[1] + rows_n * wd.shape[1]),
        ),
    )(x, wg, wu, wd)


def gather_ffn_kernel(
    n, x_ref, wg_hbm, wu_hbm, wd_hbm, o_ref,
    y_ref, wg_v, wu_v, wd_v, g_acc, u_acc, send_sems, recv_sems, w_sems,
):
    chips = n // 2
    width = x_ref.shape[1]
    half = x_ref.shape[0] // 2
    me = lax.axis_index("exp")
    z, core = me // 2, me % 2
    sib = 2 * z + 1 - core
    up = 2 * lax.rem(z + 1, chips) + core
    dn = 2 * lax.rem(z + chips - 1, chips) + core
    far = 2 * lax.rem(z + 2, chips) + core

    weight_copies = [
        pltpu.make_async_copy(src.at[0], dst, w_sems.at[i])
        for i, (src, dst) in enumerate(((wg_hbm, wg_v), (wu_hbm, wu_v), (wd_hbm, wd_v)))
    ]
    for copy in weight_copies:
        copy.start()

    def cols(block):
        return pl.ds(pl.multiple_of(block * width, width), width)

    def rows(part):
        return pl.ds(part * half, half)

    barrier = pltpu.get_barrier_semaphore()
    for peer in (sib, up, dn):
        pl.semaphore_signal(barrier, inc=1, device_id={"exp": peer}, device_id_type=MESH)
    pl.semaphore_wait(barrier, 3)

    def remote(src, dst, slot, peer):
        return pltpu.make_async_remote_copy(
            src_ref=src, dst_ref=dst, send_sem=send_sems.at[slot],
            recv_sem=recv_sems.at[slot], device_id={"exp": peer}, device_id_type=MESH,
        )

    def consume(block, first=False):
        rows_in = x_ref[...] if first else y_ref[:, cols(block)]
        w_rows = pl.ds(pl.multiple_of(block * width, width), width)
        g_part = jnp.dot(rows_in, wg_v[w_rows, :], preferred_element_type=jnp.float32)
        u_part = jnp.dot(rows_in, wu_v[w_rows, :], preferred_element_type=jnp.float32)
        if first:
            g_acc[...] = g_part
            u_acc[...] = u_part
        else:
            g_acc[...] += g_part
            u_acc[...] += u_part

    own_cols = cols(me)
    sends = [
        remote(x_ref, y_ref.at[:, own_cols], 0, up),
        remote(x_ref, y_ref.at[:, own_cols], 1, dn),
        remote(x_ref, y_ref.at[:, own_cols], 2, sib),
    ]
    for copy in sends:
        copy.start()
    weight_copies[0].wait()
    weight_copies[1].wait()
    consume(me, first=True)
    remote(x_ref, y_ref.at[:, cols(dn)], 0, dn).wait_recv()
    remote(x_ref, y_ref.at[:, cols(up)], 1, up).wait_recv()
    second = [
        remote(y_ref.at[rows(1), cols(dn)], y_ref.at[rows(1), cols(dn)], 3, up),
        remote(y_ref.at[rows(0), cols(up)], y_ref.at[rows(0), cols(up)], 4, dn),
        remote(y_ref.at[:, cols(dn)], y_ref.at[:, cols(dn)], 5, sib),
        remote(y_ref.at[:, cols(up)], y_ref.at[:, cols(up)], 6, sib),
    ]
    for copy in second:
        copy.start()
    sends += second
    consume(dn)
    consume(up)
    remote(y_ref.at[rows(1), cols(far)], y_ref.at[rows(1), cols(far)], 3, dn).wait_recv()
    remote(y_ref.at[rows(0), cols(far)], y_ref.at[rows(0), cols(far)], 4, up).wait_recv()
    third = remote(y_ref.at[:, cols(far)], y_ref.at[:, cols(far)], 7, sib)
    third.start()
    sends.append(third)
    consume(far)
    sib_up = 2 * lax.rem(z + 1, chips) + 1 - core
    sib_dn = 2 * lax.rem(z + chips - 1, chips) + 1 - core
    sib_far = 2 * lax.rem(z + 2, chips) + 1 - core
    for block, slot in ((sib, 2), (sib_dn, 5), (sib_up, 6), (sib_far, 7)):
        remote(y_ref.at[:, cols(block)], y_ref.at[:, cols(block)], slot, sib).wait_recv()
        consume(block)
    g = g_acc[...]
    act = (g / (1.0 + jnp.exp(-g)) * u_acc[...]).astype(wd_v.dtype)
    weight_copies[2].wait()
    out_cols = o_ref.shape[1]
    chunk = out_cols // 8
    for c in range(8):
        span = pl.ds(c * chunk, chunk)
        o_ref[:, span] = jnp.dot(act, wd_v[:, span], preferred_element_type=jnp.float32).astype(
            o_ref.dtype
        )
    for copy in sends:
        copy.wait_send()


def gather_ffn(x, w_gate, w_up, w_down, n, collective_id):
    rows_n, width = x.shape
    d, ff = w_gate.shape[1], w_gate.shape[2]
    return pl.pallas_call(
        functools.partial(gather_ffn_kernel, n),
        out_shape=jax.ShapeDtypeStruct((rows_n, w_down.shape[2]), x.dtype),
        in_specs=[pl.BlockSpec(memory_space=pltpu.VMEM)] + [pl.BlockSpec(memory_space=pl.ANY)] * 3,
        out_specs=pl.BlockSpec(memory_space=pltpu.VMEM),
        scratch_shapes=[
            pltpu.VMEM((rows_n, n * width), x.dtype),
            pltpu.VMEM((d, ff), w_gate.dtype),
            pltpu.VMEM((d, ff), w_up.dtype),
            pltpu.VMEM((ff, w_down.shape[2]), w_down.dtype),
            pltpu.VMEM((rows_n, ff), jnp.float32),
            pltpu.VMEM((rows_n, ff), jnp.float32),
            pltpu.SemaphoreType.DMA((8,)),
            pltpu.SemaphoreType.DMA((8,)),
            pltpu.SemaphoreType.DMA((3,)),
        ],
        compiler_params=pltpu.CompilerParams(
            collective_id=collective_id, has_side_effects=True, vmem_limit_bytes=60 * 1024 * 1024
        ),
    )(x, w_gate, w_up, w_down)


def pick_rows(source, row_index, live_slot):
    taken_rows = jnp.take(source, row_index, axis=0)
    return jnp.where(live_slot[:, None], taken_rows, jnp.zeros((), source.dtype))


def body(
    attention_out,
    residual,
    w_out,
    router_w,
    norm_gain,
    page_pool,
    page_table,
    cache_len,
    came_from,
    routes,
    w_gate,
    w_up,
    w_down,
):
    groups = lax.axis_size("req")
    own_group = lax.axis_index("req")
    row_req = attention_out.shape[0]
    rows_all = came_from.shape[0]
    pages_req = page_table.shape[1]
    page_len = page_pool.shape[1]
    kv_slice = page_pool.shape[2]
    experts = groups // 2
    targets = jnp.arange(groups, dtype=jnp.int32)
    local_ids = jnp.arange(row_req, dtype=jnp.int32)
    dest_of = (
        jnp.zeros((rows_all,), jnp.int32).at[came_from].set(jnp.arange(rows_all, dtype=jnp.int32))
    )
    dest_group = dest_of // row_req
    dest_hot = (
        (dest_group[:, None] == targets[None, :]).astype(jnp.int32).reshape(groups, row_req, groups)
    )
    pair_rank = jnp.sum((jnp.cumsum(dest_hot, axis=1) - dest_hot) * dest_hot, axis=2).reshape(
        rows_all
    )
    own_dest = lax.dynamic_slice_in_dim(dest_group, own_group * row_req, row_req)
    own_rank = lax.dynamic_slice_in_dim(pair_rank, own_group * row_req, row_req)
    chosen_send = (
        (own_dest[None, None, :] == targets[:, None, None])
        & (own_rank[None, None, :] == jnp.arange(MIG_PAIR, dtype=jnp.int32)[None, :, None])
        & (targets[:, None, None] != own_group)
    )
    send_index = jnp.sum(jnp.where(chosen_send, local_ids[None, None, :], 0), axis=2).reshape(-1)
    send_live = jnp.any(chosen_send, axis=2).reshape(-1)
    moved_attn, moved_resid = (
        lax.all_to_all(
            pick_rows(attention_out, send_index, send_live),
            "req",
            split_axis=0,
            concat_axis=0,
            tiled=True,
        ),
        lax.all_to_all(
            pick_rows(residual, send_index, send_live),
            "req",
            split_axis=0,
            concat_axis=0,
            tiled=True,
        ),
    )
    new_source = lax.dynamic_slice_in_dim(came_from, own_group * row_req, row_req)
    source_group = new_source // row_req
    stays_home = source_group == own_group
    arrival = jnp.where(
        stays_home,
        new_source - own_group * row_req,
        row_req + source_group * MIG_PAIR + jnp.take(pair_rank, new_source),
    )
    attn_new = jnp.take(jnp.concatenate([attention_out, moved_attn], axis=0), arrival, axis=0)
    resid_new = jnp.take(jnp.concatenate([residual, moved_resid], axis=0), arrival, axis=0)
    projected = jnp.dot(
        attn_new,
        lax.all_gather(w_out, "req", axis=0, tiled=True),
        preferred_element_type=jnp.float32,
    )
    hidden = resid_new.astype(jnp.float32) + projected
    squares = jnp.sum(hidden * hidden, axis=1)
    scaled = hidden * norm_gain[None, :]
    raw_logits = jnp.sum(scaled[:, None, :] * router_w.T[None, :, :], axis=2)
    stats_t = jnp.concatenate([squares[None, :], raw_logits.T], axis=0)
    stats_t = jnp.pad(stats_t, ((0, 16 - stats_t.shape[0]), (0, 0)))
    n_exp = lax.axis_size("exp")
    row_stats = jnp.sum(exchange(stats_t, "exp", n_exp, True, 0), axis=0)[:9].T
    total_sq = row_stats[:, 0]
    inverse = lax.rsqrt(total_sq / D + EPSILON)
    normed = scaled * inverse[:, None]
    logits = row_stats[:, 1:] * inverse[:, None]
    normed_rows = normed.astype(jnp.bfloat16)
    expert_ids = jnp.arange(experts, dtype=jnp.int32)
    chosen = jnp.sum(
        jnp.where(routes[:, :, None] == expert_ids[None, None, :], logits[:, None, :], 0.0), axis=2
    )
    gate_first = jax.nn.sigmoid(chosen[:, 0] - chosen[:, 1])
    gate_second = jax.nn.sigmoid(chosen[:, 1] - chosen[:, 0])
    flat_routes = routes.reshape(-1)
    expert_hot = (flat_routes[:, None] == expert_ids[None, :]).astype(jnp.int32)
    expert_rank = jnp.sum((jnp.cumsum(expert_hot, axis=0) - expert_hot) * expert_hot, axis=1)
    target_dev = flat_routes + experts * (expert_rank % 2)
    slot_index = expert_rank // 2
    assign_ids = jnp.arange(flat_routes.shape[0], dtype=jnp.int32)
    chosen_slot = (target_dev[None, None, :] == targets[:, None, None]) & (
        slot_index[None, None, :] == jnp.arange(CAP, dtype=jnp.int32)[None, :, None]
    )
    slot_source = jnp.sum(
        jnp.where(chosen_slot, assign_ids[None, None, :] // 2, 0), axis=2
    ).reshape(-1)
    slot_live = jnp.any(chosen_slot, axis=2).reshape(-1)
    outgoing = pick_rows(normed_rows, slot_source, slot_live)
    arrived = exchange(
        outgoing.reshape(groups, -1, outgoing.shape[-1]), "req", groups, False, 1
    ).reshape(outgoing.shape)
    partial_value = gather_ffn(arrived, w_gate, w_up, w_down, lax.axis_size("exp"), 3)
    partial_value, page_pool = lax.optimization_barrier((partial_value, page_pool))
    summed_value = lax.psum_scatter(partial_value, "exp", scatter_dimension=1, tiled=True)
    page_rows = jnp.take(page_pool, page_table.reshape(-1), axis=0).reshape(
        row_req, pages_req, page_len, kv_slice
    )
    position = (
        jnp.arange(pages_req, dtype=jnp.int32)[:, None] * page_len
        + jnp.arange(page_len, dtype=jnp.int32)[None, :]
    )
    kept_mask = position[None, :, :] < cache_len[:, None, None]
    page_rows = jnp.where(kept_mask[..., None], page_rows, jnp.zeros((), page_rows.dtype)).reshape(
        row_req, -1
    )
    moved_pages = lax.all_to_all(
        pick_rows(page_rows, send_index, send_live), "req", split_axis=0, concat_axis=0, tiled=True
    )
    new_pages = jnp.take(
        jnp.concatenate([page_rows, moved_pages], axis=0), arrival, axis=0
    ).reshape(row_req, pages_req, page_len, kv_slice)
    lookup = target_dev * CAP + slot_index
    returned = exchange(
        summed_value.reshape(groups, -1, summed_value.shape[-1]), "req", groups, False, 2
    ).reshape(summed_value.shape)
    taken_rows = jnp.take(returned, lookup, axis=0).reshape(row_req, 2, -1).astype(jnp.float32)
    expert_part = gate_first[:, None] * taken_rows[:, 0] + gate_second[:, None] * taken_rows[:, 1]
    mixed = hidden + expert_part
    return (mixed, new_pages)


def solution(mesh):
    in_specs = (
        P("req", None),
        P("req", "exp"),
        P("req", "exp"),
        P("exp", None),
        P("exp"),
        P("req", None, "exp"),
        P("req", None),
        P("req"),
        P(),
        P("req", None),
        P("req", None, "exp"),
        P("req", None, "exp"),
        P("req", "exp", None),
    )
    out_specs = (P("req", "exp"), P("req", None, None, "exp"))
    return jax.shard_map(body, mesh=mesh, in_specs=in_specs, out_specs=out_specs, check_vma=False)
```

```python
import jax
import jax.numpy as jnp
from jax import lax
from jax.experimental import pallas as pl
from jax.experimental.pallas import tpu as pltpu
from jax.sharding import PartitionSpec as P
import functools

D = 4096
CAP = 32
MIG_PAIR = 4


EPSILON = 1e-05

MESH = pl.DeviceIdType.MESH


def exchange_kernel(axis, n, gather, x_ref, y_ref, send_sems, recv_sems):
    me = lax.axis_index(axis)
    barrier = pltpu.get_barrier_semaphore()
    for k in range(1, n):
        pl.semaphore_signal(
            barrier, inc=1, device_id={axis: lax.rem(me + k, n)}, device_id_type=MESH
        )
    pl.semaphore_wait(barrier, n - 1)
    copies = []
    for k in range(1, n):
        peer = lax.rem(me + k, n)
        copy = pltpu.make_async_remote_copy(
            src_ref=x_ref if gather else x_ref.at[peer],
            dst_ref=y_ref.at[me],
            send_sem=send_sems.at[k],
            recv_sem=recv_sems.at[k],
            device_id={axis: peer},
            device_id_type=MESH,
        )
        copy.start()
        copies.append(copy)
    if gather:
        y_ref[me] = x_ref[...]
    else:
        y_ref[me] = x_ref[me]
    for k in range(1, n):
        copies[k - 1].wait_send()
        source = lax.rem(me + n - k, n)
        pltpu.make_async_remote_copy(
            src_ref=x_ref if gather else x_ref.at[source],
            dst_ref=y_ref.at[source],
            send_sem=send_sems.at[k],
            recv_sem=recv_sems.at[k],
            device_id={axis: source},
            device_id_type=MESH,
        ).wait_recv()


def exchange(x, axis, n, gather, collective_id):
    out_shape = (n,) + x.shape if gather else x.shape
    return pl.pallas_call(
        functools.partial(exchange_kernel, axis, n, gather),
        out_shape=jax.ShapeDtypeStruct(out_shape, x.dtype),
        in_specs=[pl.BlockSpec(memory_space=pltpu.VMEM)],
        out_specs=pl.BlockSpec(memory_space=pltpu.VMEM),
        scratch_shapes=[pltpu.SemaphoreType.DMA((n,)), pltpu.SemaphoreType.DMA((n,))],
        compiler_params=pltpu.CompilerParams(collective_id=collective_id, has_side_effects=True),
    )(x)


def exp_gather_kernel(n, x_ref, y_ref, send_sems, recv_sems):
    chips = n // 2
    width = x_ref.shape[1]
    half = x_ref.shape[0] // 2
    me = lax.axis_index("exp")
    z, core = me // 2, me % 2
    sib = 2 * z + 1 - core
    up = 2 * lax.rem(z + 1, chips) + core
    dn = 2 * lax.rem(z + chips - 1, chips) + core
    far = 2 * lax.rem(z + 2, chips) + core

    def cols(block):
        return pl.ds(pl.multiple_of(block * width, width), width)

    def rows(part):
        return pl.ds(part * half, half)

    barrier = pltpu.get_barrier_semaphore()
    for peer in (sib, up, dn):
        pl.semaphore_signal(barrier, inc=1, device_id={"exp": peer}, device_id_type=MESH)
    pl.semaphore_wait(barrier, 3)

    def remote(src, dst, slot, peer):
        return pltpu.make_async_remote_copy(
            src_ref=src, dst_ref=dst, send_sem=send_sems.at[slot],
            recv_sem=recv_sems.at[slot], device_id={"exp": peer}, device_id_type=MESH,
        )

    own_cols = cols(me)
    first = [
        remote(x_ref, y_ref.at[:, own_cols], 0, up),
        remote(x_ref, y_ref.at[:, own_cols], 1, dn),
        remote(x_ref, y_ref.at[:, own_cols], 2, sib),
    ]
    for copy in first:
        copy.start()
    y_ref[:, own_cols] = x_ref[...]
    remote(x_ref, y_ref.at[:, cols(dn)], 0, dn).wait_recv()
    remote(x_ref, y_ref.at[:, cols(up)], 1, up).wait_recv()
    second = [
        remote(y_ref.at[rows(1), cols(dn)], y_ref.at[rows(1), cols(dn)], 3, up),
        remote(y_ref.at[rows(0), cols(up)], y_ref.at[rows(0), cols(up)], 4, dn),
        remote(y_ref.at[:, cols(dn)], y_ref.at[:, cols(dn)], 5, sib),
        remote(y_ref.at[:, cols(up)], y_ref.at[:, cols(up)], 6, sib),
    ]
    for copy in second:
        copy.start()
    remote(y_ref.at[rows(1), cols(far)], y_ref.at[rows(1), cols(far)], 3, dn).wait_recv()
    remote(y_ref.at[rows(0), cols(far)], y_ref.at[rows(0), cols(far)], 4, up).wait_recv()
    third = remote(y_ref.at[:, cols(far)], y_ref.at[:, cols(far)], 7, sib)
    third.start()
    sib_z = 2 * z + 1 - core
    sib_up = 2 * lax.rem(z + 1, chips) + 1 - core
    sib_dn = 2 * lax.rem(z + chips - 1, chips) + 1 - core
    sib_far = 2 * lax.rem(z + 2, chips) + 1 - core
    remote(x_ref, y_ref.at[:, cols(sib_z)], 2, sib).wait_recv()
    remote(y_ref.at[:, cols(sib_dn)], y_ref.at[:, cols(sib_dn)], 5, sib).wait_recv()
    remote(y_ref.at[:, cols(sib_up)], y_ref.at[:, cols(sib_up)], 6, sib).wait_recv()
    remote(y_ref.at[:, cols(sib_far)], y_ref.at[:, cols(sib_far)], 7, sib).wait_recv()
    for copy in first + second + [third]:
        copy.wait_send()


def exp_gather(x, n, collective_id):
    return pl.pallas_call(
        functools.partial(exp_gather_kernel, n),
        out_shape=jax.ShapeDtypeStruct((x.shape[0], n * x.shape[1]), x.dtype),
        in_specs=[pl.BlockSpec(memory_space=pltpu.VMEM)],
        out_specs=pl.BlockSpec(memory_space=pltpu.VMEM),
        scratch_shapes=[pltpu.SemaphoreType.DMA((8,)), pltpu.SemaphoreType.DMA((8,))],
        compiler_params=pltpu.CompilerParams(collective_id=collective_id, has_side_effects=True),
    )(x)


def ffn_kernel(x_ref, wg_ref, wu_ref, wd_ref, o_ref, g_acc, u_acc):
    step = pl.program_id(0)

    @pl.when(step == 0)
    def _():
        g_acc[...] = jnp.zeros_like(g_acc)
        u_acc[...] = jnp.zeros_like(u_acc)

    x = x_ref[...]
    g_acc[...] += jnp.dot(x, wg_ref[...], preferred_element_type=jnp.float32)
    u_acc[...] += jnp.dot(x, wu_ref[...], preferred_element_type=jnp.float32)

    @pl.when(step == pl.num_programs(0) - 1)
    def _():
        g = g_acc[...]
        act = (g / (1.0 + jnp.exp(-g)) * u_acc[...]).astype(wd_ref.dtype)
        o_ref[...] = jnp.dot(act, wd_ref[...], preferred_element_type=jnp.float32).astype(
            o_ref.dtype
        )


def expert_ffn(x, wg, wu, wd, tk=512):
    rows_n, d = x.shape
    ff = wg.shape[1]
    return pl.pallas_call(
        ffn_kernel,
        out_shape=jax.ShapeDtypeStruct((rows_n, wd.shape[1]), x.dtype),
        grid=(d // tk,),
        in_specs=[
            pl.BlockSpec((rows_n, tk), lambda k: (0, k)),
            pl.BlockSpec((tk, ff), lambda k: (k, 0)),
            pl.BlockSpec((tk, ff), lambda k: (k, 0)),
            pl.BlockSpec((ff, wd.shape[1]), lambda k: (0, 0)),
        ],
        out_specs=pl.BlockSpec((rows_n, wd.shape[1]), lambda k: (0, 0)),
        scratch_shapes=[
            pltpu.VMEM((rows_n, ff), jnp.float32),
            pltpu.VMEM((rows_n, ff), jnp.float32),
        ],
        compiler_params=pltpu.CompilerParams(
            dimension_semantics=("arbitrary",), vmem_limit_bytes=56 * 1024 * 1024
        ),
        cost_estimate=pl.CostEstimate(
            flops=2 * rows_n * d * ff * 2 + 2 * rows_n * ff * wd.shape[1],
            transcendentals=rows_n * ff,
            bytes_accessed=2 * (rows_n * d + 2 * d * ff + ff * wd.shape[1] + rows_n * wd.shape[1]),
        ),
    )(x, wg, wu, wd)


def gather_ffn_kernel(
    n, groups, x_ref, wg_hbm, wu_hbm, wd_hbm, pg_ref, o_ref, pg_out,
    y_ref, wg_v, wu_v, wd_v, g_acc, u_acc, send_sems, recv_sems, w_sems,
    sib_out, sib_buf, acc, stage, half_buf, near_buf, rs_send, rs_recv, pg_send, pg_recv,
):
    chips = n // 2
    width = x_ref.shape[1]
    half = x_ref.shape[0] // 2
    me = lax.axis_index("exp")
    z, core = me // 2, me % 2
    sib = 2 * z + 1 - core
    up = 2 * lax.rem(z + 1, chips) + core
    dn = 2 * lax.rem(z + chips - 1, chips) + core
    far = 2 * lax.rem(z + 2, chips) + core

    weight_copies = [
        pltpu.make_async_copy(src.at[0], dst, w_sems.at[i])
        for i, (src, dst) in enumerate(((wg_hbm, wg_v), (wu_hbm, wu_v), (wd_hbm, wd_v)))
    ]
    for copy in weight_copies:
        copy.start()

    def cols(block):
        return pl.ds(pl.multiple_of(block * width, width), width)

    def rows(part):
        return pl.ds(part * half, half)

    barrier = pltpu.get_barrier_semaphore()
    for peer in (sib, up, dn):
        pl.semaphore_signal(barrier, inc=1, device_id={"exp": peer}, device_id_type=MESH)
    own_group = lax.axis_index("req")
    for k in range(1, groups):
        pl.semaphore_signal(
            barrier, inc=1, device_id={"req": lax.rem(own_group + k, groups)},
            device_id_type=MESH,
        )
    pl.semaphore_wait(barrier, 3 + groups - 1)
    page_copies = []
    for k in range(1, groups):
        peer = lax.rem(own_group + k, groups)
        copy = pltpu.make_async_remote_copy(
            src_ref=pg_ref.at[peer], dst_ref=pg_out.at[own_group], send_sem=pg_send.at[k],
            recv_sem=pg_recv.at[k], device_id={"req": peer}, device_id_type=MESH,
        )
        copy.start()
        page_copies.append(copy)
    pg_out[own_group] = pg_ref[own_group]

    def remote(src, dst, slot, peer):
        return pltpu.make_async_remote_copy(
            src_ref=src, dst_ref=dst, send_sem=send_sems.at[slot],
            recv_sem=recv_sems.at[slot], device_id={"exp": peer}, device_id_type=MESH,
        )

    def consume(block, first=False):
        rows_in = x_ref[...] if first else y_ref[:, cols(block)]
        w_rows = pl.ds(pl.multiple_of(block * width, width), width)
        g_part = jnp.dot(rows_in, wg_v[w_rows, :], preferred_element_type=jnp.float32)
        u_part = jnp.dot(rows_in, wu_v[w_rows, :], preferred_element_type=jnp.float32)
        if first:
            g_acc[...] = g_part
            u_acc[...] = u_part
        else:
            g_acc[...] += g_part
            u_acc[...] += u_part

    own_cols = cols(me)
    sends = [
        remote(x_ref, y_ref.at[:, own_cols], 0, up),
        remote(x_ref, y_ref.at[:, own_cols], 1, dn),
        remote(x_ref, y_ref.at[:, own_cols], 2, sib),
    ]
    for copy in sends:
        copy.start()
    weight_copies[0].wait()
    weight_copies[1].wait()
    consume(me, first=True)
    remote(x_ref, y_ref.at[:, cols(dn)], 0, dn).wait_recv()
    remote(x_ref, y_ref.at[:, cols(up)], 1, up).wait_recv()
    second = [
        remote(y_ref.at[rows(1), cols(dn)], y_ref.at[rows(1), cols(dn)], 3, up),
        remote(y_ref.at[rows(0), cols(up)], y_ref.at[rows(0), cols(up)], 4, dn),
        remote(y_ref.at[:, cols(dn)], y_ref.at[:, cols(dn)], 5, sib),
        remote(y_ref.at[:, cols(up)], y_ref.at[:, cols(up)], 6, sib),
    ]
    for copy in second:
        copy.start()
    sends += second
    consume(dn)
    consume(up)
    remote(y_ref.at[rows(1), cols(far)], y_ref.at[rows(1), cols(far)], 3, dn).wait_recv()
    remote(y_ref.at[rows(0), cols(far)], y_ref.at[rows(0), cols(far)], 4, up).wait_recv()
    third = remote(y_ref.at[:, cols(far)], y_ref.at[:, cols(far)], 7, sib)
    third.start()
    sends.append(third)
    consume(far)
    sib_up = 2 * lax.rem(z + 1, chips) + 1 - core
    sib_dn = 2 * lax.rem(z + chips - 1, chips) + 1 - core
    sib_far = 2 * lax.rem(z + 2, chips) + 1 - core
    for block, slot in ((sib, 2), (sib_dn, 5), (sib_up, 6), (sib_far, 7)):
        remote(y_ref.at[:, cols(block)], y_ref.at[:, cols(block)], slot, sib).wait_recv()
        consume(block)
    g = g_acc[...]
    act = (g / (1.0 + jnp.exp(-g)) * u_acc[...]).astype(wd_v.dtype)
    weight_copies[2].wait()

    def down(block):
        return jnp.dot(act, wd_v[:, cols(block)], preferred_element_type=jnp.float32).astype(
            sib_out.dtype
        )

    def rs_remote(src, dst, slot, peer):
        return pltpu.make_async_remote_copy(
            src_ref=src, dst_ref=dst, send_sem=rs_send.at[slot],
            recv_sem=rs_recv.at[slot], device_id={"exp": peer}, device_id_type=MESH,
        )

    mine = (me, up, dn, far)
    theirs = tuple(block + 1 - 2 * core for block in mine)
    for k in range(4):
        sib_out[k] = down(theirs[k])
        copy = rs_remote(sib_out.at[k], sib_buf.at[k], k, sib)
        copy.start()
        sends.append(copy)
    for k in (3, 1, 2, 0):
        own_part = down(mine[k]).astype(jnp.float32)
        rs_remote(sib_out.at[k], sib_buf.at[k], k, sib).wait_recv()
        acc[k] = own_part + sib_buf[k].astype(jnp.float32)
        if k == 3:
            stage[0] = acc[3].astype(stage.dtype)
            for part, peer, slot in ((0, up, 4), (1, dn, 5)):
                copy = rs_remote(stage.at[0, rows(part)], half_buf.at[part], slot, peer)
                copy.start()
                sends.append(copy)
    rs_remote(stage.at[0, rows(0)], half_buf.at[0], 4, dn).wait_recv()
    acc[1, rows(0)] = acc[1, rows(0)] + half_buf[0].astype(jnp.float32)
    stage[1] = acc[1].astype(stage.dtype)
    copy = rs_remote(stage.at[1], near_buf.at[0], 6, up)
    copy.start()
    sends.append(copy)
    rs_remote(stage.at[0, rows(1)], half_buf.at[1], 5, up).wait_recv()
    acc[2, rows(1)] = acc[2, rows(1)] + half_buf[1].astype(jnp.float32)
    stage[2] = acc[2].astype(stage.dtype)
    copy = rs_remote(stage.at[2], near_buf.at[1], 7, dn)
    copy.start()
    sends.append(copy)
    rs_remote(stage.at[1], near_buf.at[0], 6, dn).wait_recv()
    rs_remote(stage.at[2], near_buf.at[1], 7, up).wait_recv()
    o_ref[...] = (
        acc[0] + near_buf[0].astype(jnp.float32) + near_buf[1].astype(jnp.float32)
    ).astype(o_ref.dtype)
    for copy in sends:
        copy.wait_send()
    for k in range(1, groups):
        page_copies[k - 1].wait_send()
        source = lax.rem(own_group + groups - k, groups)
        pltpu.make_async_remote_copy(
            src_ref=pg_ref.at[source], dst_ref=pg_out.at[source], send_sem=pg_send.at[k],
            recv_sem=pg_recv.at[k], device_id={"req": source}, device_id_type=MESH,
        ).wait_recv()


def gather_ffn(x, w_gate, w_up, w_down, pages, n, groups, collective_id):
    rows_n, width = x.shape
    d, ff = w_gate.shape[1], w_gate.shape[2]
    return pl.pallas_call(
        functools.partial(gather_ffn_kernel, n, groups),
        out_shape=(
            jax.ShapeDtypeStruct((rows_n, w_down.shape[2] // n), x.dtype),
            jax.ShapeDtypeStruct(pages.shape, pages.dtype),
        ),
        in_specs=[pl.BlockSpec(memory_space=pltpu.VMEM)] + [pl.BlockSpec(memory_space=pl.ANY)] * 3
        + [pl.BlockSpec(memory_space=pltpu.VMEM)],
        out_specs=(pl.BlockSpec(memory_space=pltpu.VMEM), pl.BlockSpec(memory_space=pltpu.VMEM)),
        scratch_shapes=[
            pltpu.VMEM((rows_n, n * width), x.dtype),
            pltpu.VMEM((d, ff), w_gate.dtype),
            pltpu.VMEM((d, ff), w_up.dtype),
            pltpu.VMEM((ff, w_down.shape[2]), w_down.dtype),
            pltpu.VMEM((rows_n, ff), jnp.float32),
            pltpu.VMEM((rows_n, ff), jnp.float32),
            pltpu.SemaphoreType.DMA((8,)),
            pltpu.SemaphoreType.DMA((8,)),
            pltpu.SemaphoreType.DMA((3,)),
            pltpu.VMEM((4, rows_n, width), x.dtype),
            pltpu.VMEM((4, rows_n, width), x.dtype),
            pltpu.VMEM((4, rows_n, width), jnp.float32),
            pltpu.VMEM((3, rows_n, width), x.dtype),
            pltpu.VMEM((2, rows_n // 2, width), x.dtype),
            pltpu.VMEM((2, rows_n, width), x.dtype),
            pltpu.SemaphoreType.DMA((8,)),
            pltpu.SemaphoreType.DMA((8,)),
            pltpu.SemaphoreType.DMA((groups,)),
            pltpu.SemaphoreType.DMA((groups,)),
        ],
        compiler_params=pltpu.CompilerParams(
            collective_id=collective_id, has_side_effects=True, vmem_limit_bytes=60 * 1024 * 1024
        ),
    )(x, w_gate, w_up, w_down, pages)

def pick_rows(source, row_index, live_slot):
    taken_rows = jnp.take(source, row_index, axis=0)
    return jnp.where(live_slot[:, None], taken_rows, jnp.zeros((), source.dtype))


def body(
    attention_out,
    residual,
    w_out,
    router_w,
    norm_gain,
    page_pool,
    page_table,
    cache_len,
    came_from,
    routes,
    w_gate,
    w_up,
    w_down,
):
    groups = lax.axis_size("req")
    own_group = lax.axis_index("req")
    row_req = attention_out.shape[0]
    rows_all = came_from.shape[0]
    pages_req = page_table.shape[1]
    page_len = page_pool.shape[1]
    kv_slice = page_pool.shape[2]
    experts = groups // 2
    targets = jnp.arange(groups, dtype=jnp.int32)
    local_ids = jnp.arange(row_req, dtype=jnp.int32)
    dest_of = (
        jnp.zeros((rows_all,), jnp.int32).at[came_from].set(jnp.arange(rows_all, dtype=jnp.int32))
    )
    dest_group = dest_of // row_req
    dest_hot = (
        (dest_group[:, None] == targets[None, :]).astype(jnp.int32).reshape(groups, row_req, groups)
    )
    pair_rank = jnp.sum((jnp.cumsum(dest_hot, axis=1) - dest_hot) * dest_hot, axis=2).reshape(
        rows_all
    )
    own_dest = lax.dynamic_slice_in_dim(dest_group, own_group * row_req, row_req)
    own_rank = lax.dynamic_slice_in_dim(pair_rank, own_group * row_req, row_req)
    chosen_send = (
        (own_dest[None, None, :] == targets[:, None, None])
        & (own_rank[None, None, :] == jnp.arange(MIG_PAIR, dtype=jnp.int32)[None, :, None])
        & (targets[:, None, None] != own_group)
    )
    send_index = jnp.sum(jnp.where(chosen_send, local_ids[None, None, :], 0), axis=2).reshape(-1)
    send_live = jnp.any(chosen_send, axis=2).reshape(-1)
    moved_attn, moved_resid = (
        lax.all_to_all(
            pick_rows(attention_out, send_index, send_live),
            "req",
            split_axis=0,
            concat_axis=0,
            tiled=True,
        ),
        lax.all_to_all(
            pick_rows(residual, send_index, send_live),
            "req",
            split_axis=0,
            concat_axis=0,
            tiled=True,
        ),
    )
    new_source = lax.dynamic_slice_in_dim(came_from, own_group * row_req, row_req)
    source_group = new_source // row_req
    stays_home = source_group == own_group
    arrival = jnp.where(
        stays_home,
        new_source - own_group * row_req,
        row_req + source_group * MIG_PAIR + jnp.take(pair_rank, new_source),
    )
    attn_new = jnp.take(jnp.concatenate([attention_out, moved_attn], axis=0), arrival, axis=0)
    resid_new = jnp.take(jnp.concatenate([residual, moved_resid], axis=0), arrival, axis=0)
    projected = jnp.dot(
        attn_new,
        lax.all_gather(w_out, "req", axis=0, tiled=True),
        preferred_element_type=jnp.float32,
    )
    hidden = resid_new.astype(jnp.float32) + projected
    squares = jnp.sum(hidden * hidden, axis=1)
    scaled = hidden * norm_gain[None, :]
    raw_logits = jnp.dot(scaled, router_w, precision=lax.Precision.HIGHEST)
    stats_t = jnp.concatenate([squares[None, :], raw_logits.T], axis=0)
    stats_t = jnp.pad(stats_t, ((0, 16 - stats_t.shape[0]), (0, 0)))
    n_exp = lax.axis_size("exp")
    row_stats = jnp.sum(exchange(stats_t, "exp", n_exp, True, 0), axis=0)[:9].T
    total_sq = row_stats[:, 0]
    inverse = lax.rsqrt(total_sq / D + EPSILON)
    normed = scaled * inverse[:, None]
    logits = row_stats[:, 1:] * inverse[:, None]
    normed_rows = normed.astype(jnp.bfloat16)
    expert_ids = jnp.arange(experts, dtype=jnp.int32)
    chosen = jnp.sum(
        jnp.where(routes[:, :, None] == expert_ids[None, None, :], logits[:, None, :], 0.0), axis=2
    )
    gate_first = jax.nn.sigmoid(chosen[:, 0] - chosen[:, 1])
    gate_second = jax.nn.sigmoid(chosen[:, 1] - chosen[:, 0])
    flat_routes = routes.reshape(-1)
    expert_hot = (flat_routes[:, None] == expert_ids[None, :]).astype(jnp.int32)
    expert_rank = jnp.sum((jnp.cumsum(expert_hot, axis=0) - expert_hot) * expert_hot, axis=1)
    target_dev = flat_routes + experts * (expert_rank % 2)
    slot_index = expert_rank // 2
    assign_ids = jnp.arange(flat_routes.shape[0], dtype=jnp.int32)
    chosen_slot = (target_dev[None, None, :] == targets[:, None, None]) & (
        slot_index[None, None, :] == jnp.arange(CAP, dtype=jnp.int32)[None, :, None]
    )
    slot_source = jnp.sum(
        jnp.where(chosen_slot, assign_ids[None, None, :] // 2, 0), axis=2
    ).reshape(-1)
    slot_live = jnp.any(chosen_slot, axis=2).reshape(-1)
    outgoing = pick_rows(normed_rows, slot_source, slot_live)
    arrived = exchange(
        outgoing.reshape(groups, -1, outgoing.shape[-1]), "req", groups, False, 1
    ).reshape(outgoing.shape)
    page_rows = jnp.take(page_pool, page_table.reshape(-1), axis=0).reshape(
        row_req, pages_req, page_len, kv_slice
    )
    position = (
        jnp.arange(pages_req, dtype=jnp.int32)[:, None] * page_len
        + jnp.arange(page_len, dtype=jnp.int32)[None, :]
    )
    kept_mask = position[None, :, :] < cache_len[:, None, None]
    page_rows = jnp.where(kept_mask[..., None], page_rows, jnp.zeros((), page_rows.dtype)).reshape(
        row_req, -1
    )
    page_send = pick_rows(page_rows, send_index, send_live)
    partial_value, moved_pages = gather_ffn(
        arrived,
        w_gate,
        w_up,
        w_down,
        page_send.reshape(groups, MIG_PAIR, -1),
        lax.axis_size("exp"),
        groups,
        3,
    )
    moved_pages = moved_pages.reshape(groups * MIG_PAIR, -1)
    summed_value = partial_value
    lookup = target_dev * CAP + slot_index
    new_pages = jnp.take(
        jnp.concatenate([page_rows, moved_pages], axis=0), arrival, axis=0
    ).reshape(row_req, pages_req, page_len, kv_slice)
    returned = exchange(
        summed_value.reshape(groups, -1, summed_value.shape[-1]), "req", groups, False, 2
    ).reshape(summed_value.shape)
    taken_rows = jnp.take(returned, lookup, axis=0).reshape(row_req, 2, -1).astype(jnp.float32)
    expert_part = gate_first[:, None] * taken_rows[:, 0] + gate_second[:, None] * taken_rows[:, 1]
    mixed = hidden + expert_part
    return (mixed, new_pages)


def solution(mesh):
    in_specs = (
        P("req", None),
        P("req", "exp"),
        P("req", "exp"),
        P("exp", None),
        P("exp"),
        P("req", None, "exp"),
        P("req", None),
        P("req"),
        P(),
        P("req", None),
        P("req", None, "exp"),
        P("req", None, "exp"),
        P("req", "exp", None),
    )
    out_specs = (P("req", "exp"), P("req", None, None, "exp"))
    return jax.shard_map(body, mesh=mesh, in_specs=in_specs, out_specs=out_specs, check_vma=False)
```

```python
import jax
import jax.numpy as jnp
from jax import lax
from jax.experimental import pallas as pl
from jax.experimental.pallas import tpu as pltpu
from jax.sharding import PartitionSpec as P
import functools

D = 4096
CAP = 32
MIG_PAIR = 4


EPSILON = 1e-05

MESH = pl.DeviceIdType.MESH


def exchange_kernel(axis, n, gather, x_ref, y_ref, send_sems, recv_sems):
    me = lax.axis_index(axis)
    barrier = pltpu.get_barrier_semaphore()
    for k in range(1, n):
        pl.semaphore_signal(
            barrier, inc=1, device_id={axis: lax.rem(me + k, n)}, device_id_type=MESH
        )
    pl.semaphore_wait(barrier, n - 1)
    copies = []
    for k in range(1, n):
        peer = lax.rem(me + k, n)
        copy = pltpu.make_async_remote_copy(
            src_ref=x_ref if gather else x_ref.at[peer],
            dst_ref=y_ref.at[me],
            send_sem=send_sems.at[k],
            recv_sem=recv_sems.at[k],
            device_id={axis: peer},
            device_id_type=MESH,
        )
        copy.start()
        copies.append(copy)
    if gather:
        y_ref[me] = x_ref[...]
    else:
        y_ref[me] = x_ref[me]
    for k in range(1, n):
        copies[k - 1].wait_send()
        source = lax.rem(me + n - k, n)
        pltpu.make_async_remote_copy(
            src_ref=x_ref if gather else x_ref.at[source],
            dst_ref=y_ref.at[source],
            send_sem=send_sems.at[k],
            recv_sem=recv_sems.at[k],
            device_id={axis: source},
            device_id_type=MESH,
        ).wait_recv()


def exchange(x, axis, n, gather, collective_id):
    out_shape = (n,) + x.shape if gather else x.shape
    return pl.pallas_call(
        functools.partial(exchange_kernel, axis, n, gather),
        out_shape=jax.ShapeDtypeStruct(out_shape, x.dtype),
        in_specs=[pl.BlockSpec(memory_space=pltpu.VMEM)],
        out_specs=pl.BlockSpec(memory_space=pltpu.VMEM),
        scratch_shapes=[pltpu.SemaphoreType.DMA((n,)), pltpu.SemaphoreType.DMA((n,))],
        compiler_params=pltpu.CompilerParams(collective_id=collective_id, has_side_effects=True),
    )(x)


def exp_gather_kernel(n, x_ref, y_ref, send_sems, recv_sems):
    chips = n // 2
    width = x_ref.shape[1]
    half = x_ref.shape[0] // 2
    me = lax.axis_index("exp")
    z, core = me // 2, me % 2
    sib = 2 * z + 1 - core
    up = 2 * lax.rem(z + 1, chips) + core
    dn = 2 * lax.rem(z + chips - 1, chips) + core
    far = 2 * lax.rem(z + 2, chips) + core

    def cols(block):
        return pl.ds(pl.multiple_of(block * width, width), width)

    def rows(part):
        return pl.ds(part * half, half)

    barrier = pltpu.get_barrier_semaphore()
    for peer in (sib, up, dn):
        pl.semaphore_signal(barrier, inc=1, device_id={"exp": peer}, device_id_type=MESH)
    pl.semaphore_wait(barrier, 3)

    def remote(src, dst, slot, peer):
        return pltpu.make_async_remote_copy(
            src_ref=src, dst_ref=dst, send_sem=send_sems.at[slot],
            recv_sem=recv_sems.at[slot], device_id={"exp": peer}, device_id_type=MESH,
        )

    own_cols = cols(me)
    first = [
        remote(x_ref, y_ref.at[:, own_cols], 0, up),
        remote(x_ref, y_ref.at[:, own_cols], 1, dn),
        remote(x_ref, y_ref.at[:, own_cols], 2, sib),
    ]
    for copy in first:
        copy.start()
    y_ref[:, own_cols] = x_ref[...]
    remote(x_ref, y_ref.at[:, cols(dn)], 0, dn).wait_recv()
    remote(x_ref, y_ref.at[:, cols(up)], 1, up).wait_recv()
    second = [
        remote(y_ref.at[rows(1), cols(dn)], y_ref.at[rows(1), cols(dn)], 3, up),
        remote(y_ref.at[rows(0), cols(up)], y_ref.at[rows(0), cols(up)], 4, dn),
        remote(y_ref.at[:, cols(dn)], y_ref.at[:, cols(dn)], 5, sib),
        remote(y_ref.at[:, cols(up)], y_ref.at[:, cols(up)], 6, sib),
    ]
    for copy in second:
        copy.start()
    remote(y_ref.at[rows(1), cols(far)], y_ref.at[rows(1), cols(far)], 3, dn).wait_recv()
    remote(y_ref.at[rows(0), cols(far)], y_ref.at[rows(0), cols(far)], 4, up).wait_recv()
    third = remote(y_ref.at[:, cols(far)], y_ref.at[:, cols(far)], 7, sib)
    third.start()
    sib_z = 2 * z + 1 - core
    sib_up = 2 * lax.rem(z + 1, chips) + 1 - core
    sib_dn = 2 * lax.rem(z + chips - 1, chips) + 1 - core
    sib_far = 2 * lax.rem(z + 2, chips) + 1 - core
    remote(x_ref, y_ref.at[:, cols(sib_z)], 2, sib).wait_recv()
    remote(y_ref.at[:, cols(sib_dn)], y_ref.at[:, cols(sib_dn)], 5, sib).wait_recv()
    remote(y_ref.at[:, cols(sib_up)], y_ref.at[:, cols(sib_up)], 6, sib).wait_recv()
    remote(y_ref.at[:, cols(sib_far)], y_ref.at[:, cols(sib_far)], 7, sib).wait_recv()
    for copy in first + second + [third]:
        copy.wait_send()


def exp_gather(x, n, collective_id):
    return pl.pallas_call(
        functools.partial(exp_gather_kernel, n),
        out_shape=jax.ShapeDtypeStruct((x.shape[0], n * x.shape[1]), x.dtype),
        in_specs=[pl.BlockSpec(memory_space=pltpu.VMEM)],
        out_specs=pl.BlockSpec(memory_space=pltpu.VMEM),
        scratch_shapes=[pltpu.SemaphoreType.DMA((8,)), pltpu.SemaphoreType.DMA((8,))],
        compiler_params=pltpu.CompilerParams(collective_id=collective_id, has_side_effects=True),
    )(x)


def ffn_kernel(x_ref, wg_ref, wu_ref, wd_ref, o_ref, g_acc, u_acc):
    step = pl.program_id(0)

    @pl.when(step == 0)
    def _():
        g_acc[...] = jnp.zeros_like(g_acc)
        u_acc[...] = jnp.zeros_like(u_acc)

    x = x_ref[...]
    g_acc[...] += jnp.dot(x, wg_ref[...], preferred_element_type=jnp.float32)
    u_acc[...] += jnp.dot(x, wu_ref[...], preferred_element_type=jnp.float32)

    @pl.when(step == pl.num_programs(0) - 1)
    def _():
        g = g_acc[...]
        act = (g / (1.0 + jnp.exp(-g)) * u_acc[...]).astype(wd_ref.dtype)
        o_ref[...] = jnp.dot(act, wd_ref[...], preferred_element_type=jnp.float32).astype(
            o_ref.dtype
        )


def expert_ffn(x, wg, wu, wd, tk=512):
    rows_n, d = x.shape
    ff = wg.shape[1]
    return pl.pallas_call(
        ffn_kernel,
        out_shape=jax.ShapeDtypeStruct((rows_n, wd.shape[1]), x.dtype),
        grid=(d // tk,),
        in_specs=[
            pl.BlockSpec((rows_n, tk), lambda k: (0, k)),
            pl.BlockSpec((tk, ff), lambda k: (k, 0)),
            pl.BlockSpec((tk, ff), lambda k: (k, 0)),
            pl.BlockSpec((ff, wd.shape[1]), lambda k: (0, 0)),
        ],
        out_specs=pl.BlockSpec((rows_n, wd.shape[1]), lambda k: (0, 0)),
        scratch_shapes=[
            pltpu.VMEM((rows_n, ff), jnp.float32),
            pltpu.VMEM((rows_n, ff), jnp.float32),
        ],
        compiler_params=pltpu.CompilerParams(
            dimension_semantics=("arbitrary",), vmem_limit_bytes=56 * 1024 * 1024
        ),
        cost_estimate=pl.CostEstimate(
            flops=2 * rows_n * d * ff * 2 + 2 * rows_n * ff * wd.shape[1],
            transcendentals=rows_n * ff,
            bytes_accessed=2 * (rows_n * d + 2 * d * ff + ff * wd.shape[1] + rows_n * wd.shape[1]),
        ),
    )(x, wg, wu, wd)


def gather_ffn_kernel(
    n, groups, x_ref, wg_hbm, wu_hbm, wd_hbm, pg_ref, o_ref, pg_out,
    y_ref, wg_v, wu_v, wd_v, g_acc, u_acc, send_sems, recv_sems, w_sems,
    sib_out, sib_buf, acc, stage, half_buf, near_buf, rs_send, rs_recv, pg_send, pg_recv,
):
    chips = n // 2
    width = x_ref.shape[1]
    half = x_ref.shape[0] // 2
    me = lax.axis_index("exp")
    z, core = me // 2, me % 2
    sib = 2 * z + 1 - core
    up = 2 * lax.rem(z + 1, chips) + core
    dn = 2 * lax.rem(z + chips - 1, chips) + core
    far = 2 * lax.rem(z + 2, chips) + core

    weight_copies = [
        pltpu.make_async_copy(src.at[0], dst, w_sems.at[i])
        for i, (src, dst) in enumerate(((wg_hbm, wg_v), (wu_hbm, wu_v), (wd_hbm, wd_v)))
    ]
    for copy in weight_copies:
        copy.start()

    def cols(block):
        return pl.ds(pl.multiple_of(block * width, width), width)

    def rows(part):
        return pl.ds(part * half, half)

    barrier = pltpu.get_barrier_semaphore()
    for peer in (sib, up, dn):
        pl.semaphore_signal(barrier, inc=1, device_id={"exp": peer}, device_id_type=MESH)
    own_group = lax.axis_index("req")
    for k in range(1, groups):
        pl.semaphore_signal(
            barrier, inc=1, device_id={"req": lax.rem(own_group + k, groups)},
            device_id_type=MESH,
        )
    pl.semaphore_wait(barrier, 3 + groups - 1)
    page_copies = []
    for k in range(1, groups):
        peer = lax.rem(own_group + k, groups)
        copy = pltpu.make_async_remote_copy(
            src_ref=pg_ref.at[peer], dst_ref=pg_out.at[own_group], send_sem=pg_send.at[k],
            recv_sem=pg_recv.at[k], device_id={"req": peer}, device_id_type=MESH,
        )
        copy.start()
        page_copies.append(copy)
    pg_out[own_group] = pg_ref[own_group]

    def remote(src, dst, slot, peer):
        return pltpu.make_async_remote_copy(
            src_ref=src, dst_ref=dst, send_sem=send_sems.at[slot],
            recv_sem=recv_sems.at[slot], device_id={"exp": peer}, device_id_type=MESH,
        )

    def consume(block, first=False):
        rows_in = x_ref[...] if first else y_ref[:, cols(block)]
        w_rows = pl.ds(pl.multiple_of(block * width, width), width)
        g_part = jnp.dot(rows_in, wg_v[w_rows, :], preferred_element_type=jnp.float32)
        u_part = jnp.dot(rows_in, wu_v[w_rows, :], preferred_element_type=jnp.float32)
        if first:
            g_acc[...] = g_part
            u_acc[...] = u_part
        else:
            g_acc[...] += g_part
            u_acc[...] += u_part

    own_cols = cols(me)
    sends = [
        remote(x_ref, y_ref.at[:, own_cols], 0, up),
        remote(x_ref, y_ref.at[:, own_cols], 1, dn),
        remote(x_ref, y_ref.at[:, own_cols], 2, sib),
    ]
    for copy in sends:
        copy.start()
    weight_copies[0].wait()
    weight_copies[1].wait()
    consume(me, first=True)
    remote(x_ref, y_ref.at[:, cols(dn)], 0, dn).wait_recv()
    remote(x_ref, y_ref.at[:, cols(up)], 1, up).wait_recv()
    second = [
        remote(y_ref.at[rows(1), cols(dn)], y_ref.at[rows(1), cols(dn)], 3, up),
        remote(y_ref.at[rows(0), cols(up)], y_ref.at[rows(0), cols(up)], 4, dn),
        remote(y_ref.at[:, cols(dn)], y_ref.at[:, cols(dn)], 5, sib),
        remote(y_ref.at[:, cols(up)], y_ref.at[:, cols(up)], 6, sib),
    ]
    for copy in second:
        copy.start()
    sends += second
    consume(dn)
    consume(up)
    remote(y_ref.at[rows(1), cols(far)], y_ref.at[rows(1), cols(far)], 3, dn).wait_recv()
    remote(y_ref.at[rows(0), cols(far)], y_ref.at[rows(0), cols(far)], 4, up).wait_recv()
    third = remote(y_ref.at[:, cols(far)], y_ref.at[:, cols(far)], 7, sib)
    third.start()
    sends.append(third)
    consume(far)
    sib_up = 2 * lax.rem(z + 1, chips) + 1 - core
    sib_dn = 2 * lax.rem(z + chips - 1, chips) + 1 - core
    sib_far = 2 * lax.rem(z + 2, chips) + 1 - core
    for block, slot in ((sib, 2), (sib_dn, 5), (sib_up, 6), (sib_far, 7)):
        remote(y_ref.at[:, cols(block)], y_ref.at[:, cols(block)], slot, sib).wait_recv()
        consume(block)
    g = g_acc[...]
    act = (g / (1.0 + jnp.exp(-g)) * u_acc[...]).astype(wd_v.dtype)
    weight_copies[2].wait()

    def down(block):
        return jnp.dot(act, wd_v[:, cols(block)], preferred_element_type=jnp.float32).astype(
            sib_out.dtype
        )

    def rs_remote(src, dst, slot, peer):
        return pltpu.make_async_remote_copy(
            src_ref=src, dst_ref=dst, send_sem=rs_send.at[slot],
            recv_sem=rs_recv.at[slot], device_id={"exp": peer}, device_id_type=MESH,
        )

    mine = (me, up, dn, far)
    theirs = tuple(block + 1 - 2 * core for block in mine)
    for k in range(4):
        sib_out[k] = down(theirs[k])
        copy = rs_remote(sib_out.at[k], sib_buf.at[k], k, sib)
        copy.start()
        sends.append(copy)
    for k in (3, 1, 2, 0):
        own_part = down(mine[k]).astype(jnp.float32)
        rs_remote(sib_out.at[k], sib_buf.at[k], k, sib).wait_recv()
        acc[k] = own_part + sib_buf[k].astype(jnp.float32)
        if k == 3:
            stage[0] = acc[3].astype(stage.dtype)
            for part, peer, slot in ((0, up, 4), (1, dn, 5)):
                copy = rs_remote(stage.at[0, rows(part)], half_buf.at[part], slot, peer)
                copy.start()
                sends.append(copy)
    rs_remote(stage.at[0, rows(0)], half_buf.at[0], 4, dn).wait_recv()
    acc[1, rows(0)] = acc[1, rows(0)] + half_buf[0].astype(jnp.float32)
    stage[1] = acc[1].astype(stage.dtype)
    copy = rs_remote(stage.at[1], near_buf.at[0], 6, up)
    copy.start()
    sends.append(copy)
    rs_remote(stage.at[0, rows(1)], half_buf.at[1], 5, up).wait_recv()
    acc[2, rows(1)] = acc[2, rows(1)] + half_buf[1].astype(jnp.float32)
    stage[2] = acc[2].astype(stage.dtype)
    copy = rs_remote(stage.at[2], near_buf.at[1], 7, dn)
    copy.start()
    sends.append(copy)
    rs_remote(stage.at[1], near_buf.at[0], 6, dn).wait_recv()
    rs_remote(stage.at[2], near_buf.at[1], 7, up).wait_recv()
    o_ref[...] = (
        acc[0] + near_buf[0].astype(jnp.float32) + near_buf[1].astype(jnp.float32)
    ).astype(o_ref.dtype)
    for copy in sends:
        copy.wait_send()
    for k in range(1, groups):
        page_copies[k - 1].wait_send()
        source = lax.rem(own_group + groups - k, groups)
        pltpu.make_async_remote_copy(
            src_ref=pg_ref.at[source], dst_ref=pg_out.at[source], send_sem=pg_send.at[k],
            recv_sem=pg_recv.at[k], device_id={"req": source}, device_id_type=MESH,
        ).wait_recv()


def gather_ffn(x, w_gate, w_up, w_down, pages, n, groups, collective_id):
    rows_n, width = x.shape
    d, ff = w_gate.shape[1], w_gate.shape[2]
    return pl.pallas_call(
        functools.partial(gather_ffn_kernel, n, groups),
        out_shape=(
            jax.ShapeDtypeStruct((rows_n, w_down.shape[2] // n), x.dtype),
            jax.ShapeDtypeStruct(pages.shape, pages.dtype),
        ),
        in_specs=[pl.BlockSpec(memory_space=pltpu.VMEM)] + [pl.BlockSpec(memory_space=pl.ANY)] * 3
        + [pl.BlockSpec(memory_space=pltpu.VMEM)],
        out_specs=(pl.BlockSpec(memory_space=pltpu.VMEM), pl.BlockSpec(memory_space=pltpu.VMEM)),
        scratch_shapes=[
            pltpu.VMEM((rows_n, n * width), x.dtype),
            pltpu.VMEM((d, ff), w_gate.dtype),
            pltpu.VMEM((d, ff), w_up.dtype),
            pltpu.VMEM((ff, w_down.shape[2]), w_down.dtype),
            pltpu.VMEM((rows_n, ff), jnp.float32),
            pltpu.VMEM((rows_n, ff), jnp.float32),
            pltpu.SemaphoreType.DMA((8,)),
            pltpu.SemaphoreType.DMA((8,)),
            pltpu.SemaphoreType.DMA((3,)),
            pltpu.VMEM((4, rows_n, width), x.dtype),
            pltpu.VMEM((4, rows_n, width), x.dtype),
            pltpu.VMEM((4, rows_n, width), jnp.float32),
            pltpu.VMEM((3, rows_n, width), x.dtype),
            pltpu.VMEM((2, rows_n // 2, width), x.dtype),
            pltpu.VMEM((2, rows_n, width), x.dtype),
            pltpu.SemaphoreType.DMA((8,)),
            pltpu.SemaphoreType.DMA((8,)),
            pltpu.SemaphoreType.DMA((groups,)),
            pltpu.SemaphoreType.DMA((groups,)),
        ],
        compiler_params=pltpu.CompilerParams(
            collective_id=collective_id, has_side_effects=True, vmem_limit_bytes=60 * 1024 * 1024
        ),
    )(x, w_gate, w_up, w_down, pages)

def pick_rows(source, row_index, live_slot):
    taken_rows = jnp.take(source, row_index, axis=0)
    return jnp.where(live_slot[:, None], taken_rows, jnp.zeros((), source.dtype))


def body(
    attention_out,
    residual,
    w_out,
    router_w,
    norm_gain,
    page_pool,
    page_table,
    cache_len,
    came_from,
    routes,
    w_gate,
    w_up,
    w_down,
):
    groups = lax.axis_size("req")
    own_group = lax.axis_index("req")
    row_req = attention_out.shape[0]
    rows_all = came_from.shape[0]
    pages_req = page_table.shape[1]
    page_len = page_pool.shape[1]
    kv_slice = page_pool.shape[2]
    experts = groups // 2
    targets = jnp.arange(groups, dtype=jnp.int32)
    local_ids = jnp.arange(row_req, dtype=jnp.int32)
    dest_of = (
        jnp.zeros((rows_all,), jnp.int32).at[came_from].set(jnp.arange(rows_all, dtype=jnp.int32))
    )
    dest_group = dest_of // row_req
    dest_hot = (
        (dest_group[:, None] == targets[None, :]).astype(jnp.int32).reshape(groups, row_req, groups)
    )
    pair_rank = jnp.sum((jnp.cumsum(dest_hot, axis=1) - dest_hot) * dest_hot, axis=2).reshape(
        rows_all
    )
    own_dest = lax.dynamic_slice_in_dim(dest_group, own_group * row_req, row_req)
    own_rank = lax.dynamic_slice_in_dim(pair_rank, own_group * row_req, row_req)
    chosen_send = (
        (own_dest[None, None, :] == targets[:, None, None])
        & (own_rank[None, None, :] == jnp.arange(MIG_PAIR, dtype=jnp.int32)[None, :, None])
        & (targets[:, None, None] != own_group)
    )
    send_index = jnp.sum(jnp.where(chosen_send, local_ids[None, None, :], 0), axis=2).reshape(-1)
    send_live = jnp.any(chosen_send, axis=2).reshape(-1)
    attn_send, page_pool = lax.optimization_barrier(
        (pick_rows(attention_out, send_index, send_live), page_pool)
    )
    moved_attn, moved_resid = (
        lax.all_to_all(
            attn_send,
            "req",
            split_axis=0,
            concat_axis=0,
            tiled=True,
        ),
        lax.all_to_all(
            pick_rows(residual, send_index, send_live),
            "req",
            split_axis=0,
            concat_axis=0,
            tiled=True,
        ),
    )
    new_source = lax.dynamic_slice_in_dim(came_from, own_group * row_req, row_req)
    source_group = new_source // row_req
    stays_home = source_group == own_group
    arrival = jnp.where(
        stays_home,
        new_source - own_group * row_req,
        row_req + source_group * MIG_PAIR + jnp.take(pair_rank, new_source),
    )
    attn_new = jnp.take(jnp.concatenate([attention_out, moved_attn], axis=0), arrival, axis=0)
    resid_new = jnp.take(jnp.concatenate([residual, moved_resid], axis=0), arrival, axis=0)
    projected = jnp.dot(
        attn_new,
        lax.all_gather(w_out, "req", axis=0, tiled=True),
        preferred_element_type=jnp.float32,
    )
    hidden = resid_new.astype(jnp.float32) + projected
    squares = jnp.sum(hidden * hidden, axis=1)
    scaled = hidden * norm_gain[None, :]
    raw_logits = jnp.dot(scaled, router_w, precision=lax.Precision.HIGHEST)
    stats_t = jnp.concatenate([squares[None, :], raw_logits.T], axis=0)
    stats_t = jnp.pad(stats_t, ((0, 16 - stats_t.shape[0]), (0, 0)))
    n_exp = lax.axis_size("exp")
    row_stats = jnp.sum(exchange(stats_t, "exp", n_exp, True, 0), axis=0)[:9].T
    total_sq = row_stats[:, 0]
    inverse = lax.rsqrt(total_sq / D + EPSILON)
    normed = scaled * inverse[:, None]
    logits = row_stats[:, 1:] * inverse[:, None]
    normed_rows = normed.astype(jnp.bfloat16)
    expert_ids = jnp.arange(experts, dtype=jnp.int32)
    chosen = jnp.sum(
        jnp.where(routes[:, :, None] == expert_ids[None, None, :], logits[:, None, :], 0.0), axis=2
    )
    gate_first = jax.nn.sigmoid(chosen[:, 0] - chosen[:, 1])
    gate_second = jax.nn.sigmoid(chosen[:, 1] - chosen[:, 0])
    flat_routes = routes.reshape(-1)
    expert_hot = (flat_routes[:, None] == expert_ids[None, :]).astype(jnp.int32)
    expert_rank = jnp.sum((jnp.cumsum(expert_hot, axis=0) - expert_hot) * expert_hot, axis=1)
    target_dev = flat_routes + experts * (expert_rank % 2)
    slot_index = expert_rank // 2
    assign_ids = jnp.arange(flat_routes.shape[0], dtype=jnp.int32)
    chosen_slot = (target_dev[None, None, :] == targets[:, None, None]) & (
        slot_index[None, None, :] == jnp.arange(CAP, dtype=jnp.int32)[None, :, None]
    )
    slot_source = jnp.sum(
        jnp.where(chosen_slot, assign_ids[None, None, :] // 2, 0), axis=2
    ).reshape(-1)
    slot_live = jnp.any(chosen_slot, axis=2).reshape(-1)
    outgoing = pick_rows(normed_rows, slot_source, slot_live)
    arrived = exchange(
        outgoing.reshape(groups, -1, outgoing.shape[-1]), "req", groups, False, 1
    ).reshape(outgoing.shape)
    page_rows = jnp.take(page_pool, page_table.reshape(-1), axis=0).reshape(
        row_req, pages_req, page_len, kv_slice
    )
    position = (
        jnp.arange(pages_req, dtype=jnp.int32)[:, None] * page_len
        + jnp.arange(page_len, dtype=jnp.int32)[None, :]
    )
    kept_mask = position[None, :, :] < cache_len[:, None, None]
    page_rows = jnp.where(kept_mask[..., None], page_rows, jnp.zeros((), page_rows.dtype)).reshape(
        row_req, -1
    )
    page_send = pick_rows(page_rows, send_index, send_live)
    partial_value, moved_pages = gather_ffn(
        arrived,
        w_gate,
        w_up,
        w_down,
        page_send.reshape(groups, MIG_PAIR, -1),
        lax.axis_size("exp"),
        groups,
        3,
    )
    moved_pages = moved_pages.reshape(groups * MIG_PAIR, -1)
    summed_value = partial_value
    lookup = target_dev * CAP + slot_index
    new_pages = jnp.take(
        jnp.concatenate([page_rows, moved_pages], axis=0), arrival, axis=0
    ).reshape(row_req, pages_req, page_len, kv_slice)
    returned = exchange(
        summed_value.reshape(groups, -1, summed_value.shape[-1]), "req", groups, False, 2
    ).reshape(summed_value.shape)
    taken_rows = jnp.take(returned, lookup, axis=0).reshape(row_req, 2, -1).astype(jnp.float32)
    expert_part = gate_first[:, None] * taken_rows[:, 0] + gate_second[:, None] * taken_rows[:, 1]
    mixed = hidden + expert_part
    return (mixed, new_pages)


def solution(mesh):
    in_specs = (
        P("req", None),
        P("req", "exp"),
        P("req", "exp"),
        P("exp", None),
        P("exp"),
        P("req", None, "exp"),
        P("req", None),
        P("req"),
        P(),
        P("req", None),
        P("req", None, "exp"),
        P("req", None, "exp"),
        P("req", "exp", None),
    )
    out_specs = (P("req", "exp"), P("req", None, None, "exp"))
    return jax.shard_map(body, mesh=mesh, in_specs=in_specs, out_specs=out_specs, check_vma=False)
```

```python
import jax
import jax.numpy as jnp
from jax import lax
from jax.experimental import pallas as pl
from jax.experimental.pallas import tpu as pltpu
from jax.sharding import PartitionSpec as P
import functools

D = 4096
CAP = 32
MIG_PAIR = 4


EPSILON = 1e-05

MESH = pl.DeviceIdType.MESH


def exchange_kernel(axis, n, gather, x_ref, y_ref, send_sems, recv_sems):
    me = lax.axis_index(axis)
    barrier = pltpu.get_barrier_semaphore()
    for k in range(1, n):
        pl.semaphore_signal(
            barrier, inc=1, device_id={axis: lax.rem(me + k, n)}, device_id_type=MESH
        )
    pl.semaphore_wait(barrier, n - 1)
    copies = []
    for k in range(1, n):
        peer = lax.rem(me + k, n)
        copy = pltpu.make_async_remote_copy(
            src_ref=x_ref if gather else x_ref.at[peer],
            dst_ref=y_ref.at[me],
            send_sem=send_sems.at[k],
            recv_sem=recv_sems.at[k],
            device_id={axis: peer},
            device_id_type=MESH,
        )
        copy.start()
        copies.append(copy)
    if gather:
        y_ref[me] = x_ref[...]
    else:
        y_ref[me] = x_ref[me]
    for k in range(1, n):
        copies[k - 1].wait_send()
        source = lax.rem(me + n - k, n)
        pltpu.make_async_remote_copy(
            src_ref=x_ref if gather else x_ref.at[source],
            dst_ref=y_ref.at[source],
            send_sem=send_sems.at[k],
            recv_sem=recv_sems.at[k],
            device_id={axis: source},
            device_id_type=MESH,
        ).wait_recv()


def exchange(x, axis, n, gather, collective_id):
    out_shape = (n,) + x.shape if gather else x.shape
    return pl.pallas_call(
        functools.partial(exchange_kernel, axis, n, gather),
        out_shape=jax.ShapeDtypeStruct(out_shape, x.dtype),
        in_specs=[pl.BlockSpec(memory_space=pltpu.VMEM)],
        out_specs=pl.BlockSpec(memory_space=pltpu.VMEM),
        scratch_shapes=[pltpu.SemaphoreType.DMA((n,)), pltpu.SemaphoreType.DMA((n,))],
        compiler_params=pltpu.CompilerParams(collective_id=collective_id, has_side_effects=True),
    )(x)


def exp_gather_kernel(n, x_ref, y_ref, send_sems, recv_sems):
    chips = n // 2
    width = x_ref.shape[1]
    half = x_ref.shape[0] // 2
    me = lax.axis_index("exp")
    z, core = me // 2, me % 2
    sib = 2 * z + 1 - core
    up = 2 * lax.rem(z + 1, chips) + core
    dn = 2 * lax.rem(z + chips - 1, chips) + core
    far = 2 * lax.rem(z + 2, chips) + core

    def cols(block):
        return pl.ds(pl.multiple_of(block * width, width), width)

    def rows(part):
        return pl.ds(part * half, half)

    barrier = pltpu.get_barrier_semaphore()
    for peer in (sib, up, dn):
        pl.semaphore_signal(barrier, inc=1, device_id={"exp": peer}, device_id_type=MESH)
    pl.semaphore_wait(barrier, 3)

    def remote(src, dst, slot, peer):
        return pltpu.make_async_remote_copy(
            src_ref=src, dst_ref=dst, send_sem=send_sems.at[slot],
            recv_sem=recv_sems.at[slot], device_id={"exp": peer}, device_id_type=MESH,
        )

    own_cols = cols(me)
    first = [
        remote(x_ref, y_ref.at[:, own_cols], 0, up),
        remote(x_ref, y_ref.at[:, own_cols], 1, dn),
        remote(x_ref, y_ref.at[:, own_cols], 2, sib),
    ]
    for copy in first:
        copy.start()
    y_ref[:, own_cols] = x_ref[...]
    remote(x_ref, y_ref.at[:, cols(dn)], 0, dn).wait_recv()
    remote(x_ref, y_ref.at[:, cols(up)], 1, up).wait_recv()
    second = [
        remote(y_ref.at[rows(1), cols(dn)], y_ref.at[rows(1), cols(dn)], 3, up),
        remote(y_ref.at[rows(0), cols(up)], y_ref.at[rows(0), cols(up)], 4, dn),
        remote(y_ref.at[:, cols(dn)], y_ref.at[:, cols(dn)], 5, sib),
        remote(y_ref.at[:, cols(up)], y_ref.at[:, cols(up)], 6, sib),
    ]
    for copy in second:
        copy.start()
    remote(y_ref.at[rows(1), cols(far)], y_ref.at[rows(1), cols(far)], 3, dn).wait_recv()
    remote(y_ref.at[rows(0), cols(far)], y_ref.at[rows(0), cols(far)], 4, up).wait_recv()
    third = remote(y_ref.at[:, cols(far)], y_ref.at[:, cols(far)], 7, sib)
    third.start()
    sib_z = 2 * z + 1 - core
    sib_up = 2 * lax.rem(z + 1, chips) + 1 - core
    sib_dn = 2 * lax.rem(z + chips - 1, chips) + 1 - core
    sib_far = 2 * lax.rem(z + 2, chips) + 1 - core
    remote(x_ref, y_ref.at[:, cols(sib_z)], 2, sib).wait_recv()
    remote(y_ref.at[:, cols(sib_dn)], y_ref.at[:, cols(sib_dn)], 5, sib).wait_recv()
    remote(y_ref.at[:, cols(sib_up)], y_ref.at[:, cols(sib_up)], 6, sib).wait_recv()
    remote(y_ref.at[:, cols(sib_far)], y_ref.at[:, cols(sib_far)], 7, sib).wait_recv()
    for copy in first + second + [third]:
        copy.wait_send()


def exp_gather(x, n, collective_id):
    return pl.pallas_call(
        functools.partial(exp_gather_kernel, n),
        out_shape=jax.ShapeDtypeStruct((x.shape[0], n * x.shape[1]), x.dtype),
        in_specs=[pl.BlockSpec(memory_space=pltpu.VMEM)],
        out_specs=pl.BlockSpec(memory_space=pltpu.VMEM),
        scratch_shapes=[pltpu.SemaphoreType.DMA((8,)), pltpu.SemaphoreType.DMA((8,))],
        compiler_params=pltpu.CompilerParams(collective_id=collective_id, has_side_effects=True),
    )(x)


def ffn_kernel(x_ref, wg_ref, wu_ref, wd_ref, o_ref, g_acc, u_acc):
    step = pl.program_id(0)

    @pl.when(step == 0)
    def _():
        g_acc[...] = jnp.zeros_like(g_acc)
        u_acc[...] = jnp.zeros_like(u_acc)

    x = x_ref[...]
    g_acc[...] += jnp.dot(x, wg_ref[...], preferred_element_type=jnp.float32)
    u_acc[...] += jnp.dot(x, wu_ref[...], preferred_element_type=jnp.float32)

    @pl.when(step == pl.num_programs(0) - 1)
    def _():
        g = g_acc[...]
        act = (g / (1.0 + jnp.exp(-g)) * u_acc[...]).astype(wd_ref.dtype)
        o_ref[...] = jnp.dot(act, wd_ref[...], preferred_element_type=jnp.float32).astype(
            o_ref.dtype
        )


def expert_ffn(x, wg, wu, wd, tk=512):
    rows_n, d = x.shape
    ff = wg.shape[1]
    return pl.pallas_call(
        ffn_kernel,
        out_shape=jax.ShapeDtypeStruct((rows_n, wd.shape[1]), x.dtype),
        grid=(d // tk,),
        in_specs=[
            pl.BlockSpec((rows_n, tk), lambda k: (0, k)),
            pl.BlockSpec((tk, ff), lambda k: (k, 0)),
            pl.BlockSpec((tk, ff), lambda k: (k, 0)),
            pl.BlockSpec((ff, wd.shape[1]), lambda k: (0, 0)),
        ],
        out_specs=pl.BlockSpec((rows_n, wd.shape[1]), lambda k: (0, 0)),
        scratch_shapes=[
            pltpu.VMEM((rows_n, ff), jnp.float32),
            pltpu.VMEM((rows_n, ff), jnp.float32),
        ],
        compiler_params=pltpu.CompilerParams(
            dimension_semantics=("arbitrary",), vmem_limit_bytes=56 * 1024 * 1024
        ),
        cost_estimate=pl.CostEstimate(
            flops=2 * rows_n * d * ff * 2 + 2 * rows_n * ff * wd.shape[1],
            transcendentals=rows_n * ff,
            bytes_accessed=2 * (rows_n * d + 2 * d * ff + ff * wd.shape[1] + rows_n * wd.shape[1]),
        ),
    )(x, wg, wu, wd)


def gather_ffn_kernel(
    n, groups, x_ref, wg_hbm, wu_hbm, wd_hbm, pg_ref, o_ref, pg_out,
    y_ref, wg_v, wu_v, wd_v, g_acc, u_acc, send_sems, recv_sems, w_sems,
    sib_out, sib_buf, acc, stage, half_buf, near_buf, rs_send, rs_recv, pg_send, pg_recv,
):
    chips = n // 2
    width = x_ref.shape[1]
    half = x_ref.shape[0] // 2
    me = lax.axis_index("exp")
    z, core = me // 2, me % 2
    sib = 2 * z + 1 - core
    up = 2 * lax.rem(z + 1, chips) + core
    dn = 2 * lax.rem(z + chips - 1, chips) + core
    far = 2 * lax.rem(z + 2, chips) + core

    weight_copies = [
        pltpu.make_async_copy(src.at[0], dst, w_sems.at[i])
        for i, (src, dst) in enumerate(((wg_hbm, wg_v), (wu_hbm, wu_v), (wd_hbm, wd_v)))
    ]
    for copy in weight_copies:
        copy.start()

    def cols(block):
        return pl.ds(pl.multiple_of(block * width, width), width)

    def rows(part):
        return pl.ds(part * half, half)

    barrier = pltpu.get_barrier_semaphore()
    for peer in (sib, up, dn):
        pl.semaphore_signal(barrier, inc=1, device_id={"exp": peer}, device_id_type=MESH)
    own_group = lax.axis_index("req")
    for k in range(1, groups):
        pl.semaphore_signal(
            barrier, inc=1, device_id={"req": lax.rem(own_group + k, groups)},
            device_id_type=MESH,
        )
    pl.semaphore_wait(barrier, 3 + groups - 1)
    page_copies = []
    for k in range(1, groups):
        peer = lax.rem(own_group + k, groups)
        copy = pltpu.make_async_remote_copy(
            src_ref=pg_ref.at[peer], dst_ref=pg_out.at[own_group], send_sem=pg_send.at[k],
            recv_sem=pg_recv.at[k], device_id={"req": peer}, device_id_type=MESH,
        )
        copy.start()
        page_copies.append(copy)
    pg_out[own_group] = pg_ref[own_group]

    def remote(src, dst, slot, peer):
        return pltpu.make_async_remote_copy(
            src_ref=src, dst_ref=dst, send_sem=send_sems.at[slot],
            recv_sem=recv_sems.at[slot], device_id={"exp": peer}, device_id_type=MESH,
        )

    def consume(block, first=False):
        rows_in = x_ref[...] if first else y_ref[:, cols(block)]
        w_rows = pl.ds(pl.multiple_of(block * width, width), width)
        g_part = jnp.dot(rows_in, wg_v[w_rows, :], preferred_element_type=jnp.float32)
        u_part = jnp.dot(rows_in, wu_v[w_rows, :], preferred_element_type=jnp.float32)
        if first:
            g_acc[...] = g_part
            u_acc[...] = u_part
        else:
            g_acc[...] += g_part
            u_acc[...] += u_part

    own_cols = cols(me)
    sends = [
        remote(x_ref, y_ref.at[:, own_cols], 0, up),
        remote(x_ref, y_ref.at[:, own_cols], 1, dn),
        remote(x_ref, y_ref.at[:, own_cols], 2, sib),
    ]
    for copy in sends:
        copy.start()
    weight_copies[0].wait()
    weight_copies[1].wait()
    consume(me, first=True)
    remote(x_ref, y_ref.at[:, cols(dn)], 0, dn).wait_recv()
    remote(x_ref, y_ref.at[:, cols(up)], 1, up).wait_recv()
    second = [
        remote(y_ref.at[rows(1), cols(dn)], y_ref.at[rows(1), cols(dn)], 3, up),
        remote(y_ref.at[rows(0), cols(up)], y_ref.at[rows(0), cols(up)], 4, dn),
        remote(y_ref.at[:, cols(dn)], y_ref.at[:, cols(dn)], 5, sib),
        remote(y_ref.at[:, cols(up)], y_ref.at[:, cols(up)], 6, sib),
    ]
    for copy in second:
        copy.start()
    sends += second
    consume(dn)
    consume(up)
    remote(y_ref.at[rows(1), cols(far)], y_ref.at[rows(1), cols(far)], 3, dn).wait_recv()
    remote(y_ref.at[rows(0), cols(far)], y_ref.at[rows(0), cols(far)], 4, up).wait_recv()
    third = remote(y_ref.at[:, cols(far)], y_ref.at[:, cols(far)], 7, sib)
    third.start()
    sends.append(third)
    consume(far)
    sib_up = 2 * lax.rem(z + 1, chips) + 1 - core
    sib_dn = 2 * lax.rem(z + chips - 1, chips) + 1 - core
    sib_far = 2 * lax.rem(z + 2, chips) + 1 - core
    for block, slot in ((sib, 2), (sib_dn, 5), (sib_up, 6), (sib_far, 7)):
        remote(y_ref.at[:, cols(block)], y_ref.at[:, cols(block)], slot, sib).wait_recv()
        consume(block)
    g = g_acc[...]
    act = (g / (1.0 + jnp.exp(-g)) * u_acc[...]).astype(wd_v.dtype)
    weight_copies[2].wait()

    def down(block):
        return jnp.dot(act, wd_v[:, cols(block)], preferred_element_type=jnp.float32).astype(
            sib_out.dtype
        )

    def rs_remote(src, dst, slot, peer):
        return pltpu.make_async_remote_copy(
            src_ref=src, dst_ref=dst, send_sem=rs_send.at[slot],
            recv_sem=rs_recv.at[slot], device_id={"exp": peer}, device_id_type=MESH,
        )

    mine = (me, up, dn, far)
    theirs = tuple(block + 1 - 2 * core for block in mine)
    for k in range(4):
        sib_out[k] = down(theirs[k])
        copy = rs_remote(sib_out.at[k], sib_buf.at[k], k, sib)
        copy.start()
        sends.append(copy)
    for k in (3, 1, 2, 0):
        own_part = down(mine[k]).astype(jnp.float32)
        rs_remote(sib_out.at[k], sib_buf.at[k], k, sib).wait_recv()
        acc[k] = own_part + sib_buf[k].astype(jnp.float32)
        if k == 3:
            stage[0] = acc[3].astype(stage.dtype)
            for part, peer, slot in ((0, up, 4), (1, dn, 5)):
                copy = rs_remote(stage.at[0, rows(part)], half_buf.at[part], slot, peer)
                copy.start()
                sends.append(copy)
    rs_remote(stage.at[0, rows(0)], half_buf.at[0], 4, dn).wait_recv()
    acc[1, rows(0)] = acc[1, rows(0)] + half_buf[0].astype(jnp.float32)
    stage[1] = acc[1].astype(stage.dtype)
    copy = rs_remote(stage.at[1], near_buf.at[0], 6, up)
    copy.start()
    sends.append(copy)
    rs_remote(stage.at[0, rows(1)], half_buf.at[1], 5, up).wait_recv()
    acc[2, rows(1)] = acc[2, rows(1)] + half_buf[1].astype(jnp.float32)
    stage[2] = acc[2].astype(stage.dtype)
    copy = rs_remote(stage.at[2], near_buf.at[1], 7, dn)
    copy.start()
    sends.append(copy)
    rs_remote(stage.at[1], near_buf.at[0], 6, dn).wait_recv()
    rs_remote(stage.at[2], near_buf.at[1], 7, up).wait_recv()
    o_ref[...] = (
        acc[0] + near_buf[0].astype(jnp.float32) + near_buf[1].astype(jnp.float32)
    ).astype(o_ref.dtype)
    for copy in sends:
        copy.wait_send()
    for k in range(1, groups):
        page_copies[k - 1].wait_send()
        source = lax.rem(own_group + groups - k, groups)
        pltpu.make_async_remote_copy(
            src_ref=pg_ref.at[source], dst_ref=pg_out.at[source], send_sem=pg_send.at[k],
            recv_sem=pg_recv.at[k], device_id={"req": source}, device_id_type=MESH,
        ).wait_recv()


def gather_ffn(x, w_gate, w_up, w_down, pages, n, groups, collective_id):
    rows_n, width = x.shape
    d, ff = w_gate.shape[1], w_gate.shape[2]
    return pl.pallas_call(
        functools.partial(gather_ffn_kernel, n, groups),
        out_shape=(
            jax.ShapeDtypeStruct((rows_n, w_down.shape[2] // n), x.dtype),
            jax.ShapeDtypeStruct(pages.shape, pages.dtype),
        ),
        in_specs=[pl.BlockSpec(memory_space=pltpu.VMEM)] + [pl.BlockSpec(memory_space=pl.ANY)] * 3
        + [pl.BlockSpec(memory_space=pltpu.VMEM)],
        out_specs=(pl.BlockSpec(memory_space=pltpu.VMEM), pl.BlockSpec(memory_space=pltpu.VMEM)),
        scratch_shapes=[
            pltpu.VMEM((rows_n, n * width), x.dtype),
            pltpu.VMEM((d, ff), w_gate.dtype),
            pltpu.VMEM((d, ff), w_up.dtype),
            pltpu.VMEM((ff, w_down.shape[2]), w_down.dtype),
            pltpu.VMEM((rows_n, ff), jnp.float32),
            pltpu.VMEM((rows_n, ff), jnp.float32),
            pltpu.SemaphoreType.DMA((8,)),
            pltpu.SemaphoreType.DMA((8,)),
            pltpu.SemaphoreType.DMA((3,)),
            pltpu.VMEM((4, rows_n, width), x.dtype),
            pltpu.VMEM((4, rows_n, width), x.dtype),
            pltpu.VMEM((4, rows_n, width), jnp.float32),
            pltpu.VMEM((3, rows_n, width), x.dtype),
            pltpu.VMEM((2, rows_n // 2, width), x.dtype),
            pltpu.VMEM((2, rows_n, width), x.dtype),
            pltpu.SemaphoreType.DMA((8,)),
            pltpu.SemaphoreType.DMA((8,)),
            pltpu.SemaphoreType.DMA((groups,)),
            pltpu.SemaphoreType.DMA((groups,)),
        ],
        compiler_params=pltpu.CompilerParams(
            collective_id=collective_id, has_side_effects=True, vmem_limit_bytes=60 * 1024 * 1024
        ),
    )(x, w_gate, w_up, w_down, pages)

def pick_rows(source, row_index, live_slot):
    taken_rows = jnp.take(source, row_index, axis=0)
    return jnp.where(live_slot[:, None], taken_rows, jnp.zeros((), source.dtype))


def body(
    attention_out,
    residual,
    w_out,
    router_w,
    norm_gain,
    page_pool,
    page_table,
    cache_len,
    came_from,
    routes,
    w_gate,
    w_up,
    w_down,
):
    groups = lax.axis_size("req")
    own_group = lax.axis_index("req")
    row_req = attention_out.shape[0]
    rows_all = came_from.shape[0]
    pages_req = page_table.shape[1]
    page_len = page_pool.shape[1]
    kv_slice = page_pool.shape[2]
    experts = groups // 2
    targets = jnp.arange(groups, dtype=jnp.int32)
    local_ids = jnp.arange(row_req, dtype=jnp.int32)
    dest_of = (
        jnp.zeros((rows_all,), jnp.int32).at[came_from].set(jnp.arange(rows_all, dtype=jnp.int32))
    )
    dest_group = dest_of // row_req
    dest_hot = (
        (dest_group[:, None] == targets[None, :]).astype(jnp.int32).reshape(groups, row_req, groups)
    )
    pair_rank = jnp.sum((jnp.cumsum(dest_hot, axis=1) - dest_hot) * dest_hot, axis=2).reshape(
        rows_all
    )
    own_dest = lax.dynamic_slice_in_dim(dest_group, own_group * row_req, row_req)
    own_rank = lax.dynamic_slice_in_dim(pair_rank, own_group * row_req, row_req)
    chosen_send = (
        (own_dest[None, None, :] == targets[:, None, None])
        & (own_rank[None, None, :] == jnp.arange(MIG_PAIR, dtype=jnp.int32)[None, :, None])
        & (targets[:, None, None] != own_group)
    )
    send_index = jnp.sum(jnp.where(chosen_send, local_ids[None, None, :], 0), axis=2).reshape(-1)
    send_live = jnp.any(chosen_send, axis=2).reshape(-1)
    attn_send, page_pool = lax.optimization_barrier(
        (pick_rows(attention_out, send_index, send_live), page_pool)
    )
    moved_attn, moved_resid = (
        lax.all_to_all(
            attn_send,
            "req",
            split_axis=0,
            concat_axis=0,
            tiled=True,
        ),
        lax.all_to_all(
            pick_rows(residual, send_index, send_live),
            "req",
            split_axis=0,
            concat_axis=0,
            tiled=True,
        ),
    )
    new_source = lax.dynamic_slice_in_dim(came_from, own_group * row_req, row_req)
    source_group = new_source // row_req
    stays_home = source_group == own_group
    arrival = jnp.where(
        stays_home,
        new_source - own_group * row_req,
        row_req + source_group * MIG_PAIR + jnp.take(pair_rank, new_source),
    )
    attn_new = jnp.take(jnp.concatenate([attention_out, moved_attn], axis=0), arrival, axis=0)
    resid_new = jnp.take(jnp.concatenate([residual, moved_resid], axis=0), arrival, axis=0)
    projected = jnp.dot(
        attn_new,
        lax.all_gather(w_out, "req", axis=0, tiled=True),
        preferred_element_type=jnp.float32,
    )
    hidden = resid_new.astype(jnp.float32) + projected
    squares = jnp.sum(hidden * hidden, axis=1)
    scaled = hidden * norm_gain[None, :]
    raw_logits = jnp.dot(scaled, router_w, precision=lax.Precision.HIGHEST)
    stats_t = jnp.concatenate([squares[None, :], raw_logits.T], axis=0)
    stats_t = jnp.pad(stats_t, ((0, 16 - stats_t.shape[0]), (0, 0)))
    n_exp = lax.axis_size("exp")
    row_stats = jnp.sum(exchange(stats_t, "exp", n_exp, True, 0), axis=0)[:9].T
    total_sq = row_stats[:, 0]
    inverse = lax.rsqrt(total_sq / D + EPSILON)
    normed = scaled * inverse[:, None]
    logits = row_stats[:, 1:] * inverse[:, None]
    normed_rows = normed.astype(jnp.bfloat16)
    expert_ids = jnp.arange(experts, dtype=jnp.int32)
    chosen = jnp.sum(
        jnp.where(routes[:, :, None] == expert_ids[None, None, :], logits[:, None, :], 0.0), axis=2
    )
    gate_first = jax.nn.sigmoid(chosen[:, 0] - chosen[:, 1])
    gate_second = jax.nn.sigmoid(chosen[:, 1] - chosen[:, 0])
    flat_routes = routes.reshape(-1)
    expert_hot = (flat_routes[:, None] == expert_ids[None, :]).astype(jnp.int32)
    expert_rank = jnp.sum((jnp.cumsum(expert_hot, axis=0) - expert_hot) * expert_hot, axis=1)
    target_dev = flat_routes + experts * (expert_rank % 2)
    slot_index = expert_rank // 2
    assign_ids = jnp.arange(flat_routes.shape[0], dtype=jnp.int32)
    chosen_slot = (target_dev[None, None, :] == targets[:, None, None]) & (
        slot_index[None, None, :] == jnp.arange(CAP, dtype=jnp.int32)[None, :, None]
    )
    slot_source = jnp.sum(
        jnp.where(chosen_slot, assign_ids[None, None, :] // 2, 0), axis=2
    ).reshape(-1)
    slot_live = jnp.any(chosen_slot, axis=2).reshape(-1)
    outgoing = pick_rows(normed_rows, slot_source, slot_live)
    arrived = exchange(
        outgoing.reshape(groups, -1, outgoing.shape[-1]), "req", groups, False, 1
    ).reshape(outgoing.shape)
    page_rows = jnp.take(page_pool, page_table.reshape(-1), axis=0).reshape(
        row_req, pages_req, page_len, kv_slice
    )
    position = (
        jnp.arange(pages_req, dtype=jnp.int32)[:, None] * page_len
        + jnp.arange(page_len, dtype=jnp.int32)[None, :]
    )
    kept_mask = position[None, :, :] < cache_len[:, None, None]
    page_rows = jnp.where(kept_mask[..., None], page_rows, jnp.zeros((), page_rows.dtype)).reshape(
        row_req, -1
    )
    page_send = pick_rows(page_rows, send_index, send_live)
    partial_value, moved_pages = gather_ffn(
        arrived,
        w_gate,
        w_up,
        w_down,
        page_send.reshape(groups, MIG_PAIR, -1),
        lax.axis_size("exp"),
        groups,
        3,
    )
    moved_pages = moved_pages.reshape(groups * MIG_PAIR, -1)
    summed_value = partial_value
    lookup = target_dev * CAP + slot_index
    pick_home = (arrival[:, None] == jnp.arange(row_req)[None, :]).astype(page_rows.dtype)
    pick_moved = (
        arrival[:, None] == row_req + jnp.arange(moved_pages.shape[0])[None, :]
    ).astype(page_rows.dtype)
    new_pages = (
        jnp.dot(pick_home, page_rows, preferred_element_type=jnp.float32)
        + jnp.dot(pick_moved, moved_pages, preferred_element_type=jnp.float32)
    ).astype(page_rows.dtype).reshape(row_req, pages_req, page_len, kv_slice)
    returned = exchange(
        summed_value.reshape(groups, -1, summed_value.shape[-1]), "req", groups, False, 2
    ).reshape(summed_value.shape)
    taken_rows = jnp.take(returned, lookup, axis=0).reshape(row_req, 2, -1).astype(jnp.float32)
    expert_part = gate_first[:, None] * taken_rows[:, 0] + gate_second[:, None] * taken_rows[:, 1]
    mixed = hidden + expert_part
    return (mixed, new_pages)


def solution(mesh):
    in_specs = (
        P("req", None),
        P("req", "exp"),
        P("req", "exp"),
        P("exp", None),
        P("exp"),
        P("req", None, "exp"),
        P("req", None),
        P("req"),
        P(),
        P("req", None),
        P("req", None, "exp"),
        P("req", None, "exp"),
        P("req", "exp", None),
    )
    out_specs = (P("req", "exp"), P("req", None, None, "exp"))
    return jax.shard_map(body, mesh=mesh, in_specs=in_specs, out_specs=out_specs, check_vma=False)
```

```python
import jax
import jax.numpy as jnp
from jax import lax
from jax.experimental import pallas as pl
from jax.experimental.pallas import tpu as pltpu
from jax.sharding import PartitionSpec as P
import functools

D = 4096
CAP = 32
MIG_PAIR = 4


EPSILON = 1e-05

MESH = pl.DeviceIdType.MESH


def exchange_kernel(axis, n, gather, x_ref, y_ref, send_sems, recv_sems):
    me = lax.axis_index(axis)
    barrier = pltpu.get_barrier_semaphore()
    for k in range(1, n):
        pl.semaphore_signal(
            barrier, inc=1, device_id={axis: lax.rem(me + k, n)}, device_id_type=MESH
        )
    pl.semaphore_wait(barrier, n - 1)
    copies = []
    for k in range(1, n):
        peer = lax.rem(me + k, n)
        copy = pltpu.make_async_remote_copy(
            src_ref=x_ref if gather else x_ref.at[peer],
            dst_ref=y_ref.at[me],
            send_sem=send_sems.at[k],
            recv_sem=recv_sems.at[k],
            device_id={axis: peer},
            device_id_type=MESH,
        )
        copy.start()
        copies.append(copy)
    if gather:
        y_ref[me] = x_ref[...]
    else:
        y_ref[me] = x_ref[me]
    for k in range(1, n):
        copies[k - 1].wait_send()
        source = lax.rem(me + n - k, n)
        pltpu.make_async_remote_copy(
            src_ref=x_ref if gather else x_ref.at[source],
            dst_ref=y_ref.at[source],
            send_sem=send_sems.at[k],
            recv_sem=recv_sems.at[k],
            device_id={axis: source},
            device_id_type=MESH,
        ).wait_recv()


def exchange(x, axis, n, gather, collective_id):
    out_shape = (n,) + x.shape if gather else x.shape
    return pl.pallas_call(
        functools.partial(exchange_kernel, axis, n, gather),
        out_shape=jax.ShapeDtypeStruct(out_shape, x.dtype),
        in_specs=[pl.BlockSpec(memory_space=pltpu.VMEM)],
        out_specs=pl.BlockSpec(memory_space=pltpu.VMEM),
        scratch_shapes=[pltpu.SemaphoreType.DMA((n,)), pltpu.SemaphoreType.DMA((n,))],
        compiler_params=pltpu.CompilerParams(collective_id=collective_id, has_side_effects=True),
    )(x)


def exp_gather_kernel(n, x_ref, y_ref, send_sems, recv_sems):
    chips = n // 2
    width = x_ref.shape[1]
    half = x_ref.shape[0] // 2
    me = lax.axis_index("exp")
    z, core = me // 2, me % 2
    sib = 2 * z + 1 - core
    up = 2 * lax.rem(z + 1, chips) + core
    dn = 2 * lax.rem(z + chips - 1, chips) + core
    far = 2 * lax.rem(z + 2, chips) + core

    def cols(block):
        return pl.ds(pl.multiple_of(block * width, width), width)

    def rows(part):
        return pl.ds(part * half, half)

    barrier = pltpu.get_barrier_semaphore()
    for peer in (sib, up, dn):
        pl.semaphore_signal(barrier, inc=1, device_id={"exp": peer}, device_id_type=MESH)
    pl.semaphore_wait(barrier, 3)

    def remote(src, dst, slot, peer):
        return pltpu.make_async_remote_copy(
            src_ref=src, dst_ref=dst, send_sem=send_sems.at[slot],
            recv_sem=recv_sems.at[slot], device_id={"exp": peer}, device_id_type=MESH,
        )

    own_cols = cols(me)
    first = [
        remote(x_ref, y_ref.at[:, own_cols], 0, up),
        remote(x_ref, y_ref.at[:, own_cols], 1, dn),
        remote(x_ref, y_ref.at[:, own_cols], 2, sib),
    ]
    for copy in first:
        copy.start()
    y_ref[:, own_cols] = x_ref[...]
    remote(x_ref, y_ref.at[:, cols(dn)], 0, dn).wait_recv()
    remote(x_ref, y_ref.at[:, cols(up)], 1, up).wait_recv()
    second = [
        remote(y_ref.at[rows(1), cols(dn)], y_ref.at[rows(1), cols(dn)], 3, up),
        remote(y_ref.at[rows(0), cols(up)], y_ref.at[rows(0), cols(up)], 4, dn),
        remote(y_ref.at[:, cols(dn)], y_ref.at[:, cols(dn)], 5, sib),
        remote(y_ref.at[:, cols(up)], y_ref.at[:, cols(up)], 6, sib),
    ]
    for copy in second:
        copy.start()
    remote(y_ref.at[rows(1), cols(far)], y_ref.at[rows(1), cols(far)], 3, dn).wait_recv()
    remote(y_ref.at[rows(0), cols(far)], y_ref.at[rows(0), cols(far)], 4, up).wait_recv()
    third = remote(y_ref.at[:, cols(far)], y_ref.at[:, cols(far)], 7, sib)
    third.start()
    sib_z = 2 * z + 1 - core
    sib_up = 2 * lax.rem(z + 1, chips) + 1 - core
    sib_dn = 2 * lax.rem(z + chips - 1, chips) + 1 - core
    sib_far = 2 * lax.rem(z + 2, chips) + 1 - core
    remote(x_ref, y_ref.at[:, cols(sib_z)], 2, sib).wait_recv()
    remote(y_ref.at[:, cols(sib_dn)], y_ref.at[:, cols(sib_dn)], 5, sib).wait_recv()
    remote(y_ref.at[:, cols(sib_up)], y_ref.at[:, cols(sib_up)], 6, sib).wait_recv()
    remote(y_ref.at[:, cols(sib_far)], y_ref.at[:, cols(sib_far)], 7, sib).wait_recv()
    for copy in first + second + [third]:
        copy.wait_send()


def exp_gather(x, n, collective_id):
    return pl.pallas_call(
        functools.partial(exp_gather_kernel, n),
        out_shape=jax.ShapeDtypeStruct((x.shape[0], n * x.shape[1]), x.dtype),
        in_specs=[pl.BlockSpec(memory_space=pltpu.VMEM)],
        out_specs=pl.BlockSpec(memory_space=pltpu.VMEM),
        scratch_shapes=[pltpu.SemaphoreType.DMA((8,)), pltpu.SemaphoreType.DMA((8,))],
        compiler_params=pltpu.CompilerParams(collective_id=collective_id, has_side_effects=True),
    )(x)


def ffn_kernel(x_ref, wg_ref, wu_ref, wd_ref, o_ref, g_acc, u_acc):
    step = pl.program_id(0)

    @pl.when(step == 0)
    def _():
        g_acc[...] = jnp.zeros_like(g_acc)
        u_acc[...] = jnp.zeros_like(u_acc)

    x = x_ref[...]
    g_acc[...] += jnp.dot(x, wg_ref[...], preferred_element_type=jnp.float32)
    u_acc[...] += jnp.dot(x, wu_ref[...], preferred_element_type=jnp.float32)

    @pl.when(step == pl.num_programs(0) - 1)
    def _():
        g = g_acc[...]
        act = (g / (1.0 + jnp.exp(-g)) * u_acc[...]).astype(wd_ref.dtype)
        o_ref[...] = jnp.dot(act, wd_ref[...], preferred_element_type=jnp.float32).astype(
            o_ref.dtype
        )


def expert_ffn(x, wg, wu, wd, tk=512):
    rows_n, d = x.shape
    ff = wg.shape[1]
    return pl.pallas_call(
        ffn_kernel,
        out_shape=jax.ShapeDtypeStruct((rows_n, wd.shape[1]), x.dtype),
        grid=(d // tk,),
        in_specs=[
            pl.BlockSpec((rows_n, tk), lambda k: (0, k)),
            pl.BlockSpec((tk, ff), lambda k: (k, 0)),
            pl.BlockSpec((tk, ff), lambda k: (k, 0)),
            pl.BlockSpec((ff, wd.shape[1]), lambda k: (0, 0)),
        ],
        out_specs=pl.BlockSpec((rows_n, wd.shape[1]), lambda k: (0, 0)),
        scratch_shapes=[
            pltpu.VMEM((rows_n, ff), jnp.float32),
            pltpu.VMEM((rows_n, ff), jnp.float32),
        ],
        compiler_params=pltpu.CompilerParams(
            dimension_semantics=("arbitrary",), vmem_limit_bytes=56 * 1024 * 1024
        ),
        cost_estimate=pl.CostEstimate(
            flops=2 * rows_n * d * ff * 2 + 2 * rows_n * ff * wd.shape[1],
            transcendentals=rows_n * ff,
            bytes_accessed=2 * (rows_n * d + 2 * d * ff + ff * wd.shape[1] + rows_n * wd.shape[1]),
        ),
    )(x, wg, wu, wd)


def gather_ffn_kernel(
    n, groups, x_ref, wg_hbm, wu_hbm, wd_hbm, pg_ref, o_ref, pg_out,
    y_ref, wg_v, wu_v, wd_v, g_acc, u_acc, send_sems, recv_sems, w_sems,
    sib_out, sib_buf, acc, stage, half_buf, near_buf, rs_send, rs_recv, pg_send, pg_recv,
):
    chips = n // 2
    width = x_ref.shape[1]
    half = x_ref.shape[0] // 2
    me = lax.axis_index("exp")
    z, core = me // 2, me % 2
    sib = 2 * z + 1 - core
    up = 2 * lax.rem(z + 1, chips) + core
    dn = 2 * lax.rem(z + chips - 1, chips) + core
    far = 2 * lax.rem(z + 2, chips) + core

    weight_copies = [
        pltpu.make_async_copy(src.at[0], dst, w_sems.at[i])
        for i, (src, dst) in enumerate(((wg_hbm, wg_v), (wu_hbm, wu_v), (wd_hbm, wd_v)))
    ]
    for copy in weight_copies:
        copy.start()

    def cols(block):
        return pl.ds(pl.multiple_of(block * width, width), width)

    def rows(part):
        return pl.ds(part * half, half)

    barrier = pltpu.get_barrier_semaphore()
    for peer in (sib, up, dn):
        pl.semaphore_signal(barrier, inc=1, device_id={"exp": peer}, device_id_type=MESH)
    own_group = lax.axis_index("req")
    for k in range(1, groups):
        pl.semaphore_signal(
            barrier, inc=1, device_id={"req": lax.rem(own_group + k, groups)},
            device_id_type=MESH,
        )
    pl.semaphore_wait(barrier, 3 + groups - 1)
    page_copies = []
    for k in range(1, groups):
        peer = lax.rem(own_group + k, groups)
        copy = pltpu.make_async_remote_copy(
            src_ref=pg_ref.at[peer], dst_ref=pg_out.at[own_group], send_sem=pg_send.at[k],
            recv_sem=pg_recv.at[k], device_id={"req": peer}, device_id_type=MESH,
        )
        copy.start()
        page_copies.append(copy)
    pg_out[own_group] = pg_ref[own_group]

    def remote(src, dst, slot, peer):
        return pltpu.make_async_remote_copy(
            src_ref=src, dst_ref=dst, send_sem=send_sems.at[slot],
            recv_sem=recv_sems.at[slot], device_id={"exp": peer}, device_id_type=MESH,
        )

    def consume(block, first=False):
        rows_in = x_ref[...] if first else y_ref[:, cols(block)]
        w_rows = pl.ds(pl.multiple_of(block * width, width), width)
        g_part = jnp.dot(rows_in, wg_v[w_rows, :], preferred_element_type=jnp.float32)
        u_part = jnp.dot(rows_in, wu_v[w_rows, :], preferred_element_type=jnp.float32)
        if first:
            g_acc[...] = g_part
            u_acc[...] = u_part
        else:
            g_acc[...] += g_part
            u_acc[...] += u_part

    own_cols = cols(me)
    sends = [
        remote(x_ref, y_ref.at[:, own_cols], 0, up),
        remote(x_ref, y_ref.at[:, own_cols], 1, dn),
        remote(x_ref, y_ref.at[:, own_cols], 2, sib),
    ]
    for copy in sends:
        copy.start()
    w_rows = pl.ds(pl.multiple_of(me * width, width), width)
    weight_copies[0].wait()
    g_acc[...] = jnp.dot(x_ref[...], wg_v[w_rows, :], preferred_element_type=jnp.float32)
    weight_copies[1].wait()
    u_acc[...] = jnp.dot(x_ref[...], wu_v[w_rows, :], preferred_element_type=jnp.float32)
    remote(x_ref, y_ref.at[:, cols(dn)], 0, dn).wait_recv()
    remote(x_ref, y_ref.at[:, cols(up)], 1, up).wait_recv()
    second = [
        remote(y_ref.at[rows(1), cols(dn)], y_ref.at[rows(1), cols(dn)], 3, up),
        remote(y_ref.at[rows(0), cols(up)], y_ref.at[rows(0), cols(up)], 4, dn),
        remote(y_ref.at[:, cols(dn)], y_ref.at[:, cols(dn)], 5, sib),
        remote(y_ref.at[:, cols(up)], y_ref.at[:, cols(up)], 6, sib),
    ]
    for copy in second:
        copy.start()
    sends += second
    consume(dn)
    consume(up)
    remote(y_ref.at[rows(1), cols(far)], y_ref.at[rows(1), cols(far)], 3, dn).wait_recv()
    remote(y_ref.at[rows(0), cols(far)], y_ref.at[rows(0), cols(far)], 4, up).wait_recv()
    third = remote(y_ref.at[:, cols(far)], y_ref.at[:, cols(far)], 7, sib)
    third.start()
    sends.append(third)
    consume(far)
    sib_up = 2 * lax.rem(z + 1, chips) + 1 - core
    sib_dn = 2 * lax.rem(z + chips - 1, chips) + 1 - core
    sib_far = 2 * lax.rem(z + 2, chips) + 1 - core
    for block, slot in ((sib, 2), (sib_dn, 5), (sib_up, 6), (sib_far, 7)):
        remote(y_ref.at[:, cols(block)], y_ref.at[:, cols(block)], slot, sib).wait_recv()
        consume(block)
    g = g_acc[...]
    act = (g / (1.0 + jnp.exp(-g)) * u_acc[...]).astype(wd_v.dtype)
    weight_copies[2].wait()

    def down(block):
        return jnp.dot(act, wd_v[:, cols(block)], preferred_element_type=jnp.float32).astype(
            sib_out.dtype
        )

    def rs_remote(src, dst, slot, peer):
        return pltpu.make_async_remote_copy(
            src_ref=src, dst_ref=dst, send_sem=rs_send.at[slot],
            recv_sem=rs_recv.at[slot], device_id={"exp": peer}, device_id_type=MESH,
        )

    mine = (me, up, dn, far)
    theirs = tuple(block + 1 - 2 * core for block in mine)
    for k in range(4):
        sib_out[k] = down(theirs[k])
        copy = rs_remote(sib_out.at[k], sib_buf.at[k], k, sib)
        copy.start()
        sends.append(copy)
    for k in (3, 1, 2, 0):
        own_part = down(mine[k]).astype(jnp.float32)
        rs_remote(sib_out.at[k], sib_buf.at[k], k, sib).wait_recv()
        acc[k] = own_part + sib_buf[k].astype(jnp.float32)
        if k == 3:
            stage[0] = acc[3].astype(stage.dtype)
            for part, peer, slot in ((0, up, 4), (1, dn, 5)):
                copy = rs_remote(stage.at[0, rows(part)], half_buf.at[part], slot, peer)
                copy.start()
                sends.append(copy)
    rs_remote(stage.at[0, rows(0)], half_buf.at[0], 4, dn).wait_recv()
    acc[1, rows(0)] = acc[1, rows(0)] + half_buf[0].astype(jnp.float32)
    stage[1] = acc[1].astype(stage.dtype)
    copy = rs_remote(stage.at[1], near_buf.at[0], 6, up)
    copy.start()
    sends.append(copy)
    rs_remote(stage.at[0, rows(1)], half_buf.at[1], 5, up).wait_recv()
    acc[2, rows(1)] = acc[2, rows(1)] + half_buf[1].astype(jnp.float32)
    stage[2] = acc[2].astype(stage.dtype)
    copy = rs_remote(stage.at[2], near_buf.at[1], 7, dn)
    copy.start()
    sends.append(copy)
    rs_remote(stage.at[1], near_buf.at[0], 6, dn).wait_recv()
    rs_remote(stage.at[2], near_buf.at[1], 7, up).wait_recv()
    o_ref[...] = (
        acc[0] + near_buf[0].astype(jnp.float32) + near_buf[1].astype(jnp.float32)
    ).astype(o_ref.dtype)
    for copy in sends:
        copy.wait_send()
    for k in range(1, groups):
        page_copies[k - 1].wait_send()
        source = lax.rem(own_group + groups - k, groups)
        pltpu.make_async_remote_copy(
            src_ref=pg_ref.at[source], dst_ref=pg_out.at[source], send_sem=pg_send.at[k],
            recv_sem=pg_recv.at[k], device_id={"req": source}, device_id_type=MESH,
        ).wait_recv()


def gather_ffn(x, w_gate, w_up, w_down, pages, n, groups, collective_id):
    rows_n, width = x.shape
    d, ff = w_gate.shape[1], w_gate.shape[2]
    return pl.pallas_call(
        functools.partial(gather_ffn_kernel, n, groups),
        out_shape=(
            jax.ShapeDtypeStruct((rows_n, w_down.shape[2] // n), x.dtype),
            jax.ShapeDtypeStruct(pages.shape, pages.dtype),
        ),
        in_specs=[pl.BlockSpec(memory_space=pltpu.VMEM)] + [pl.BlockSpec(memory_space=pl.ANY)] * 3
        + [pl.BlockSpec(memory_space=pltpu.VMEM)],
        out_specs=(pl.BlockSpec(memory_space=pltpu.VMEM), pl.BlockSpec(memory_space=pltpu.VMEM)),
        scratch_shapes=[
            pltpu.VMEM((rows_n, n * width), x.dtype),
            pltpu.VMEM((d, ff), w_gate.dtype),
            pltpu.VMEM((d, ff), w_up.dtype),
            pltpu.VMEM((ff, w_down.shape[2]), w_down.dtype),
            pltpu.VMEM((rows_n, ff), jnp.float32),
            pltpu.VMEM((rows_n, ff), jnp.float32),
            pltpu.SemaphoreType.DMA((8,)),
            pltpu.SemaphoreType.DMA((8,)),
            pltpu.SemaphoreType.DMA((3,)),
            pltpu.VMEM((4, rows_n, width), x.dtype),
            pltpu.VMEM((4, rows_n, width), x.dtype),
            pltpu.VMEM((4, rows_n, width), jnp.float32),
            pltpu.VMEM((3, rows_n, width), x.dtype),
            pltpu.VMEM((2, rows_n // 2, width), x.dtype),
            pltpu.VMEM((2, rows_n, width), x.dtype),
            pltpu.SemaphoreType.DMA((8,)),
            pltpu.SemaphoreType.DMA((8,)),
            pltpu.SemaphoreType.DMA((groups,)),
            pltpu.SemaphoreType.DMA((groups,)),
        ],
        compiler_params=pltpu.CompilerParams(
            collective_id=collective_id, has_side_effects=True, vmem_limit_bytes=60 * 1024 * 1024
        ),
    )(x, w_gate, w_up, w_down, pages)

def pick_rows(source, row_index, live_slot):
    taken_rows = jnp.take(source, row_index, axis=0)
    return jnp.where(live_slot[:, None], taken_rows, jnp.zeros((), source.dtype))


def body(
    attention_out,
    residual,
    w_out,
    router_w,
    norm_gain,
    page_pool,
    page_table,
    cache_len,
    came_from,
    routes,
    w_gate,
    w_up,
    w_down,
):
    groups = lax.axis_size("req")
    own_group = lax.axis_index("req")
    row_req = attention_out.shape[0]
    rows_all = came_from.shape[0]
    pages_req = page_table.shape[1]
    page_len = page_pool.shape[1]
    kv_slice = page_pool.shape[2]
    experts = groups // 2
    targets = jnp.arange(groups, dtype=jnp.int32)
    local_ids = jnp.arange(row_req, dtype=jnp.int32)
    dest_of = (
        jnp.zeros((rows_all,), jnp.int32).at[came_from].set(jnp.arange(rows_all, dtype=jnp.int32))
    )
    dest_group = dest_of // row_req
    dest_hot = (
        (dest_group[:, None] == targets[None, :]).astype(jnp.int32).reshape(groups, row_req, groups)
    )
    pair_rank = jnp.sum((jnp.cumsum(dest_hot, axis=1) - dest_hot) * dest_hot, axis=2).reshape(
        rows_all
    )
    own_dest = lax.dynamic_slice_in_dim(dest_group, own_group * row_req, row_req)
    own_rank = lax.dynamic_slice_in_dim(pair_rank, own_group * row_req, row_req)
    chosen_send = (
        (own_dest[None, None, :] == targets[:, None, None])
        & (own_rank[None, None, :] == jnp.arange(MIG_PAIR, dtype=jnp.int32)[None, :, None])
        & (targets[:, None, None] != own_group)
    )
    send_index = jnp.sum(jnp.where(chosen_send, local_ids[None, None, :], 0), axis=2).reshape(-1)
    send_live = jnp.any(chosen_send, axis=2).reshape(-1)
    attn_send, page_pool = lax.optimization_barrier(
        (pick_rows(attention_out, send_index, send_live), page_pool)
    )
    moved_attn, moved_resid = (
        lax.all_to_all(
            attn_send,
            "req",
            split_axis=0,
            concat_axis=0,
            tiled=True,
        ),
        lax.all_to_all(
            pick_rows(residual, send_index, send_live),
            "req",
            split_axis=0,
            concat_axis=0,
            tiled=True,
        ),
    )
    new_source = lax.dynamic_slice_in_dim(came_from, own_group * row_req, row_req)
    source_group = new_source // row_req
    stays_home = source_group == own_group
    arrival = jnp.where(
        stays_home,
        new_source - own_group * row_req,
        row_req + source_group * MIG_PAIR + jnp.take(pair_rank, new_source),
    )
    attn_new = jnp.take(jnp.concatenate([attention_out, moved_attn], axis=0), arrival, axis=0)
    resid_new = jnp.take(jnp.concatenate([residual, moved_resid], axis=0), arrival, axis=0)
    projected = jnp.dot(
        attn_new,
        lax.all_gather(w_out, "req", axis=0, tiled=True),
        preferred_element_type=jnp.float32,
    )
    hidden = resid_new.astype(jnp.float32) + projected
    squares = jnp.sum(hidden * hidden, axis=1)
    scaled = hidden * norm_gain[None, :]
    raw_logits = jnp.dot(scaled, router_w, precision=lax.Precision.HIGHEST)
    stats_t = jnp.concatenate([squares[None, :], raw_logits.T], axis=0)
    stats_t = jnp.pad(stats_t, ((0, 16 - stats_t.shape[0]), (0, 0)))
    n_exp = lax.axis_size("exp")
    row_stats = jnp.sum(exchange(stats_t, "exp", n_exp, True, 0), axis=0)[:9].T
    total_sq = row_stats[:, 0]
    inverse = lax.rsqrt(total_sq / D + EPSILON)
    normed = scaled * inverse[:, None]
    logits = row_stats[:, 1:] * inverse[:, None]
    normed_rows = normed.astype(jnp.bfloat16)
    expert_ids = jnp.arange(experts, dtype=jnp.int32)
    chosen = jnp.sum(
        jnp.where(routes[:, :, None] == expert_ids[None, None, :], logits[:, None, :], 0.0), axis=2
    )
    gate_first = jax.nn.sigmoid(chosen[:, 0] - chosen[:, 1])
    gate_second = jax.nn.sigmoid(chosen[:, 1] - chosen[:, 0])
    flat_routes = routes.reshape(-1)
    expert_hot = (flat_routes[:, None] == expert_ids[None, :]).astype(jnp.int32)
    expert_rank = jnp.sum((jnp.cumsum(expert_hot, axis=0) - expert_hot) * expert_hot, axis=1)
    target_dev = flat_routes + experts * (expert_rank % 2)
    slot_index = expert_rank // 2
    assign_ids = jnp.arange(flat_routes.shape[0], dtype=jnp.int32)
    chosen_slot = (target_dev[None, None, :] == targets[:, None, None]) & (
        slot_index[None, None, :] == jnp.arange(CAP, dtype=jnp.int32)[None, :, None]
    )
    slot_source = jnp.sum(
        jnp.where(chosen_slot, assign_ids[None, None, :] // 2, 0), axis=2
    ).reshape(-1)
    slot_live = jnp.any(chosen_slot, axis=2).reshape(-1)
    outgoing = pick_rows(normed_rows, slot_source, slot_live)
    arrived = exchange(
        outgoing.reshape(groups, -1, outgoing.shape[-1]), "req", groups, False, 1
    ).reshape(outgoing.shape)
    page_rows = jnp.take(page_pool, page_table.reshape(-1), axis=0).reshape(
        row_req, pages_req, page_len, kv_slice
    )
    position = (
        jnp.arange(pages_req, dtype=jnp.int32)[:, None] * page_len
        + jnp.arange(page_len, dtype=jnp.int32)[None, :]
    )
    kept_mask = position[None, :, :] < cache_len[:, None, None]
    page_rows = jnp.where(kept_mask[..., None], page_rows, jnp.zeros((), page_rows.dtype)).reshape(
        row_req, -1
    )
    page_send = pick_rows(page_rows, send_index, send_live)
    partial_value, moved_pages = gather_ffn(
        arrived,
        w_gate,
        w_up,
        w_down,
        page_send.reshape(groups, MIG_PAIR, -1),
        lax.axis_size("exp"),
        groups,
        3,
    )
    moved_pages = moved_pages.reshape(groups * MIG_PAIR, -1)
    summed_value = partial_value
    lookup = target_dev * CAP + slot_index
    new_pages = jnp.take(
        jnp.concatenate([page_rows, moved_pages], axis=0), arrival, axis=0
    ).reshape(row_req, pages_req, page_len, kv_slice)
    returned = exchange(
        summed_value.reshape(groups, -1, summed_value.shape[-1]), "req", groups, False, 2
    ).reshape(summed_value.shape)
    taken_rows = jnp.take(returned, lookup, axis=0).reshape(row_req, 2, -1).astype(jnp.float32)
    expert_part = gate_first[:, None] * taken_rows[:, 0] + gate_second[:, None] * taken_rows[:, 1]
    mixed = hidden + expert_part
    return (mixed, new_pages)


def solution(mesh):
    in_specs = (
        P("req", None),
        P("req", "exp"),
        P("req", "exp"),
        P("exp", None),
        P("exp"),
        P("req", None, "exp"),
        P("req", None),
        P("req"),
        P(),
        P("req", None),
        P("req", None, "exp"),
        P("req", None, "exp"),
        P("req", "exp", None),
    )
    out_specs = (P("req", "exp"), P("req", None, None, "exp"))
    return jax.shard_map(body, mesh=mesh, in_specs=in_specs, out_specs=out_specs, check_vma=False)
```
